32 devices in a mesh: dp: 8 (over y, x, core), tensor: 4 (over z).
Axes of the slice: x: 2, y: 2, z: 4, core: 2. Of those that a mesh axis runs over, the one named last changes fastest.
Arguments:
- tokens: bfloat16 [16384, 768], P(('dp', 'tensor')), may hold values from -6 to 6
- lengths: int32 [8], P('dp'), may hold values from 256 to 1024, as said below
- noise_mask: int32 [8, 1024], P('dp'), may hold values 0 or 1
- cotangent: bfloat16 [16384, 768], P(('dp', 'tensor')), may hold values from -6 to 6
- attn_gain: float32 [2, 768], replicated, may hold values from 0.5 to 1.5
- query_weight: bfloat16 [2, 768, 768], P(None, None, 'tensor'), may hold values from -0.21875 to 0.21875
- key_weight: bfloat16 [2, 768, 768], P(None, None, 'tensor'), may hold values from -0.21875 to 0.21875
- value_weight: bfloat16 [2, 768, 768], P(None, None, 'tensor'), may hold values from -0.21875 to 0.21875
- out_weight: bfloat16 [2, 768, 768], P(None, 'tensor'), may hold values from -0.875 to 0.875
- mlp_gain: float32 [2, 768], replicated, may hold values from 0.5 to 1.5
- up_weight: bfloat16 [2, 768, 3072], P(None, None, 'tensor'), may hold values from -0.21875 to 0.21875
- down_weight: bfloat16 [2, 3072, 768], P(None, 'tensor'), may hold values from -0.109375 to 0.109375
Outputs:
- block_out: float32 [16384, 768], P(('dp', 'tensor'))
- tokens_grad: float32 [16384, 768], P(('dp', 'tensor'))
- attn_gain_grad: float32 [2, 768], replicated
- query_weight_grad: float32 [2, 768, 768], P(None, None, 'tensor')
- key_weight_grad: float32 [2, 768, 768], P(None, None, 'tensor')
- value_weight_grad: float32 [2, 768, 768], P(None, None, 'tensor')
- out_weight_grad: float32 [2, 768, 768], P(None, 'tensor')
- mlp_gain_grad: float32 [2, 768], replicated
- up_weight_grad: float32 [2, 768, 3072], P(None, None, 'tensor')
- down_weight_grad: float32 [2, 3072, 768], P(None, 'tensor')
The draws below stay inside these ranges and needn't reach their ends.
Inputs may be any that keep to these rules, and one draw needn't show every extreme that they name: `lengths`: each sequence has at least 256 and at most 1024 valid tokens; some sequence has exactly 1024 and some exactly 256.
All inputs are finite; a program needn't handle non-finite values. No bound on the sum of `noise_mask` on one device may be relied on, other than what follows from the above.
Results may differ from the reference program's by a relative error of at most 0.03.
Values may be sent and summed in bfloat16 or wider, within the bound.
A program may use at most 192 MiB of HBM per device.

```python
import math
import jax
import jax.numpy as jnp
from jax import lax

D = 768
HEADS = 12
HD = 64
FF = 3072
BLK = 16
LMAX = 1024
LAYERS = 2
SEQS = 8
ROWS = 16384


def draw_lengths(key, part):
    base = jax.random.randint(jax.random.fold_in(key, 11), (SEQS,), LMAX // 4, LMAX + 1, dtype=jnp.int32)
    order = jax.random.permutation(jax.random.fold_in(key, 12), SEQS)
    slots_idx = jnp.arange(SEQS, dtype=jnp.int32)
    base = jnp.where(slots_idx == order[0], LMAX, base)
    base = jnp.where(slots_idx == order[1], LMAX // 4, base)
    return base.astype(jnp.int32)


def plant(entries, own_key, low, top_value):
    index_at = [jax.random.randint(jax.random.fold_in(own_key, axis), (), 0, length) for axis, length in enumerate(entries.shape)]
    longest = entries.shape.index(max(entries.shape))
    beside = index_at[:longest] + [(index_at[longest] + 1) % entries.shape[longest]] + index_at[longest + 1:]
    return entries.at[tuple(index_at)].set(low).at[tuple(beside)].set(top_value)


def block_levels(key, extent, cuts, least, largest):
    def one(dim, shards_of):
        steps = jax.random.uniform(jax.random.fold_in(jax.random.fold_in(key, 6), dim), (shards_of,), jnp.float32, least / len(cuts), largest / len(cuts))
        return jnp.repeat(jnp.exp(steps), extent[dim] // shards_of).reshape((-1,) + (1,) * (len(extent) - dim - 1))

    gain = one(*cuts[0])
    for cut in cuts[1:]:
        gain = gain * one(*cut)
    return gain


def centred(own_key, extent, spread, limit, split=(), kind=jnp.bfloat16):
    factor_of = block_levels(own_key, extent, split, -0.22, 0.18) if split else 1.0
    values = jax.random.normal(own_key, extent, jnp.float32) * spread * factor_of
    return jnp.minimum(jnp.maximum(values, -limit), limit).astype(kind)


def setup_inputs(seed: int = 0) -> dict:
    splits = jax.random.split(jax.random.key(seed), 13)
    return {
        "tokens": centred(splits[0], (ROWS, D), 1.0, 6.0, ((0, 32),)),
        "lengths": draw_lengths(jax.random.fold_in(splits[12], 71), 0),
        "noise_mask": plant((jax.random.randint(splits[2], (SEQS, LMAX), 0, 2) < 1).astype(jnp.int32), jax.random.fold_in(splits[2], 1), 0, 1),
        "cotangent": centred(splits[3], (ROWS, D), 1.0, 6.0, ((0, 32),)),
        "attn_gain": jnp.clip(1.0 + 0.1 * jax.random.normal(splits[4], (LAYERS, D), jnp.float32), 0.5, 1.5),
        "query_weight": centred(splits[5], (LAYERS, D, D), D ** -0.5, 0.21875, ((2, 4),)),
        "key_weight": centred(splits[6], (LAYERS, D, D), D ** -0.5, 0.21875, ((2, 4),)),
        "value_weight": centred(splits[7], (LAYERS, D, D), D ** -0.5, 0.21875, ((2, 4),)),
        "out_weight": centred(splits[8], (LAYERS, D, D), (D // 16) ** -0.5, 0.875, ((1, 4),)),
        "mlp_gain": jnp.clip(1.0 + 0.1 * jax.random.normal(splits[9], (LAYERS, D), jnp.float32), 0.5, 1.5),
        "up_weight": centred(splits[10], (LAYERS, D, FF), D ** -0.5, 0.21875, ((2, 4),)),
        "down_weight": centred(splits[11], (LAYERS, FF, D), FF ** -0.5, 0.109375, ((1, 4),)),
    }


@jax.custom_vjp
def low(v):
    return lax.optimization_barrier(v.astype(jnp.bfloat16)).astype(jnp.float32)

@jax.custom_vjp
def low_back(v):
    return v

def low_keep(v):
    return (low(v), None)

def low_pass(kept, grad):
    return (grad,)

def back_keep(v):
    return (v, None)

def back_low(kept, grad):
    return (low(grad),)
low.defvjp(low_keep, low_pass)
low_back.defvjp(back_keep, back_low)
NORM_EPS = 1e-05
MASKED_SCORE = -1e+30
HIGHEST = lax.Precision.HIGHEST

def layer_norm(row_vals, gain_row):
    row_mean = lax.optimization_barrier(jnp.mean(row_vals, axis=-1, keepdims=True))
    centered = row_vals - row_mean
    variance = lax.optimization_barrier(jnp.mean(centered * centered, axis=-1, keepdims=True))
    return centered * lax.rsqrt(variance + NORM_EPS) * gain_row

def rotate(vectors, cosines, sines):
    half_dim = vectors.shape[-1] // 2
    front_half = vectors[..., :half_dim]
    back_half = vectors[..., half_dim:]
    return jnp.concatenate([front_half * cosines - back_half * sines, back_half * cosines + front_half * sines], axis=-1)

def tables(row_total):
    position = (jnp.arange(row_total, dtype=jnp.int32) % LMAX).astype(jnp.float32)
    frequency = jnp.exp(-math.log(10000.0) * jnp.arange(HD // 2, dtype=jnp.int32).astype(jnp.float32) / (HD // 2))
    angles = position[:, None] * frequency[None, :]
    return (jnp.cos(angles)[:, None, :], jnp.sin(angles)[:, None, :])

def visible(row_ids, col_ids, seq_len):
    block_q = row_ids % LMAX // BLK
    block_k = col_ids % LMAX // BLK
    clean_q = row_ids >= LMAX
    clean_k = col_ids >= LMAX
    both_clean = clean_k[None, :] & (block_k[None, :] <= block_q[:, None])
    noisy_query = jnp.where(clean_k[None, :], block_k[None, :] < block_q[:, None], block_k[None, :] == block_q[:, None])
    rule = jnp.where(clean_q[:, None], both_clean, noisy_query)
    live_key = col_ids % LMAX < seq_len
    return rule & live_key[None, :] | (row_ids[:, None] == col_ids[None, :])

def loss_rows(lengths, noise_mask):
    position = jnp.arange(2 * LMAX, dtype=jnp.int32) % LMAX
    live_rows = position[None, :] < lengths[:, None]
    counted = jnp.concatenate([noise_mask, jnp.ones_like(noise_mask)], axis=1)
    return (live_rows & (counted == 1)).astype(jnp.float32).reshape(-1)

def one_sequence(params, row_vals, seq_len):
    attn_gain, w_query, w_key, w_value, w_out, mlp_gain, w_up, w_down = params
    row_count = row_vals.shape[0]
    cosines, sines = tables(row_count)
    row_ids = jnp.arange(row_count, dtype=jnp.int32)
    seen = visible(row_ids, row_ids, seq_len)
    score_scale = 1.0 / math.sqrt(HD)
    for layer_idx in range(LAYERS):
        normed = low(layer_norm(row_vals, attn_gain[layer_idx]))
        queries = low(rotate(low_back(jnp.dot(normed, w_query[layer_idx], precision=HIGHEST)).reshape(row_count, HEADS, HD), cosines, sines))
        key_rows = low(rotate(low_back(jnp.dot(normed, w_key[layer_idx], precision=HIGHEST)).reshape(row_count, HEADS, HD), cosines, sines))
        value_rows = low(low_back(jnp.dot(normed, w_value[layer_idx], precision=HIGHEST))).reshape(row_count, HEADS, HD)
        scores = low_back(jnp.einsum('qhd,khd->hqk', queries, key_rows, precision=HIGHEST) * score_scale)
        soft_probs = low(jax.nn.softmax(jnp.where(seen[None], scores, MASKED_SCORE), axis=-1))
        mixed_rows = jnp.einsum('hqk,khd->qhd', soft_probs, value_rows, precision=HIGHEST).reshape(row_count, D)
        mixed_rows = low(low_back(mixed_rows))
        row_vals = row_vals + low_back(jnp.dot(mixed_rows, w_out[layer_idx], precision=HIGHEST))
        lifted = low(layer_norm(row_vals, mlp_gain[layer_idx]))
        hidden = low(jax.nn.gelu(low_back(jnp.dot(lifted, w_up[layer_idx], precision=HIGHEST))))
        row_vals = row_vals + low_back(jnp.dot(hidden, w_down[layer_idx], precision=HIGHEST))
    return row_vals

def reference(tokens, lengths, noise_mask, cotangent, attn_gain, query_weight, key_weight, value_weight, out_weight, mlp_gain, up_weight, down_weight):
    params = (attn_gain.astype(jnp.float32), query_weight.astype(jnp.float32), key_weight.astype(jnp.float32), value_weight.astype(jnp.float32), out_weight.astype(jnp.float32), mlp_gain.astype(jnp.float32), up_weight.astype(jnp.float32), down_weight.astype(jnp.float32))

    def forward(weights_all, residual):
        seq_blocks = residual.reshape(SEQS, 2 * LMAX, D)

        def per_sequence(seq_item):
            return one_sequence(weights_all, seq_item[0], seq_item[1])
        return lax.map(jax.checkpoint(per_sequence), (seq_blocks, lengths)).reshape(SEQS * 2 * LMAX, D)
    block_out, pullback = jax.vjp(forward, params, tokens.astype(jnp.float32))
    seed_grad = cotangent.astype(jnp.float32) * loss_rows(lengths, noise_mask)[:, None]
    weight_grads, tokens_grad = pullback(seed_grad)
    return (block_out, tokens_grad, weight_grads[0], weight_grads[1], weight_grads[2], weight_grads[3], weight_grads[4], weight_grads[5], weight_grads[6], weight_grads[7])
```

```python
import functools
import math

import jax
import jax.numpy as jnp
from jax import lax
from jax.experimental import pallas as pl
from jax.experimental.pallas import tpu as pltpu
from jax.sharding import PartitionSpec as P

HD = 64
BLK = 16
LMAX = 1024
LAYERS = 2
EPS = 1e-05
NEG = -1e30
SCALE = 1.0 / math.sqrt(HD)
GC = math.sqrt(2.0 / math.pi)
GA = 0.044715
F32 = jnp.float32
BF = jnp.bfloat16
QB = 256
VMEM_LIMIT = 56 << 20

NN = (((1,), (0,)), ((), ()))
NT = (((1,), (1,)), ((), ()))
TN = (((0,), (0,)), ((), ()))


def mm(a, b, dims=NN):
    return lax.dot_general(a, b, dims, preferred_element_type=F32)


def norm_stats(x):
    mean = jnp.mean(x, axis=-1, keepdims=True)
    c = x - mean
    var = jnp.mean(c * c, axis=-1, keepdims=True)
    r = lax.rsqrt(var + EPS)
    return c * r, r


def norm_back(x, gain, dy):
    xh, r = norm_stats(x)
    gy = dy * gain
    m1 = jnp.mean(gy, axis=-1, keepdims=True)
    m2 = jnp.mean(gy * xh, axis=-1, keepdims=True)
    dz = r * (gy - m1 - xh * m2)
    return dz, jnp.sum(dy * xh, axis=0, keepdims=True)


def turn(y, cos, sin):
    lane = lax.broadcasted_iota(jnp.int32, y.shape, 1) % HD
    other = jnp.where(
        lane < HD // 2, pltpu.roll(y, 128 - HD // 2, 1), pltpu.roll(y, HD // 2, 1)
    )
    return y * cos + other * sin


def vmem(n):
    return [pl.BlockSpec(memory_space=pltpu.VMEM)] * n


def smem():
    return pl.BlockSpec(memory_space=pltpu.SMEM)


def params(**kw):
    return pltpu.CompilerParams(vmem_limit_bytes=VMEM_LIMIT, **kw)


def cost(flops, nbytes, trans=0):
    return pl.CostEstimate(flops=int(flops), bytes_accessed=int(nbytes), transcendentals=int(trans))


def own_kernel(a_ref, w_ref, cos_ref, sin_ref, q_ref, k_ref, v_ref, tmp):
    d = a_ref.shape[1]
    a = a_ref[...]
    tmp[...] = mm(a, w_ref[:, 0:d])
    for g in range(d // 128):
        s = slice(g * 128, g * 128 + 128)
        q_ref[:, s] = (turn(tmp[:, s], cos_ref[...], sin_ref[...]) ).astype(BF)
    tmp[...] = mm(a, w_ref[:, d : 2 * d])
    for g in range(d // 128):
        s = slice(g * 128, g * 128 + 128)
        k_ref[:, s] = turn(tmp[:, s], cos_ref[...], sin_ref[...]).astype(BF)
    v_ref[...] = mm(a, w_ref[:, 2 * d : 3 * d]).astype(BF)


def project_own(a, w, cos, sin):
    rows, d = a.shape
    sd = jax.ShapeDtypeStruct((rows, d), BF)
    return pl.pallas_call(
        own_kernel,
        out_shape=(sd, sd, sd),
        in_specs=vmem(4),
        out_specs=tuple(vmem(3)),
        scratch_shapes=[pltpu.VMEM((rows, d), F32)],
        compiler_params=params(),
        cost_estimate=cost(6 * rows * d * d, 2 * (3 * d * d + 4 * rows * d)),
        name="project_own",
    )(a, w, cos, sin)


def make_bias(info, bias):
    n = bias.shape[0]
    length = info[0]
    t = info[1]
    noisy = t < 2
    odd = t % 2
    base = odd * n
    i = lax.broadcasted_iota(jnp.int32, (n, n), 0)
    j = lax.broadcasted_iota(jnp.int32, (n, n), 1)
    bi = i // BLK
    bj = j // BLK
    odd_lim = jnp.where(odd == 1, length, 0)
    bias[:, 0:n] = jnp.where(j < odd_lim, 0.0, NEG)
    strict_lim = jnp.where(noisy, length - base, 0)
    bias[:, n : 2 * n] = jnp.where((bj < bi) & (j < strict_lim), 0.0, NEG)
    low = jnp.where(noisy, bi, 0)
    seen = (bj <= bi) & (bj >= low) & (j + base < length)
    bias[:, 2 * n : 3 * n] = jnp.where(seen | (i == j), 0.0, NEG)


def attend_kernel(
    info, x_ref, af_ref, as_ref, q_ref, ko_ref, vo_ref, w_ref, cosf_ref, sinf_ref,
    cos_ref, sin_ref, gain_ref,
    o_ref, lse_ref, xm_ref, m_ref, kf_ref, vf_ref, ks_ref, vs_ref,
    tmp, bias,
):
    n, d = x_ref.shape
    pairs = d // 128
    for src, kk, vv, c, s in (
        (af_ref, kf_ref, vf_ref, cosf_ref, sinf_ref),
        (as_ref, ks_ref, vs_ref, cos_ref, sin_ref),
    ):
        a = src[...]
        tmp[...] = mm(a, w_ref[:, d : 2 * d])
        for g in range(pairs):
            sl = slice(g * 128, g * 128 + 128)
            kk[:, sl] = turn(tmp[:, sl], c[...], s[...]).astype(BF)
        vv[...] = mm(a, w_ref[:, 2 * d : 3 * d]).astype(BF)
    make_bias(info, bias)
    lane = lax.broadcasted_iota(jnp.int32, (QB, 128), 1)
    lse_ref[...] = jnp.zeros_like(lse_ref)

    def pair(g, carry):
        sl = pl.ds(pl.multiple_of(g * 128, 128), 128)
        for b in range(n // QB):
            rs = slice(b * QB, b * QB + QB)
            width = (b + 1) * QB
            q2 = q_ref[rs, sl] * SCALE
            keys = (kf_ref[:, sl], ks_ref[0:width, sl], ko_ref[0:width, sl])
            vals = (vf_ref[:, sl], vs_ref[0:width, sl], vo_ref[0:width, sl])
            bs = (
                bias[rs, 0:n],
                bias[rs, n : n + width],
                bias[rs, 2 * n : 2 * n + width],
            )
            outs = []
            for h in range(2):
                mine = (lane < HD) if h == 0 else (lane >= HD)
                qh = jnp.where(mine, q2, jnp.zeros_like(q2))
                sc = [mm(qh, k, NT) + bb for k, bb in zip(keys, bs)]
                top = functools.reduce(
                    jnp.maximum, [jnp.max(s, axis=-1, keepdims=True) for s in sc]
                )
                ex = [jnp.exp(s - top) for s in sc]
                tot = functools.reduce(
                    jnp.add, [jnp.sum(e, axis=-1, keepdims=True) for e in ex]
                )
                acc = functools.reduce(
                    jnp.add, [mm(e.astype(BF), v) for e, v in zip(ex, vals)]
                )
                outs.append(acc / tot)
                head = 2 * g + h
                lse_ref[rs, :] = jnp.where(lane == head, top + jnp.log(tot), lse_ref[rs, :])
            o_ref[rs, sl] = jnp.where(lane < HD, outs[0], outs[1]).astype(BF)
        return carry

    lax.fori_loop(0, pairs, pair, 0)
    xm = x_ref[...].astype(F32) + mm(o_ref[...], w_ref[:, 3 * d : 4 * d], NT)
    xm_ref[...] = xm
    xh, _ = norm_stats(xm)
    m_ref[...] = (xh * gain_ref[...]).astype(BF)


def attend(info, x, af, as_, q, ko, vo, w, cosf, sinf, cos, sin, gain):
    n, d = x.shape
    sd = jax.ShapeDtypeStruct((n, d), BF)
    return pl.pallas_call(
        attend_kernel,
        out_shape=(
            sd,
            jax.ShapeDtypeStruct((n, 128), F32),
            jax.ShapeDtypeStruct((n, d), F32),
            sd, sd, sd, sd, sd,
        ),
        in_specs=[smem()] + vmem(12),
        out_specs=tuple(vmem(8)),
        scratch_shapes=[pltpu.VMEM((n, d), F32), pltpu.VMEM((n, 3 * n), F32)],
        compiler_params=params(),
        cost_estimate=cost(10 * n * d * d + 40 * QB * QB * d * 4, 2 * (4 * d * d + 12 * n * d)),
        name="attend",
    )(info, x, af, as_, q, ko, vo, w, cosf, sinf, cos, sin, gain)


def gelu(u):
    return 0.5 * u * (1.0 + jnp.tanh(GC * (u + GA * (u * u * u))))


def mlp_kernel(xm_ref, m_ref, up_ref, dn_ref, gain_ref, x_ref, a_ref, u_ref, acc):
    step = pl.program_id(0)

    @pl.when(step == 0)
    def _():
        acc[...] = xm_ref[...]

    u = mm(m_ref[...], up_ref[...])
    u_ref[...] = u.astype(BF)
    acc[...] += mm(gelu(u).astype(BF), dn_ref[...], NT)

    @pl.when(step == pl.num_programs(0) - 1)
    def _():
        x = acc[...]
        x_ref[...] = x
        xh, _ = norm_stats(x)
        a_ref[...] = (xh * gain_ref[...]).astype(BF)


def mlp(xm, m, w, gain, fc=512):
    n, d = xm.shape
    ff = w.shape[1] // 2
    steps = ff // fc
    full = pl.BlockSpec((n, d), lambda i: (0, 0))
    return pl.pallas_call(
        mlp_kernel,
        grid=(steps,),
        out_shape=(
            jax.ShapeDtypeStruct((n, d), F32),
            jax.ShapeDtypeStruct((n, d), BF),
            jax.ShapeDtypeStruct((n, ff), BF),
        ),
        in_specs=[
            full,
            full,
            pl.BlockSpec((d, fc), lambda i: (0, i)),
            pl.BlockSpec((d, fc), lambda i: (0, i + steps)),
            pl.BlockSpec((1, d), lambda i: (0, 0)),
        ],
        out_specs=(full, full, pl.BlockSpec((n, fc), lambda i: (0, i))),
        scratch_shapes=[pltpu.VMEM((n, d), F32)],
        compiler_params=params(),
        cost_estimate=cost(4 * n * d * ff, 4 * d * ff + 2 * n * ff + 10 * n * d),
        name="mlp",
    )(xm, m, w, w, gain)


def mlp_back_kernel(
    g_ref, xm_ref, m_ref, u_ref, up_ref, dn_ref, gain_ref,
    gm_ref, go_ref, dup_ref, ddn_ref, dgain_ref,
    gy, gyt, mt, dm,
):
    step = pl.program_id(0)

    @pl.when(step == 0)
    def _():
        gb = g_ref[...].astype(BF)
        gy[...] = gb
        gyt[...] = gb.T
        mt[...] = m_ref[...].T
        dm[...] = jnp.zeros_like(dm)

    u = u_ref[...].astype(F32)
    dh = mm(gy[...], dn_ref[...])
    u2 = u * u
    th = jnp.tanh(GC * (u + GA * (u2 * u)))
    half = 0.5 * (1.0 + th)
    h = (u * half).astype(BF)
    slope = half + 0.5 * u * (1.0 - th * th) * (GC * (1.0 + 3.0 * GA * u2))
    du = (dh * slope).astype(BF)
    dm[...] += mm(du, up_ref[...], NT)
    dup_ref[...] = mm(mt[...], du).astype(BF)
    ddn_ref[...] = mm(gyt[...], h).astype(BF)

    @pl.when(step == pl.num_programs(0) - 1)
    def _():
        dz, dgain = norm_back(xm_ref[...], gain_ref[...], dm[...])
        gm = g_ref[...] + dz
        gm_ref[...] = gm
        go_ref[...] = gm.astype(BF)
        dgain_ref[...] = dgain


def mlp_back(g, xm, m, u, w, gain, fc=512):
    n, d = xm.shape
    ff = w.shape[1] // 2
    steps = ff // fc
    full = pl.BlockSpec((n, d), lambda i: (0, 0))
    row = pl.BlockSpec((1, d), lambda i: (0, 0))
    wide = pl.BlockSpec((d, fc), lambda i: (0, i))
    return pl.pallas_call(
        mlp_back_kernel,
        grid=(steps,),
        out_shape=(
            jax.ShapeDtypeStruct((n, d), F32),
            jax.ShapeDtypeStruct((n, d), BF),
            jax.ShapeDtypeStruct((d, ff), BF),
            jax.ShapeDtypeStruct((d, ff), BF),
            jax.ShapeDtypeStruct((1, d), F32),
        ),
        in_specs=[
            full,
            full,
            full,
            pl.BlockSpec((n, fc), lambda i: (0, i)),
            wide,
            pl.BlockSpec((d, fc), lambda i: (0, i + steps)),
            row,
        ],
        out_specs=(full, full, wide, wide, row),
        scratch_shapes=[
            pltpu.VMEM((n, d), BF),
            pltpu.VMEM((d, n), BF),
            pltpu.VMEM((d, n), BF),
            pltpu.VMEM((n, d), F32),
        ],
        compiler_params=params(),
        cost_estimate=cost(8 * n * d * ff, 8 * d * ff + 2 * n * ff + 16 * n * d),
        name="mlp_back",
    )(g, xm, m, u, w, w, gain)


def attend_back_kernel(
    info, go_ref, o_ref, lse_ref, q_ref, kf_ref, vf_ref, ks_ref, vs_ref, ko_ref, vo_ref,
    w_ref, cosf_ref, sinf_ref, cos_ref, sin_ref,
    dq_ref, dkf_ref, dvf_ref, dks_ref, dvs_ref, dko_ref, dvo_ref, daf_ref, das_ref, dao_ref,
    do_s, bias, dqa, dka, dva,
):
    n, d = go_ref.shape
    pairs = d // 128
    make_bias(info, bias)
    do_s[...] = mm(go_ref[...], w_ref[:, 3 * d : 4 * d]).astype(BF)
    lane_q = lax.broadcasted_iota(jnp.int32, (QB, 128), 1)

    def pair(g, carry):
        sl = pl.ds(pl.multiple_of(g * 128, 128), 128)
        dqa[...] = jnp.zeros_like(dqa)
        dka[...] = jnp.zeros_like(dka)
        dva[...] = jnp.zeros_like(dva)
        for b in range(n // QB):
            rs = slice(b * QB, b * QB + QB)
            q2 = q_ref[rs, sl] * SCALE
            do2 = do_s[rs, sl]
            prod = do2.astype(F32) * o_ref[rs, sl].astype(F32)
            lses = lse_ref[rs, :]
            for h in range(2):
                mine = (lane_q < HD) if h == 0 else (lane_q >= HD)
                qh = jnp.where(mine, q2, jnp.zeros_like(q2))
                doh = jnp.where(mine, do2, jnp.zeros_like(do2))
                dsum = jnp.sum(jnp.where(mine, prod, 0.0), axis=-1, keepdims=True)
                ls = jnp.sum(
                    jnp.where(lane_q == 2 * g + h, lses, 0.0), axis=-1, keepdims=True
                )
                for seg, (kr, vr) in enumerate(
                    ((kf_ref, vf_ref), (ks_ref, vs_ref), (ko_ref, vo_ref))
                ):
                    tiles = n // QB if seg == 0 else b + 1
                    for c in range(tiles):
                        cs = slice(c * QB, c * QB + QB)
                        col = seg * n + c * QB
                        k2 = kr[cs, sl]
                        v2 = vr[cs, sl]
                        s = mm(qh, k2, NT) + bias[rs, col : col + QB]
                        p = jnp.exp(s - ls)
                        dp = mm(doh, v2, NT)
                        ds = (p * (dp - dsum)).astype(BF)
                        pb = p.astype(BF)
                        acc = slice(seg * n + c * QB, seg * n + c * QB + QB)
                        dva[acc, :] += mm(pb, doh, TN)
                        dka[acc, :] += mm(ds, qh, TN)
                        kh = jnp.where(mine, k2, jnp.zeros_like(k2))
                        dqa[rs, :] += mm(ds, kh)
        dq_ref[:, sl] = turn(dqa[...] * SCALE, cos_ref[...], -sin_ref[...]).astype(BF)
        dkf_ref[:, sl] = turn(dka[0:n, :], cosf_ref[...], -sinf_ref[...]).astype(BF)
        dks_ref[:, sl] = turn(dka[n : 2 * n, :], cos_ref[...], -sin_ref[...]).astype(BF)
        dko_ref[:, sl] = turn(dka[2 * n : 3 * n, :], cos_ref[...], -sin_ref[...]).astype(BF)
        dvf_ref[:, sl] = dva[0:n, :].astype(BF)
        dvs_ref[:, sl] = dva[n : 2 * n, :].astype(BF)
        dvo_ref[:, sl] = dva[2 * n : 3 * n, :].astype(BF)
        return carry

    lax.fori_loop(0, pairs, pair, 0)
    wk = w_ref[:, d : 2 * d]
    wv = w_ref[:, 2 * d : 3 * d]
    daf_ref[...] = (mm(dkf_ref[...], wk, NT) + mm(dvf_ref[...], wv, NT)).astype(BF)
    das_ref[...] = (mm(dks_ref[...], wk, NT) + mm(dvs_ref[...], wv, NT)).astype(BF)
    dao_ref[...] = (
        mm(dko_ref[...], wk, NT) + mm(dvo_ref[...], wv, NT) + mm(dq_ref[...], w_ref[:, 0:d], NT)
    )


def attend_back(info, go, o, lse, q, kf, vf, ks, vs, ko, vo, w, cosf, sinf, cos, sin):
    n, d = go.shape
    sd = jax.ShapeDtypeStruct((n, d), BF)
    return pl.pallas_call(
        attend_back_kernel,
        out_shape=(sd,) * 9 + (jax.ShapeDtypeStruct((n, d), F32),),
        in_specs=[smem()] + vmem(15),
        out_specs=tuple(vmem(10)),
        scratch_shapes=[
            pltpu.VMEM((n, d), BF),
            pltpu.VMEM((n, 3 * n), F32),
            pltpu.VMEM((n, 128), F32),
            pltpu.VMEM((3 * n, 128), F32),
            pltpu.VMEM((3 * n, 128), F32),
        ],
        compiler_params=params(),
        cost_estimate=cost(16 * n * d * d + 100 * QB * QB * d * 4, 2 * (4 * d * d + 24 * n * d)),
        name="attend_back",
    )(info, go, o, lse, q, kf, vf, ks, vs, ko, vo, w, cosf, sinf, cos, sin)


def weight_kernel(
    ao_ref, af_ref, as_ref, go_ref, o_ref, dq_ref, dkf_ref, dvf_ref, dks_ref, dvs_ref,
    dko_ref, dvo_ref, dw_ref,
):
    n, d = ao_ref.shape
    aot = ao_ref[...].T
    aft = af_ref[...].T
    ast = as_ref[...].T
    dw_ref[:, 0:d] = mm(aot, dq_ref[...]).astype(BF)
    dw_ref[:, d : 2 * d] = (
        mm(aot, dko_ref[...]) + mm(aft, dkf_ref[...]) + mm(ast, dks_ref[...])
    ).astype(BF)
    dw_ref[:, 2 * d : 3 * d] = (
        mm(aot, dvo_ref[...]) + mm(aft, dvf_ref[...]) + mm(ast, dvs_ref[...])
    ).astype(BF)
    dw_ref[:, 3 * d : 4 * d] = mm(go_ref[...].T, o_ref[...]).astype(BF)


def weight_grads(ao, af, as_, go, o, dq, dkf, dvf, dks, dvs, dko, dvo):
    n, d = ao.shape
    return pl.pallas_call(
        weight_kernel,
        out_shape=jax.ShapeDtypeStruct((d, 4 * d), BF),
        in_specs=vmem(12),
        out_specs=pl.BlockSpec(memory_space=pltpu.VMEM),
        compiler_params=params(),
        cost_estimate=cost(16 * n * d * d, 2 * (4 * d * d + 12 * n * d)),
        name="weight_grads",
    )(ao, af, as_, go, o, dq, dkf, dvf, dks, dvs, dko, dvo)


def norm_back_kernel(gm_ref, x_ref, da_ref, r1_ref, r2_ref, gain_ref, g_ref, dgain_ref):
    da = da_ref[...] + r1_ref[...].astype(F32) + r2_ref[...].astype(F32)
    dz, dgain = norm_back(x_ref[...].astype(F32), gain_ref[...], da)
    g_ref[...] = gm_ref[...] + dz
    dgain_ref[...] = dgain


def norm_back_call(gm, x, da, r1, r2, gain):
    n, d = gm.shape
    return pl.pallas_call(
        norm_back_kernel,
        out_shape=(jax.ShapeDtypeStruct((n, d), F32), jax.ShapeDtypeStruct((1, d), F32)),
        in_specs=vmem(6),
        out_specs=tuple(vmem(2)),
        compiler_params=params(),
        cost_estimate=cost(20 * n * d, 20 * n * d),
        name="norm_back",
    )(gm, x, da, r1, r2, gain)


def first_norm_kernel(x_ref, gain_ref, a_ref):
    xh, _ = norm_stats(x_ref[...].astype(F32))
    a_ref[...] = (xh * gain_ref[...]).astype(BF)


def first_norm(x, gain):
    n, d = x.shape
    return pl.pallas_call(
        first_norm_kernel,
        out_shape=jax.ShapeDtypeStruct((n, d), BF),
        in_specs=vmem(2),
        out_specs=pl.BlockSpec(memory_space=pltpu.VMEM),
        compiler_params=params(),
        cost_estimate=cost(10 * n * d, 4 * n * d),
        name="first_norm",
    )(x, gain)


def send(x, pairs):
    return lax.ppermute(x, "tensor", pairs)


def spread_clean(a, t):
    p1 = send(a, [(2, 3), (3, 1)])
    p2 = send(a, [(2, 1)])
    p3 = send(p2, [(1, 0)])
    return jnp.where(t == 1, p2, p1), jnp.where(t == 1, p1, p3)


def return_clean(daf, das, t):
    q1 = send(das, [(0, 1)])
    q3 = send(jnp.where(t == 1, das, daf), [(1, 3), (3, 2)])
    q2 = send((daf.astype(F32) + q1.astype(F32)).astype(BF), [(1, 2)])
    return q2, q3


def gather_weights(pieces, dp):
    count = lax.axis_size("dp")
    outs = []
    for w in pieces:
        rows = w.shape[0] // count
        mine = lax.dynamic_slice_in_dim(w, dp * rows, rows, 0)
        all_z = lax.all_gather(mine, "tensor", axis=0)
        outs.append(all_z.transpose(1, 0, 2).reshape(rows, -1))
    return lax.all_gather(jnp.concatenate(outs, axis=1), "dp", axis=0, tiled=True)


def reduce_weights(dw, widths):
    zs = lax.axis_size("tensor")
    part = lax.psum_scatter(dw, "dp", scatter_dimension=0, tiled=True)
    rows = part.shape[0]
    at = 0
    cols = []
    for w in widths:
        cols.append(part[:, at : at + w].reshape(rows, zs, w // zs).transpose(1, 0, 2))
        at += w
    mine = lax.psum_scatter(jnp.concatenate(cols, axis=2), "tensor", scatter_dimension=0, tiled=False)
    full = lax.all_gather(mine, "dp", axis=0, tiled=True).astype(F32)
    out = []
    at = 0
    for w in widths:
        out.append(full[:, at : at + w // zs])
        at += w // zs
    return out


def sum_all(x):
    n = lax.axis_size("dp")
    step = 1
    while step < n:
        x = x + lax.ppermute(x, "dp", [(i, i ^ step) for i in range(n)])
        step *= 2
    for step in (1, 2):
        x = x + lax.ppermute(x, "tensor", [(i, i ^ step) for i in range(4)])
    return x


def on_device(
    tokens, lengths, noise_mask, cotangent, attn_gain, query_weight, key_weight, value_weight,
    out_weight, mlp_gain, up_weight, down_weight,
):
    n, d = tokens.shape
    dp = lax.axis_index("dp")
    t = lax.axis_index("tensor")
    info = jnp.stack([lengths[0], t]).astype(jnp.int32)
    base = (t % 2) * n

    position = jnp.arange(LMAX, dtype=jnp.int32).astype(F32)
    frequency = jnp.exp(
        -math.log(10000.0) * jnp.arange(HD // 2, dtype=jnp.int32).astype(F32) / (HD // 2)
    )
    angles = position[:, None] * frequency[None, :]
    cos1 = jnp.cos(angles)
    sin1 = jnp.sin(angles)
    cos_all = jnp.concatenate([cos1] * 4, axis=1)
    sin_all = jnp.concatenate([-sin1, sin1] * 2, axis=1)
    cosf, sinf = cos_all[:n], sin_all[:n]
    cos = lax.dynamic_slice_in_dim(cos_all, base, n, 0)
    sin = lax.dynamic_slice_in_dim(sin_all, base, n, 0)

    pos = base + jnp.arange(n, dtype=jnp.int32)
    masked = lax.dynamic_slice_in_dim(noise_mask[0], base, n, 0)
    weight = ((pos < lengths[0]) & ((t >= 2) | (masked == 1))).astype(F32)

    wa = []
    wm = []
    for layer in range(LAYERS):
        wa.append(
            gather_weights(
                [query_weight[layer], key_weight[layer], value_weight[layer], out_weight[layer].T],
                dp,
            )
        )
        wm.append(gather_weights([up_weight[layer], down_weight[layer].T], dp))

    saved = []
    x = tokens
    a = first_norm(tokens, attn_gain[0:1])
    for layer in range(LAYERS):
        af, as_ = spread_clean(a, t)
        q, ko, vo = project_own(a, wa[layer], cos, sin)
        o, lse, xm, m, kf, vf, ks, vs = attend(
            info, x, af, as_, q, ko, vo, wa[layer], cosf, sinf, cos, sin, mlp_gain[layer : layer + 1]
        )
        nxt = min(layer + 1, LAYERS - 1)
        x_next, a_next, u = mlp(xm, m, wm[layer], attn_gain[nxt : nxt + 1])
        saved.append((x, a, af, as_, q, kf, vf, ks, vs, ko, vo, o, lse, xm, m, u))
        x, a = x_next, a_next
    block_out = x

    g = cotangent.astype(F32) * weight[:, None]
    gains = [None] * (2 * LAYERS)
    grads = [None] * LAYERS
    for layer in reversed(range(LAYERS)):
        x, a, af, as_, q, kf, vf, ks, vs, ko, vo, o, lse, xm, m, u = saved[layer]
        gm, go, dup, ddn, gains[LAYERS + layer] = mlp_back(
            g, xm, m, u, wm[layer], mlp_gain[layer : layer + 1]
        )
        dq, dkf, dvf, dks, dvs, dko, dvo, daf, das, dao = attend_back(
            info, go, o, lse, q, kf, vf, ks, vs, ko, vo, wa[layer], cosf, sinf, cos, sin
        )
        r1, r2 = return_clean(daf, das, t)
        dwa = weight_grads(a, af, as_, go, o, dq, dkf, dvf, dks, dvs, dko, dvo)
        ups = reduce_weights(jnp.concatenate([dup, ddn], axis=1), (dup.shape[1], ddn.shape[1]))
        ats = reduce_weights(dwa, (d, d, d, d))
        g, gains[layer] = norm_back_call(gm, x, dao, r1, r2, attn_gain[layer : layer + 1])
        grads[layer] = (ats[0], ats[1], ats[2], ats[3].T, ups[0], ups[1].T)
    gain_sums = sum_all(jnp.concatenate(gains, axis=0))
    stacked = [jnp.stack([grads[layer][i] for layer in range(LAYERS)]) for i in range(6)]
    return (
        block_out, g, gain_sums[:LAYERS], stacked[0], stacked[1], stacked[2], stacked[3],
        gain_sums[LAYERS:], stacked[4], stacked[5],
    )


def solution(mesh):
    rows = P(("dp", "tensor"), None)
    cols = P(None, None, "tensor")
    mids = P(None, "tensor", None)
    return jax.shard_map(
        on_device,
        mesh=mesh,
        in_specs=(
            rows, P("dp"), P("dp", None), rows, P(), cols, cols, cols, mids, P(), cols, mids,
        ),
        out_specs=(rows, rows, P(), cols, cols, cols, mids, P(), cols, mids),
        check_vma=False,
    )
```

```python
import functools
import math

import jax
import jax.numpy as jnp
from jax import lax
from jax.experimental import pallas as pl
from jax.experimental.pallas import tpu as pltpu
from jax.sharding import PartitionSpec as P

HD = 64
BLK = 16
LMAX = 1024
LAYERS = 2
EPS = 1e-05
NEG = -1e30
SCALE = 1.0 / math.sqrt(HD)
GC = math.sqrt(2.0 / math.pi)
GA = 0.044715
F32 = jnp.float32
BF = jnp.bfloat16
QB = 256
VMEM_LIMIT = 56 << 20

NN = (((1,), (0,)), ((), ()))
NT = (((1,), (1,)), ((), ()))
TN = (((0,), (0,)), ((), ()))


def mm(a, b, dims=NN):
    return lax.dot_general(a, b, dims, preferred_element_type=F32)


def norm_stats(x):
    mean = jnp.mean(x, axis=-1, keepdims=True)
    c = x - mean
    var = jnp.mean(c * c, axis=-1, keepdims=True)
    r = lax.rsqrt(var + EPS)
    return c * r, r


def norm_back(x, gain, dy):
    xh, r = norm_stats(x)
    gy = dy * gain
    m1 = jnp.mean(gy, axis=-1, keepdims=True)
    m2 = jnp.mean(gy * xh, axis=-1, keepdims=True)
    dz = r * (gy - m1 - xh * m2)
    return dz, jnp.sum(dy * xh, axis=0, keepdims=True)


def turn(y, cos, sin):
    lane = lax.broadcasted_iota(jnp.int32, y.shape, 1) % HD
    other = jnp.where(
        lane < HD // 2, pltpu.roll(y, 128 - HD // 2, 1), pltpu.roll(y, HD // 2, 1)
    )
    return y * cos + other * sin


def vmem(n):
    return [pl.BlockSpec(memory_space=pltpu.VMEM)] * n


def smem():
    return pl.BlockSpec(memory_space=pltpu.SMEM)


def params(**kw):
    return pltpu.CompilerParams(vmem_limit_bytes=VMEM_LIMIT, **kw)


def cost(flops, nbytes, trans=0):
    return pl.CostEstimate(flops=int(flops), bytes_accessed=int(nbytes), transcendentals=int(trans))


MESH = pl.DeviceIdType.MESH
BITS = 3
ORDERS = ((0, 1, 2), (0, 2, 1))


def bit_of(dp, b):
    return dp // (1 << b) % 2


def slot_of(dp, order):
    out = 0
    for b in order:
        out = out * 2 + bit_of(dp, b)
    return out


def partner(dp, b):
    return dp + (1 - 2 * bit_of(dp, b)) * (1 << b)


def greet():
    dp = lax.axis_index("dp")
    t = lax.axis_index("tensor")
    barrier = pltpu.get_barrier_semaphore()
    for b in range(BITS):
        pl.semaphore_signal(barrier, inc=1, device_id=(partner(dp, b), t), device_id_type=MESH)
    pl.semaphore_wait(barrier, BITS)


def aligned(x):
    return pl.multiple_of(x, 16)


class Gather:
    def __init__(self, piece, whole, send, recv, local):
        self.piece, self.whole, self.send, self.recv, self.local = piece, whole, send, recv, local
        self.dp = lax.axis_index("dp")
        self.t = lax.axis_index("tensor")
        self.rows = piece.shape[0]
        self.half = piece.shape[1] // 2

    def cols(self, i):
        return pl.ds(i * self.half, self.half)

    def own(self, i):
        slot = slot_of(self.dp, ORDERS[i])
        return pltpu.make_async_copy(
            self.piece.at[:, self.cols(i)],
            self.whole.at[pl.ds(aligned(slot * self.rows), self.rows), self.cols(i)],
            self.local.at[i],
        )

    def copy(self, s, i):
        b = ORDERS[i][BITS - 1 - s]
        size = self.rows << s
        at = slot_of(self.dp, ORDERS[i]) // (1 << s) * size
        there = self.whole.at[pl.ds(aligned(at), size), self.cols(i)]
        return pltpu.make_async_remote_copy(
            src_ref=self.piece.at[:, self.cols(i)] if s == 0 else there,
            dst_ref=there,
            send_sem=self.send.at[2 * s + i],
            recv_sem=self.recv.at[2 * s + i],
            device_id=(partner(self.dp, b), self.t),
            device_id_type=MESH,
        )

    def start(self, s):
        for i in range(2):
            self.copy(s, i).start()
            if s == 0:
                self.own(i).start()

    def wait(self, s):
        for i in range(2):
            self.copy(s, i).wait()
            if s == 0:
                self.own(i).wait()

    @staticmethod
    def scratch():
        return [
            pltpu.SemaphoreType.DMA((2 * BITS,)),
            pltpu.SemaphoreType.DMA((2 * BITS,)),
            pltpu.SemaphoreType.DMA((2,)),
        ]


class Reduce:
    def __init__(self, src, out, scratch):
        self.src, self.out = src, out
        self.keep = scratch[0:2]
        self.got = (scratch[2 : 2 + BITS], scratch[2 + BITS : 2 + 2 * BITS])
        self.send, self.recv, self.local = scratch[2 + 2 * BITS :]
        self.dp = lax.axis_index("dp")
        self.t = lax.axis_index("tensor")
        self.full = src[0].shape[0]

    def offset(self, s, i):
        at = 0
        for j in range(1, s):
            at = at + bit_of(self.dp, ORDERS[i][j]) * (self.full >> (j + 1))
        return at

    def copy(self, s, i):
        b = ORDERS[i][s]
        size = self.full >> (s + 1)
        at = (1 - bit_of(self.dp, b)) * size
        if s == 0:
            there = self.src[i].at[pl.ds(aligned(at), size), :]
        else:
            there = self.keep[i].at[pl.ds(aligned(self.offset(s, i) + at), size), :]
        return pltpu.make_async_remote_copy(
            src_ref=there,
            dst_ref=self.got[i][s],
            send_sem=self.send.at[2 * s + i],
            recv_sem=self.recv.at[2 * s + i],
            device_id=(partner(self.dp, b), self.t),
            device_id_type=MESH,
        )

    def own(self, i):
        size = self.full // 2
        at = bit_of(self.dp, ORDERS[i][0]) * size
        return pltpu.make_async_copy(
            self.src[i].at[pl.ds(aligned(at), size), :], self.keep[i], self.local.at[i]
        )

    def start(self, s):
        for i in range(2):
            self.copy(s, i).start()
            if s == 0:
                self.own(i).start()

    def wait(self, s):
        for i in range(2):
            self.copy(s, i).wait()
            if s == 0:
                self.own(i).wait()
            size = self.full >> (s + 1)
            base = self.offset(s + 1, i)
            keep, got = self.keep[i], self.got[i][s]
            last = s == BITS - 1
            step = 48 if size % 48 == 0 else size

            def add(j, carry):
                rows = pl.ds(aligned(base + j * step), step)
                here = pl.ds(aligned(j * step), step)
                total = (keep[rows, :].astype(F32) + got[here, :].astype(F32)).astype(BF)
                if last:
                    self.out[i][here, :] = total
                else:
                    keep[rows, :] = total
                return carry

            lax.fori_loop(0, size // step, add, 0)

    @staticmethod
    def scratch(full, widths):
        out = [pltpu.VMEM((full // 2, w), BF) for w in widths]
        for w in widths:
            out += [pltpu.VMEM((full >> (s + 1), w), BF) for s in range(BITS)]
        return out + [
            pltpu.SemaphoreType.DMA((2 * BITS,)),
            pltpu.SemaphoreType.DMA((2 * BITS,)),
            pltpu.SemaphoreType.DMA((2,)),
        ]

    COUNT = 2 + 2 * BITS + 3


def pump(comms, point, points):
    for s in range(BITS):
        if s * points // BITS == point:
            for c in comms:
                if s > 0:
                    c.wait(s - 1)
                c.start(s)


def drain(comms):
    for c in comms:
        c.wait(BITS - 1)


def any_spec(n=1):
    return [pl.BlockSpec(memory_space=pl.ANY)] * n


def begin_kernel(p_ref, w_ref, *sems):
    greet()
    comms = [Gather(p_ref, w_ref, *sems)]
    for point in range(BITS):
        pump(comms, point, BITS)
    drain(comms)


def gather_call(piece):
    rows, n = piece.shape
    return pl.pallas_call(
        begin_kernel,
        out_shape=jax.ShapeDtypeStruct((rows << BITS, n), BF),
        in_specs=vmem(1),
        out_specs=any_spec()[0],
        scratch_shapes=Gather.scratch(),
        compiler_params=params(collective_id=0, has_side_effects=True),
        cost_estimate=cost(1, 10 * rows * n * 16),
        name="gather_weights",
    )(piece)


def end_kernel(count, *refs):
    greet()
    pieces, wholes, sems = refs[:count], refs[count : 2 * count], refs[2 * count :]
    comms = [
        Gather(p, w, *sems[3 * i : 3 * i + 3]) for i, (p, w) in enumerate(zip(pieces, wholes))
    ]
    for point in range(BITS):
        pump(comms, point, BITS)
    drain(comms)


def gather_many(pieces):
    count = len(pieces)
    return pl.pallas_call(
        functools.partial(end_kernel, count),
        out_shape=tuple(
            jax.ShapeDtypeStruct((p.shape[0] << BITS, p.shape[1]), BF) for p in pieces
        ),
        in_specs=vmem(count),
        out_specs=tuple(any_spec(count)),
        scratch_shapes=Gather.scratch() * count,
        compiler_params=params(collective_id=1, has_side_effects=True),
        cost_estimate=cost(1, 10 * sum(p.size for p in pieces) * 16),
        name="gather_grads",
    )(*pieces)


def own_kernel(a_ref, w_ref, cos_ref, sin_ref, q_ref, k_ref, v_ref, tmp):
    d = a_ref.shape[1]
    a = a_ref[...]
    tmp[...] = mm(a, w_ref[:, 0:d])
    for g in range(d // 128):
        s = slice(g * 128, g * 128 + 128)
        q_ref[:, s] = (turn(tmp[:, s], cos_ref[...], sin_ref[...]) ).astype(BF)
    tmp[...] = mm(a, w_ref[:, d : 2 * d])
    for g in range(d // 128):
        s = slice(g * 128, g * 128 + 128)
        k_ref[:, s] = turn(tmp[:, s], cos_ref[...], sin_ref[...]).astype(BF)
    v_ref[...] = mm(a, w_ref[:, 2 * d : 3 * d]).astype(BF)


def project_own(a, w, cos, sin):
    rows, d = a.shape
    sd = jax.ShapeDtypeStruct((rows, d), BF)
    return pl.pallas_call(
        own_kernel,
        out_shape=(sd, sd, sd),
        in_specs=vmem(4),
        out_specs=tuple(vmem(3)),
        scratch_shapes=[pltpu.VMEM((rows, d), F32)],
        compiler_params=params(),
        cost_estimate=cost(6 * rows * d * d, 2 * (3 * d * d + 4 * rows * d)),
        name="project_own",
    )(a, w, cos, sin)


def make_bias(info, bias):
    n = bias.shape[0]
    length = info[0]
    t = info[1]
    noisy = t < 2
    odd = t % 2
    base = odd * n
    i = lax.broadcasted_iota(jnp.int32, (n, n), 0)
    j = lax.broadcasted_iota(jnp.int32, (n, n), 1)
    bi = i // BLK
    bj = j // BLK
    odd_lim = jnp.where(odd == 1, length, 0)
    bias[:, 0:n] = jnp.where(j < odd_lim, 0.0, NEG)
    strict_lim = jnp.where(noisy, length - base, 0)
    bias[:, n : 2 * n] = jnp.where((bj < bi) & (j < strict_lim), 0.0, NEG)
    low = jnp.where(noisy, bi, 0)
    seen = (bj <= bi) & (bj >= low) & (j + base < length)
    bias[:, 2 * n : 3 * n] = jnp.where(seen | (i == j), 0.0, NEG)


def attend_kernel(
    info, x_ref, af_ref, as_ref, q_ref, ko_ref, vo_ref, w_ref, cosf_ref, sinf_ref,
    cos_ref, sin_ref, gain_ref, p_ref,
    o_ref, lse_ref, xm_ref, m_ref, kf_ref, vf_ref, ks_ref, vs_ref, wn_ref,
    tmp, bias, *sems,
):
    n, d = x_ref.shape
    pairs = d // 128
    greet()
    comms = [Gather(p_ref, wn_ref, *sems)]
    pump(comms, 0, 3)
    for src, kk, vv, c, s in (
        (af_ref, kf_ref, vf_ref, cosf_ref, sinf_ref),
        (as_ref, ks_ref, vs_ref, cos_ref, sin_ref),
    ):
        a = src[...]
        tmp[...] = mm(a, w_ref[:, d : 2 * d])
        for g in range(pairs):
            sl = slice(g * 128, g * 128 + 128)
            kk[:, sl] = turn(tmp[:, sl], c[...], s[...]).astype(BF)
        vv[...] = mm(a, w_ref[:, 2 * d : 3 * d]).astype(BF)
    make_bias(info, bias)
    lane = lax.broadcasted_iota(jnp.int32, (QB, 128), 1)
    lse_ref[...] = jnp.zeros_like(lse_ref)

    def pair(g, carry):
        sl = pl.ds(pl.multiple_of(g * 128, 128), 128)
        for b in range(n // QB):
            rs = slice(b * QB, b * QB + QB)
            width = (b + 1) * QB
            q2 = q_ref[rs, sl] * SCALE
            keys = (kf_ref[:, sl], ks_ref[0:width, sl], ko_ref[0:width, sl])
            vals = (vf_ref[:, sl], vs_ref[0:width, sl], vo_ref[0:width, sl])
            bs = (
                bias[rs, 0:n],
                bias[rs, n : n + width],
                bias[rs, 2 * n : 2 * n + width],
            )
            outs = []
            for h in range(2):
                mine = (lane < HD) if h == 0 else (lane >= HD)
                qh = jnp.where(mine, q2, jnp.zeros_like(q2))
                sc = [mm(qh, k, NT) + bb for k, bb in zip(keys, bs)]
                top = functools.reduce(
                    jnp.maximum, [jnp.max(s, axis=-1, keepdims=True) for s in sc]
                )
                ex = [jnp.exp(s - top) for s in sc]
                tot = functools.reduce(
                    jnp.add, [jnp.sum(e, axis=-1, keepdims=True) for e in ex]
                )
                acc = functools.reduce(
                    jnp.add, [mm(e.astype(BF), v) for e, v in zip(ex, vals)]
                )
                outs.append(acc / tot)
                head = 2 * g + h
                lse_ref[rs, :] = jnp.where(lane == head, top + jnp.log(tot), lse_ref[rs, :])
            o_ref[rs, sl] = jnp.where(lane < HD, outs[0], outs[1]).astype(BF)
        return carry

    pump(comms, 1, 3)
    lax.fori_loop(0, pairs // 2, pair, 0)
    pump(comms, 2, 3)
    lax.fori_loop(pairs // 2, pairs, pair, 0)
    xm = x_ref[...].astype(F32) + mm(o_ref[...], w_ref[:, 3 * d : 4 * d], NT)
    xm_ref[...] = xm
    xh, _ = norm_stats(xm)
    m_ref[...] = (xh * gain_ref[...]).astype(BF)
    drain(comms)


def attend(info, x, af, as_, q, ko, vo, w, cosf, sinf, cos, sin, gain, piece, cid):
    n, d = x.shape
    sd = jax.ShapeDtypeStruct((n, d), BF)
    return pl.pallas_call(
        attend_kernel,
        out_shape=(
            sd,
            jax.ShapeDtypeStruct((n, 128), F32),
            jax.ShapeDtypeStruct((n, d), F32),
            sd, sd, sd, sd, sd,
            jax.ShapeDtypeStruct((piece.shape[0] << BITS, piece.shape[1]), BF),
        ),
        in_specs=[smem()] + vmem(13),
        out_specs=tuple(vmem(8) + any_spec()),
        scratch_shapes=[pltpu.VMEM((n, d), F32), pltpu.VMEM((n, 3 * n), F32)] + Gather.scratch(),
        compiler_params=params(collective_id=cid, has_side_effects=True),
        cost_estimate=cost(10 * n * d * d + 40 * QB * QB * d * 4, 2 * (4 * d * d + 12 * n * d)),
        name="attend",
    )(info, x, af, as_, q, ko, vo, w, cosf, sinf, cos, sin, gain, piece)


def gelu(u):
    return 0.5 * u * (1.0 + jnp.tanh(GC * (u + GA * (u * u * u))))


def grid_points(comms, step, last):
    for s in range(BITS):
        at = s * last // BITS

        @pl.when(step == at)
        def _(s=s):
            for c in comms:
                if s > 0:
                    c.wait(s - 1)
                c.start(s)


def mlp_kernel(*refs):
    xm_ref, m_ref, up_ref, dn_ref, gain_ref = refs[:5]
    step = pl.program_id(0)
    last = pl.num_programs(0) - 1
    comms = []
    if len(refs) == 9:
        x_ref, a_ref, u_ref, acc = refs[5:]
    else:
        p_ref, x_ref, a_ref, u_ref, wn_ref, acc = refs[5:11]
        comms = [Gather(p_ref, wn_ref, *refs[11:])]

        @pl.when(step == 0)
        def _():
            greet()

        grid_points(comms, step, MLP_STEPS - 1)

    @pl.when(step == 0)
    def _():
        acc[...] = xm_ref[...]

    u = mm(m_ref[...], up_ref[...])
    u_ref[...] = u.astype(BF)
    acc[...] += mm(gelu(u).astype(BF), dn_ref[...], NT)

    @pl.when(step == pl.num_programs(0) - 1)
    def _():
        x = acc[...]
        x_ref[...] = x
        xh, _ = norm_stats(x)
        a_ref[...] = (xh * gain_ref[...]).astype(BF)
        drain(comms)


MLP_STEPS = 6


def mlp(xm, m, w, gain, piece=None):
    n, d = xm.shape
    ff = w.shape[1] // 2
    steps = MLP_STEPS
    fc = ff // steps
    full = pl.BlockSpec((n, d), lambda i: (0, 0))
    extra = [] if piece is None else [piece]
    return pl.pallas_call(
        mlp_kernel,
        grid=(steps,),
        out_shape=(
            jax.ShapeDtypeStruct((n, d), F32),
            jax.ShapeDtypeStruct((n, d), BF),
            jax.ShapeDtypeStruct((n, ff), BF),
        )
        + tuple(jax.ShapeDtypeStruct((p.shape[0] << BITS, p.shape[1]), BF) for p in extra),
        in_specs=[
            full,
            full,
            pl.BlockSpec((d, fc), lambda i: (0, i)),
            pl.BlockSpec((d, fc), lambda i: (0, i + steps)),
            pl.BlockSpec((1, d), lambda i: (0, 0)),
        ]
        + vmem(len(extra)),
        out_specs=(full, full, pl.BlockSpec((n, fc), lambda i: (0, i))) + tuple(any_spec(len(extra))),
        scratch_shapes=[pltpu.VMEM((n, d), F32)] + (Gather.scratch() if extra else []),
        compiler_params=params(collective_id=3, has_side_effects=True) if extra else params(),
        cost_estimate=cost(4 * n * d * ff, 4 * d * ff + 2 * n * ff + 10 * n * d),
        name="mlp",
    )(xm, m, w, w, gain, *extra)


def mlp_back_kernel(*refs):
    g_ref, xm_ref, m_ref, u_ref, up_ref, dn_ref, gain_ref = refs[:7]
    step = pl.program_id(0)
    comms = []
    if len(refs) == 16:
        gm_ref, go_ref, dup_ref, ddn_ref, dgain_ref, gy, gyt, mt, dm = refs[7:]
    else:
        da_ref, db_ref, gm_ref, go_ref, dup_ref, ddn_ref, dgain_ref, sa_ref, sb_ref = refs[7:16]
        gy, gyt, mt, dm = refs[16:20]
        comms = [Reduce((da_ref, db_ref), (sa_ref, sb_ref), refs[20:])]

        @pl.when(step == 0)
        def _():
            greet()

        grid_points(comms, step, MLP_STEPS - 1)

    @pl.when(step == 0)
    def _():
        gb = g_ref[...].astype(BF)
        gy[...] = gb
        gyt[...] = gb.T
        mt[...] = m_ref[...].T
        dm[...] = jnp.zeros_like(dm)

    u = u_ref[...].astype(F32)
    dh = mm(gy[...], dn_ref[...])
    u2 = u * u
    th = jnp.tanh(GC * (u + GA * (u2 * u)))
    half = 0.5 * (1.0 + th)
    h = (u * half).astype(BF)
    slope = half + 0.5 * u * (1.0 - th * th) * (GC * (1.0 + 3.0 * GA * u2))
    du = (dh * slope).astype(BF)
    dm[...] += mm(du, up_ref[...], NT)
    dup_ref[...] = mm(mt[...], du).astype(BF)
    ddn_ref[...] = mm(gyt[...], h).astype(BF)

    @pl.when(step == pl.num_programs(0) - 1)
    def _():
        dz, dgain = norm_back(xm_ref[...], gain_ref[...], dm[...])
        gm = g_ref[...] + dz
        gm_ref[...] = gm
        go_ref[...] = gm.astype(BF)
        dgain_ref[...] = dgain
        drain(comms)


def mlp_back(g, xm, m, u, w, gain, extra=()):
    n, d = xm.shape
    ff = w.shape[1] // 2
    steps = MLP_STEPS
    fc = ff // steps
    sums = [jax.ShapeDtypeStruct((e.shape[0] >> BITS, e.shape[1]), BF) for e in extra]
    full = pl.BlockSpec((n, d), lambda i: (0, 0))
    row = pl.BlockSpec((1, d), lambda i: (0, 0))
    wide = pl.BlockSpec((d, fc), lambda i: (0, i))
    return pl.pallas_call(
        mlp_back_kernel,
        grid=(steps,),
        out_shape=(
            jax.ShapeDtypeStruct((n, d), F32),
            jax.ShapeDtypeStruct((n, d), BF),
            jax.ShapeDtypeStruct((d, ff), BF),
            jax.ShapeDtypeStruct((d, ff), BF),
            jax.ShapeDtypeStruct((1, d), F32),
        )
        + tuple(sums),
        in_specs=[
            full,
            full,
            full,
            pl.BlockSpec((n, fc), lambda i: (0, i)),
            wide,
            pl.BlockSpec((d, fc), lambda i: (0, i + steps)),
            row,
        ]
        + any_spec(len(extra)),
        out_specs=(full, full, wide, wide, row)
        + tuple(pl.BlockSpec(e.shape, lambda i: (0, 0)) for e in sums),
        scratch_shapes=[
            pltpu.VMEM((n, d), BF),
            pltpu.VMEM((d, n), BF),
            pltpu.VMEM((d, n), BF),
            pltpu.VMEM((n, d), F32),
        ]
        + (Reduce.scratch(extra[0].shape[0], [e.shape[1] for e in extra]) if extra else []),
        compiler_params=params(collective_id=4, has_side_effects=True) if extra else params(),
        cost_estimate=cost(8 * n * d * ff, 8 * d * ff + 2 * n * ff + 16 * n * d),
        name="mlp_back",
    )(g, xm, m, u, w, w, gain, *extra)


def attend_back_kernel(
    info, go_ref, o_ref, lse_ref, q_ref, kf_ref, vf_ref, ks_ref, vs_ref, ko_ref, vo_ref,
    w_ref, cosf_ref, sinf_ref, cos_ref, sin_ref, ga_ref, gb_ref,
    dq_ref, dkf_ref, dvf_ref, dks_ref, dvs_ref, dko_ref, dvo_ref, daf_ref, das_ref, dao_ref,
    sa_ref, sb_ref,
    do_s, bias, dqa, dka, dva, *rest,
):
    n, d = go_ref.shape
    pairs = d // 128
    greet()
    comms = [Reduce((ga_ref, gb_ref), (sa_ref, sb_ref), rest)]
    pump(comms, 0, 3)
    make_bias(info, bias)
    do_s[...] = mm(go_ref[...], w_ref[:, 3 * d : 4 * d]).astype(BF)
    lane_q = lax.broadcasted_iota(jnp.int32, (QB, 128), 1)

    def pair(g, carry):
        sl = pl.ds(pl.multiple_of(g * 128, 128), 128)
        dqa[...] = jnp.zeros_like(dqa)
        dka[...] = jnp.zeros_like(dka)
        dva[...] = jnp.zeros_like(dva)
        for b in range(n // QB):
            rs = slice(b * QB, b * QB + QB)
            q2 = q_ref[rs, sl] * SCALE
            do2 = do_s[rs, sl]
            prod = do2.astype(F32) * o_ref[rs, sl].astype(F32)
            lses = lse_ref[rs, :]
            for h in range(2):
                mine = (lane_q < HD) if h == 0 else (lane_q >= HD)
                qh = jnp.where(mine, q2, jnp.zeros_like(q2))
                doh = jnp.where(mine, do2, jnp.zeros_like(do2))
                dsum = jnp.sum(jnp.where(mine, prod, 0.0), axis=-1, keepdims=True)
                ls = jnp.sum(
                    jnp.where(lane_q == 2 * g + h, lses, 0.0), axis=-1, keepdims=True
                )
                for seg, (kr, vr) in enumerate(
                    ((kf_ref, vf_ref), (ks_ref, vs_ref), (ko_ref, vo_ref))
                ):
                    tiles = n // QB if seg == 0 else b + 1
                    for c in range(tiles):
                        cs = slice(c * QB, c * QB + QB)
                        col = seg * n + c * QB
                        k2 = kr[cs, sl]
                        v2 = vr[cs, sl]
                        s = mm(qh, k2, NT) + bias[rs, col : col + QB]
                        p = jnp.exp(s - ls)
                        dp = mm(doh, v2, NT)
                        ds = (p * (dp - dsum)).astype(BF)
                        pb = p.astype(BF)
                        acc = slice(seg * n + c * QB, seg * n + c * QB + QB)
                        dva[acc, :] += mm(pb, doh, TN)
                        dka[acc, :] += mm(ds, qh, TN)
                        kh = jnp.where(mine, k2, jnp.zeros_like(k2))
                        dqa[rs, :] += mm(ds, kh)
        dq_ref[:, sl] = turn(dqa[...] * SCALE, cos_ref[...], -sin_ref[...]).astype(BF)
        dkf_ref[:, sl] = turn(dka[0:n, :], cosf_ref[...], -sinf_ref[...]).astype(BF)
        dks_ref[:, sl] = turn(dka[n : 2 * n, :], cos_ref[...], -sin_ref[...]).astype(BF)
        dko_ref[:, sl] = turn(dka[2 * n : 3 * n, :], cos_ref[...], -sin_ref[...]).astype(BF)
        dvf_ref[:, sl] = dva[0:n, :].astype(BF)
        dvs_ref[:, sl] = dva[n : 2 * n, :].astype(BF)
        dvo_ref[:, sl] = dva[2 * n : 3 * n, :].astype(BF)
        return carry

    lax.fori_loop(0, pairs // 3, pair, 0)
    pump(comms, 1, 3)
    lax.fori_loop(pairs // 3, 2 * pairs // 3 + 1, pair, 0)
    pump(comms, 2, 3)
    lax.fori_loop(2 * pairs // 3 + 1, pairs, pair, 0)
    wk = w_ref[:, d : 2 * d]
    wv = w_ref[:, 2 * d : 3 * d]
    daf_ref[...] = (mm(dkf_ref[...], wk, NT) + mm(dvf_ref[...], wv, NT)).astype(BF)
    das_ref[...] = (mm(dks_ref[...], wk, NT) + mm(dvs_ref[...], wv, NT)).astype(BF)
    dao_ref[...] = (
        mm(dko_ref[...], wk, NT) + mm(dvo_ref[...], wv, NT) + mm(dq_ref[...], w_ref[:, 0:d], NT)
    )
    drain(comms)


def attend_back(info, go, o, lse, q, kf, vf, ks, vs, ko, vo, w, cosf, sinf, cos, sin, extra, cid):
    n, d = go.shape
    sums = [jax.ShapeDtypeStruct((e.shape[0] >> BITS, e.shape[1]), BF) for e in extra]
    sd = jax.ShapeDtypeStruct((n, d), BF)
    return pl.pallas_call(
        attend_back_kernel,
        out_shape=(sd,) * 9 + (jax.ShapeDtypeStruct((n, d), F32),) + tuple(sums),
        in_specs=[smem()] + vmem(15) + any_spec(2),
        out_specs=tuple(vmem(12)),
        scratch_shapes=[
            pltpu.VMEM((n, d), BF),
            pltpu.VMEM((n, 3 * n), F32),
            pltpu.VMEM((n, 128), F32),
            pltpu.VMEM((3 * n, 128), F32),
            pltpu.VMEM((3 * n, 128), F32),
        ]
        + Reduce.scratch(extra[0].shape[0], [e.shape[1] for e in extra]),
        compiler_params=params(collective_id=cid, has_side_effects=True),
        cost_estimate=cost(16 * n * d * d + 100 * QB * QB * d * 4, 2 * (4 * d * d + 24 * n * d)),
        name="attend_back",
    )(info, go, o, lse, q, kf, vf, ks, vs, ko, vo, w, cosf, sinf, cos, sin, *extra)


def weight_kernel(
    ao_ref, af_ref, as_ref, go_ref, o_ref, dq_ref, dkf_ref, dvf_ref, dks_ref, dvs_ref,
    dko_ref, dvo_ref, da_ref, db_ref,
):
    n, d = ao_ref.shape
    aot = ao_ref[...].T
    aft = af_ref[...].T
    ast = as_ref[...].T
    da_ref[:, 0:d] = mm(aot, dq_ref[...]).astype(BF)
    da_ref[:, d : 2 * d] = (
        mm(aot, dko_ref[...]) + mm(aft, dkf_ref[...]) + mm(ast, dks_ref[...])
    ).astype(BF)
    db_ref[:, 0:d] = (
        mm(aot, dvo_ref[...]) + mm(aft, dvf_ref[...]) + mm(ast, dvs_ref[...])
    ).astype(BF)
    db_ref[:, d : 2 * d] = mm(go_ref[...].T, o_ref[...]).astype(BF)


def weight_grads(ao, af, as_, go, o, dq, dkf, dvf, dks, dvs, dko, dvo):
    n, d = ao.shape
    sd = jax.ShapeDtypeStruct((d, 2 * d), BF)
    return pl.pallas_call(
        weight_kernel,
        out_shape=(sd, sd),
        in_specs=vmem(12),
        out_specs=tuple(vmem(2)),
        compiler_params=params(),
        cost_estimate=cost(16 * n * d * d, 2 * (4 * d * d + 12 * n * d)),
        name="weight_grads",
    )(ao, af, as_, go, o, dq, dkf, dvf, dks, dvs, dko, dvo)


def reduce_kernel(a_ref, b_ref, sa_ref, sb_ref, *rest):
    greet()
    comms = [Reduce((a_ref, b_ref), (sa_ref, sb_ref), rest)]
    for point in range(BITS):
        pump(comms, point, BITS)
    drain(comms)


def reduce_call(a, b):
    sums = tuple(jax.ShapeDtypeStruct((e.shape[0] >> BITS, e.shape[1]), BF) for e in (a, b))
    return pl.pallas_call(
        reduce_kernel,
        out_shape=sums,
        in_specs=any_spec(2),
        out_specs=tuple(vmem(2)),
        scratch_shapes=Reduce.scratch(a.shape[0], [a.shape[1], b.shape[1]]),
        compiler_params=params(collective_id=6, has_side_effects=True),
        cost_estimate=cost(1, 100 * a.size),
        name="reduce_grads",
    )(a, b)


def norm_back_kernel(gm_ref, x_ref, da_ref, r1_ref, r2_ref, gain_ref, g_ref, dgain_ref):
    da = da_ref[...] + r1_ref[...].astype(F32) + r2_ref[...].astype(F32)
    dz, dgain = norm_back(x_ref[...].astype(F32), gain_ref[...], da)
    g_ref[...] = gm_ref[...] + dz
    dgain_ref[...] = dgain


def norm_back_call(gm, x, da, r1, r2, gain):
    n, d = gm.shape
    return pl.pallas_call(
        norm_back_kernel,
        out_shape=(jax.ShapeDtypeStruct((n, d), F32), jax.ShapeDtypeStruct((1, d), F32)),
        in_specs=vmem(6),
        out_specs=tuple(vmem(2)),
        compiler_params=params(),
        cost_estimate=cost(20 * n * d, 20 * n * d),
        name="norm_back",
    )(gm, x, da, r1, r2, gain)


def first_norm_kernel(x_ref, gain_ref, a_ref):
    xh, _ = norm_stats(x_ref[...].astype(F32))
    a_ref[...] = (xh * gain_ref[...]).astype(BF)


def first_norm(x, gain):
    n, d = x.shape
    return pl.pallas_call(
        first_norm_kernel,
        out_shape=jax.ShapeDtypeStruct((n, d), BF),
        in_specs=vmem(2),
        out_specs=pl.BlockSpec(memory_space=pltpu.VMEM),
        compiler_params=params(),
        cost_estimate=cost(10 * n * d, 4 * n * d),
        name="first_norm",
    )(x, gain)


def send(x, pairs):
    return lax.ppermute(x, "tensor", pairs)


def spread_clean(a, t):
    p1 = send(a, [(2, 3), (3, 1)])
    p2 = send(a, [(2, 1)])
    p3 = send(p2, [(1, 0)])
    return jnp.where(t == 1, p2, p1), jnp.where(t == 1, p1, p3)


def return_clean(daf, das, t):
    q1 = send(das, [(0, 1)])
    q3 = send(jnp.where(t == 1, das, daf), [(1, 3), (3, 2)])
    q2 = send((daf.astype(F32) + q1.astype(F32)).astype(BF), [(1, 2)])
    return q2, q3


def turn_round(x, t):
    got = [x] + [send(x, [(i, (i + s) % 4) for i in range(4)]) for s in (1, 2, 3)]
    out = []
    for j in range(4):
        k = (t - j) % 4
        out.append(jnp.where(k < 2, jnp.where(k == 0, got[0], got[1]), jnp.where(k == 2, got[2], got[3])))
    return out


def piece_of(halves, dp, t):
    rows = halves[0][0].shape[0] >> BITS
    parts = []
    for i, ws in enumerate(halves):
        at = slot_of(dp, ORDERS[i]) * rows
        parts += [lax.dynamic_slice_in_dim(w, at, rows, 0) for w in ws]
    all_z = turn_round(jnp.concatenate(parts, axis=1), t)
    outs = []
    at = 0
    for p in parts:
        outs += [z[:, at : at + p.shape[1]] for z in all_z]
        at += p.shape[1]
    return jnp.concatenate(outs, axis=1)


def sum_over_z(halves, counts, t):
    n = lax.axis_size("dp")
    rows = halves[0].shape[0]
    cols = []
    for x, c in zip(halves, counts):
        for b in range(BITS, n.bit_length() - 1):
            x = x + lax.ppermute(x, "dp", [(i, i ^ (1 << b)) for i in range(n)])
        w = x.shape[1] // c
        cols += [x[:, j * w : (j + 1) * w].reshape(rows, 4, w // 4) for j in range(c)]
    every = jnp.concatenate(cols, axis=2).transpose(1, 0, 2)
    pick = lambda s: lax.dynamic_index_in_dim(every, (t + s) % 4, 0, keepdims=False)
    total = pick(0).astype(F32)
    for s in (1, 2, 3):
        total = total + send(pick(s), [(i, (i + s) % 4) for i in range(4)]).astype(F32)
    return total.astype(BF)


def sum_all(x):
    n = lax.axis_size("dp")
    step = 1
    while step < n:
        x = x + lax.ppermute(x, "dp", [(i, i ^ step) for i in range(n)])
        step *= 2
    for step in (1, 2):
        x = x + lax.ppermute(x, "tensor", [(i, i ^ step) for i in range(4)])
    return x


def on_device(
    tokens, lengths, noise_mask, cotangent, attn_gain, query_weight, key_weight, value_weight,
    out_weight, mlp_gain, up_weight, down_weight,
):
    n, d = tokens.shape
    dp = lax.axis_index("dp")
    t = lax.axis_index("tensor")
    info = jnp.stack([lengths[0], t]).astype(jnp.int32)
    base = (t % 2) * n

    position = jnp.arange(LMAX, dtype=jnp.int32).astype(F32)
    frequency = jnp.exp(
        -math.log(10000.0) * jnp.arange(HD // 2, dtype=jnp.int32).astype(F32) / (HD // 2)
    )
    angles = position[:, None] * frequency[None, :]
    cos1 = jnp.cos(angles)
    sin1 = jnp.sin(angles)
    cos_all = jnp.concatenate([cos1] * 4, axis=1)
    sin_all = jnp.concatenate([-sin1, sin1] * 2, axis=1)
    cosf, sinf = cos_all[:n], sin_all[:n]
    cos = lax.dynamic_slice_in_dim(cos_all, base, n, 0)
    sin = lax.dynamic_slice_in_dim(sin_all, base, n, 0)

    pos = base + jnp.arange(n, dtype=jnp.int32)
    masked = lax.dynamic_slice_in_dim(noise_mask[0], base, n, 0)
    weight = ((pos < lengths[0]) & ((t >= 2) | (masked == 1))).astype(F32)

    pa = []
    pm = []
    for layer in range(LAYERS):
        pa.append(
            piece_of(
                (
                    (query_weight[layer], key_weight[layer]),
                    (value_weight[layer], out_weight[layer].T),
                ),
                dp, t,
            )
        )
        pm.append(piece_of(((up_weight[layer],), (down_weight[layer].T,)), dp, t))
    wa = [gather_call(pa[0])] + [None] * (LAYERS - 1)
    wm = [None] * LAYERS

    saved = []
    x = tokens
    a = first_norm(tokens, attn_gain[0:1])
    for layer in range(LAYERS):
        af, as_ = spread_clean(a, t)
        q, ko, vo = project_own(a, wa[layer], cos, sin)
        o, lse, xm, m, kf, vf, ks, vs, wm[layer] = attend(
            info, x, af, as_, q, ko, vo, wa[layer], cosf, sinf, cos, sin,
            mlp_gain[layer : layer + 1], pm[layer], 10 + layer,
        )
        if layer + 1 < LAYERS:
            x_next, a_next, u, wa[layer + 1] = mlp(
                xm, m, wm[layer], attn_gain[layer + 1 : layer + 2], pa[layer + 1]
            )
        else:
            x_next, a_next, u = mlp(xm, m, wm[layer], attn_gain[layer : layer + 1])
        saved.append((x, a, af, as_, q, kf, vf, ks, vs, ko, vo, o, lse, xm, m, u))
        x, a = x_next, a_next
    block_out = x

    g = cotangent.astype(F32) * weight[:, None]
    gains = [None] * (2 * LAYERS)
    att = [None] * LAYERS
    mlps = [None] * LAYERS
    above = ()
    for layer in reversed(range(LAYERS)):
        x, a, af, as_, q, kf, vf, ks, vs, ko, vo, o, lse, xm, m, u = saved[layer]
        outs = mlp_back(g, xm, m, u, wm[layer], mlp_gain[layer : layer + 1], above)
        gm, go, dup, ddn, gains[LAYERS + layer] = outs[:5]
        if above:
            att[layer + 1] = sum_over_z(outs[5:], (2, 2), t)
        dq, dkf, dvf, dks, dvs, dko, dvo, daf, das, dao, su, sd = attend_back(
            info, go, o, lse, q, kf, vf, ks, vs, ko, vo, wa[layer], cosf, sinf, cos, sin, (dup, ddn),
            12 + layer,
        )
        mlps[layer] = sum_over_z((su, sd), (1, 1), t)
        r1, r2 = return_clean(daf, das, t)
        above = weight_grads(a, af, as_, go, o, dq, dkf, dvf, dks, dvs, dko, dvo)
        g, gains[layer] = norm_back_call(gm, x, dao, r1, r2, attn_gain[layer : layer + 1])
    att[0] = sum_over_z(reduce_call(*above), (2, 2), t)
    gain_sums = sum_all(jnp.concatenate(gains, axis=0))
    full = gather_many(att + mlps)
    w = d // 4
    f = up_weight.shape[2]

    def stack(parts):
        return jnp.stack(parts).astype(F32)

    layers = range(LAYERS)
    return (
        block_out,
        g,
        gain_sums[:LAYERS],
        stack([full[i][:, 0:w] for i in layers]),
        stack([full[i][:, w : 2 * w] for i in layers]),
        stack([full[i][:, 2 * w : 3 * w] for i in layers]),
        stack([full[i][:, 3 * w : 4 * w].T for i in layers]),
        gain_sums[LAYERS:],
        stack([full[LAYERS + i][:, 0:f] for i in layers]),
        stack([full[LAYERS + i][:, f : 2 * f].T for i in layers]),
    )


def solution(mesh):
    rows = P(("dp", "tensor"), None)
    cols = P(None, None, "tensor")
    mids = P(None, "tensor", None)
    return jax.shard_map(
        on_device,
        mesh=mesh,
        in_specs=(
            rows, P("dp"), P("dp", None), rows, P(), cols, cols, cols, mids, P(), cols, mids,
        ),
        out_specs=(rows, rows, P(), cols, cols, cols, mids, P(), cols, mids),
        check_vma=False,
    )
```

```python
import functools
import math

import jax
import jax.numpy as jnp
from jax import lax
from jax.experimental import pallas as pl
from jax.experimental.pallas import tpu as pltpu
from jax.sharding import PartitionSpec as P

HD = 64
BLK = 16
LMAX = 1024
LAYERS = 2
EPS = 1e-05
NEG = -1e30
SCALE = 1.0 / math.sqrt(HD)
GC = math.sqrt(2.0 / math.pi)
GA = 0.044715
F32 = jnp.float32
BF = jnp.bfloat16
QB = 256
VMEM_LIMIT = 56 << 20

NN = (((1,), (0,)), ((), ()))
NT = (((1,), (1,)), ((), ()))
TN = (((0,), (0,)), ((), ()))


def mm(a, b, dims=NN):
    return lax.dot_general(a, b, dims, preferred_element_type=F32)


def norm_stats(x):
    mean = jnp.mean(x, axis=-1, keepdims=True)
    c = x - mean
    var = jnp.mean(c * c, axis=-1, keepdims=True)
    r = lax.rsqrt(var + EPS)
    return c * r, r


def norm_back(x, gain, dy):
    xh, r = norm_stats(x)
    gy = dy * gain
    m1 = jnp.mean(gy, axis=-1, keepdims=True)
    m2 = jnp.mean(gy * xh, axis=-1, keepdims=True)
    dz = r * (gy - m1 - xh * m2)
    return dz, jnp.sum(dy * xh, axis=0, keepdims=True)


def turn(y, cos, sin):
    lane = lax.broadcasted_iota(jnp.int32, y.shape, 1) % HD
    other = jnp.where(
        lane < HD // 2, pltpu.roll(y, 128 - HD // 2, 1), pltpu.roll(y, HD // 2, 1)
    )
    return y * cos + other * sin


def vmem(n):
    return [pl.BlockSpec(memory_space=pltpu.VMEM)] * n


def smem():
    return pl.BlockSpec(memory_space=pltpu.SMEM)


def params(**kw):
    return pltpu.CompilerParams(vmem_limit_bytes=VMEM_LIMIT, **kw)


def cost(flops, nbytes, trans=0):
    return pl.CostEstimate(flops=int(flops), bytes_accessed=int(nbytes), transcendentals=int(trans))


MESH = pl.DeviceIdType.MESH
BITS = 3
ORDERS = ((0, 1, 2), (0, 2, 1))
NZ = 4


def bit_of(dp, b):
    return dp // (1 << b) % 2


def slot_of(dp, order):
    out = 0
    for b in order:
        out = out * 2 + bit_of(dp, b)
    return out


def partner(dp, b):
    return dp + (1 - 2 * bit_of(dp, b)) * (1 << b)


def greet(plane, line):
    dp = lax.axis_index("dp")
    t = lax.axis_index("tensor")
    barrier = pltpu.get_barrier_semaphore()
    if plane:
        for b in range(BITS):
            pl.semaphore_signal(barrier, inc=1, device_id=(partner(dp, b), t), device_id_type=MESH)
    if line:
        for s in range(1, NZ):
            pl.semaphore_signal(barrier, inc=1, device_id=(dp, (t + s) % NZ), device_id_type=MESH)
    pl.semaphore_wait(barrier, BITS * plane + (NZ - 1) * line)


def remote(src, dst, send, recv, dp, t):
    return pltpu.make_async_remote_copy(
        src_ref=src, dst_ref=dst, send_sem=send, recv_sem=recv, device_id=(dp, t), device_id_type=MESH
    )


def aligned(x, n=16):
    return pl.multiple_of(x, n)


def dma(n):
    return pltpu.SemaphoreType.DMA((n,))


def any_spec(n=1):
    return [pl.BlockSpec(memory_space=pl.ANY)] * n


class Job:
    plane = line = 0
    steps = BITS

    def bind(self, ins, outs, scr):
        self.at = 0
        self.i, self.o, self.s = ins, outs, scr
        self.dp = lax.axis_index("dp")
        self.t = lax.axis_index("tensor")

    def wait(self, s):
        pass

    def advance(self):
        if 0 < self.at <= self.steps:
            self.wait(self.at - 1)
        if self.at < self.steps:
            self.start(self.at)
        self.at += 1

    def complete(self):
        while self.at <= self.steps:
            self.advance()


class Gather(Job):
    plane = 1

    def __init__(self, piece):
        self.rows, n = piece.shape
        self.half = n // 2
        self.ins, self.in_specs = [piece], vmem(1)
        self.outs, self.out_specs = [jax.ShapeDtypeStruct((self.rows << BITS, n), BF)], any_spec()
        self.scratch = [dma(2 * BITS), dma(2 * BITS), dma(2)]

    def cols(self, i):
        return pl.ds(i * self.half, self.half)

    def own(self, i):
        at = slot_of(self.dp, ORDERS[i]) * self.rows
        return pltpu.make_async_copy(
            self.i[0].at[:, self.cols(i)],
            self.o[0].at[pl.ds(aligned(at), self.rows), self.cols(i)],
            self.s[2].at[i],
        )

    def copy(self, s, i):
        b = ORDERS[i][BITS - 1 - s]
        size = self.rows << s
        at = slot_of(self.dp, ORDERS[i]) // (1 << s) * size
        there = self.o[0].at[pl.ds(aligned(at), size), self.cols(i)]
        return remote(
            self.i[0].at[:, self.cols(i)] if s == 0 else there, there,
            self.s[0].at[2 * s + i], self.s[1].at[2 * s + i], partner(self.dp, b), self.t,
        )

    def start(self, s):
        for i in range(2):
            self.copy(s, i).start()
            if s == 0:
                self.own(i).start()

    def wait(self, s):
        for i in range(2):
            self.copy(s, i).wait()
            if s == 0:
                self.own(i).wait()


class Reduce(Job):
    plane = 1

    def __init__(self, a, b, part=0, parts=1):
        self.full = a.shape[0]
        widths = (a.shape[1] // parts, b.shape[1] // parts)
        self.cols = [pl.ds(part * w, w) for w in widths]
        self.ins, self.in_specs = [a, b], any_spec(2)
        self.outs = [jax.ShapeDtypeStruct((self.full >> BITS, w), BF) for w in widths]
        self.out_specs = vmem(2)
        self.scratch = [pltpu.VMEM((self.full // 2, w), BF) for w in widths]
        for w in widths:
            self.scratch += [pltpu.VMEM((self.full >> (s + 1), w), BF) for s in range(BITS)]
        self.scratch += [dma(2 * BITS), dma(2 * BITS), dma(2)]

    def got(self, s, i):
        return self.s[2 + i * BITS + s]

    def offset(self, s, i):
        at = 0
        for j in range(1, s):
            at = at + bit_of(self.dp, ORDERS[i][j]) * (self.full >> (j + 1))
        return at

    def copy(self, s, i):
        b = ORDERS[i][s]
        size = self.full >> (s + 1)
        at = (1 - bit_of(self.dp, b)) * size
        if s == 0:
            there = self.i[i].at[pl.ds(aligned(at), size), self.cols[i]]
        else:
            there = self.s[i].at[pl.ds(aligned(self.offset(s, i) + at), size), :]
        send, recv = self.s[2 + 2 * BITS], self.s[3 + 2 * BITS]
        return remote(
            there, self.got(s, i), send.at[2 * s + i], recv.at[2 * s + i], partner(self.dp, b), self.t
        )

    def own(self, i):
        size = self.full // 2
        at = bit_of(self.dp, ORDERS[i][0]) * size
        return pltpu.make_async_copy(
            self.i[i].at[pl.ds(aligned(at), size), self.cols[i]], self.s[i], self.s[4 + 2 * BITS].at[i]
        )

    def start(self, s):
        for i in range(2):
            self.copy(s, i).start()
            if s == 0:
                self.own(i).start()

    def wait(self, s):
        for i in range(2):
            self.copy(s, i).wait()
            if s == 0:
                self.own(i).wait()
            size = self.full >> (s + 1)
            base = self.offset(s + 1, i)
            keep, got, out = self.s[i], self.got(s, i), self.o[i]
            last = s == BITS - 1
            step = 48 if size % 48 == 0 else size

            def add(j, carry):
                rows = pl.ds(aligned(base + j * step), step)
                here = pl.ds(aligned(j * step), step)
                total = (keep[rows, :].astype(F32) + got[here, :].astype(F32)).astype(BF)
                if last:
                    out[here, :] = total
                else:
                    keep[rows, :] = total
                return carry

            lax.fori_loop(0, size // step, add, 0)


class Line(Job):
    line = 1
    steps = NZ - 1

    def __init__(self, parts, wide):
        self.count, self.rows, self.w = parts.shape
        self.wide = wide
        self.ins, self.in_specs = [parts], vmem(1)
        if wide:
            shape = (self.rows, self.count * NZ * self.w)
        else:
            shape = (NZ, self.count, self.rows, self.w)
        self.outs, self.out_specs = [jax.ShapeDtypeStruct(shape, BF)], any_spec()
        m = self.count * 2 * self.steps
        self.scratch = [dma(m), dma(m), dma(self.count)]

    def place(self, p, z):
        if self.wide:
            at = (p * NZ + z) * self.w
            return self.o[0].at[:, pl.ds(aligned(at, 128), self.w)]
        return self.o[0].at[z, p]

    def copy(self, s, p, way):
        z = (self.t - way * s) % NZ
        k = (s * 2 + (way > 0)) * self.count + p
        there = self.place(p, z)
        return remote(
            self.i[0].at[p] if s == 0 else there, there, self.s[0].at[k], self.s[1].at[k],
            self.dp, (self.t + way) % NZ,
        )

    def inside(self, s, way, receiver):
        t = self.t
        if receiver:
            return (t - way * (s + 1) >= 0) & (t - way * (s + 1) < NZ)
        return (t - way * s >= 0) & (t - way * s < NZ) & (t + way >= 0) & (t + way < NZ)

    def own(self, p):
        return pltpu.make_async_copy(self.i[0].at[p], self.place(p, self.t), self.s[2].at[p])

    def start(self, s):
        for way in (1, -1):

            @pl.when(self.inside(s, way, False))
            def _(way=way):
                for p in range(self.count):
                    self.copy(s, p, way).start()

        if s == 0:
            for p in range(self.count):
                self.own(p).start()

    def wait(self, s):
        for way in (1, -1):

            @pl.when(self.inside(s, way, True))
            def _(way=way):
                for p in range(self.count):
                    self.copy(s, p, way).wait_recv()

            @pl.when(self.inside(s, way, False))
            def _(way=way):
                for p in range(self.count):
                    self.copy(s, p, way).wait_send()

        if s == 0:
            for p in range(self.count):
                self.own(p).wait()


class LineSum(Job):
    line = 1
    steps = 1

    def __init__(self, parts):
        shape = parts.shape[1:]
        self.ins, self.in_specs = [parts], vmem(1)
        self.outs, self.out_specs = [jax.ShapeDtypeStruct(shape, parts.dtype)], vmem(1)
        self.scratch = [pltpu.VMEM((NZ - 1,) + shape, parts.dtype), dma(3), dma(3)]

    def copies(self):
        for s in (1, 2, 3):
            z = (self.t + s) % NZ
            yield remote(
                self.i[0].at[z], self.s[0].at[s - 1], self.s[1].at[s - 1], self.s[2].at[s - 1], self.dp, z
            )

    def start(self, s):
        for c in self.copies():
            c.start()

    def wait(self, s):
        for c in self.copies():
            c.wait()
        got = self.s[0]
        total = self.i[0][self.t].astype(F32)
        for k in range(NZ - 1):
            total = total + got[k].astype(F32)
        self.o[0][...] = total.astype(self.o[0].dtype)


class PlaneSum(Job):
    plane = 1

    def __init__(self, x):
        self.ins, self.in_specs = [x], vmem(1)
        self.outs, self.out_specs = [jax.ShapeDtypeStruct(x.shape, F32)], vmem(1)
        self.scratch = [pltpu.VMEM((BITS,) + x.shape, F32), dma(BITS), dma(BITS)]

    def copy(self, s):
        return remote(
            self.i[0] if s == 0 else self.o[0], self.s[0].at[s], self.s[1].at[s], self.s[2].at[s],
            partner(self.dp, s), self.t,
        )

    def start(self, s):
        self.copy(s).start()

    def wait(self, s):
        self.copy(s).wait()
        self.o[0][...] = (self.i[0] if s == 0 else self.o[0])[...] + self.s[0][s]


class Spread(Job):
    line = 1
    steps = 0

    def __init__(self, a):
        self.ins, self.in_specs = [a], any_spec()
        self.outs, self.out_specs = [jax.ShapeDtypeStruct(a.shape, BF)] * 2, any_spec(2)
        self.scratch = [pltpu.VMEM(a.shape, BF), pltpu.VMEM(a.shape, BF), dma(2), dma(2), dma(2)]

    def put(self, src, which, to, k):
        return remote(src, self.s[which], self.s[2].at[k], self.s[3].at[which], self.dp, to)

    def save(self, which):
        return pltpu.make_async_copy(self.s[which], self.o[which], self.s[4].at[which])

    def begin(self):
        a, t = self.i[0], self.t

        @pl.when(t == 2)
        def _():
            self.put(a, 0, 1, 0).start()
            self.put(a, 0, 3, 1).start()

        @pl.when(t % 2 == 0)
        def _():
            self.s[0][...] = jnp.zeros_like(self.s[0])

        @pl.when(t >= 2)
        def _():
            self.s[1][...] = jnp.zeros_like(self.s[1])

    def first(self):
        a, t = self.i[0], self.t

        @pl.when(t % 2 == 1)
        def _():
            self.put(a, 0, 1, 0).wait_recv()

        @pl.when(t == 1)
        def _():
            self.put(self.s[0], 1, 0, 0).start()

        @pl.when(t == 3)
        def _():
            self.put(a, 1, 1, 0).start()

        self.save(0).start()

    def second(self):
        @pl.when(self.t < 2)
        def _():
            self.put(self.i[0], 1, 1, 0).wait_recv()

        self.save(1).start()

    def end(self):
        a, t = self.i[0], self.t

        @pl.when(t >= 1)
        def _():
            self.put(a, 0, 1, 0).wait_send()

        @pl.when(t == 2)
        def _():
            self.put(a, 0, 3, 1).wait_send()

        self.save(0).wait()
        self.save(1).wait()


class Early(Job):
    line = 1
    steps = 0

    def __init__(self, shape):
        self.ins, self.in_specs = [], []
        self.outs, self.out_specs = [jax.ShapeDtypeStruct(shape, BF)], any_spec()
        self.scratch = [dma(1), dma(1)]

    def put(self, src, to):
        return remote(src, self.o[0], self.s[0].at[0], self.s[1].at[0], self.dp, to)

    def go(self, das):
        @pl.when(self.t < 2)
        def _():
            self.put(das, 2 * self.t + 1).start()

    def end(self, das):
        @pl.when(self.t < 2)
        def _():
            self.put(das, 1).wait_send()

        @pl.when(self.t % 2 == 1)
        def _():
            self.put(das, 1).wait_recv()


class Return(Job):
    line = 1
    steps = 0

    def __init__(self, daf, got):
        self.ins, self.in_specs = [daf, got], vmem(2)
        self.outs, self.out_specs = [], []
        sd = pltpu.VMEM(daf.shape, BF)
        self.scratch = [sd, sd, sd, dma(1), dma(2)]

    def put(self, src, which):
        return remote(src, self.s[which], self.s[3].at[0], self.s[4].at[which], self.dp, 2)

    def begin(self):
        daf, got = self.i

        @pl.when(self.t == 1)
        def _():
            self.s[2][...] = (daf[...].astype(F32) + got[...].astype(F32)).astype(BF)
            self.put(self.s[2], 0).start()

        @pl.when(self.t == 3)
        def _():
            self.put(daf, 1).start()

    def end(self, acc):
        daf, got = self.i

        @pl.when(self.t == 2)
        def _():
            self.put(daf, 0).wait_recv()
            self.put(daf, 1).wait_recv()
            acc[...] += self.s[0][...].astype(F32) + self.s[1][...].astype(F32)

        @pl.when(self.t == 3)
        def _():
            acc[...] += got[...].astype(F32)

        @pl.when(self.t % 2 == 1)
        def _():
            self.put(daf, 0).wait_send()


def steps_at(jobs, point, points):
    for s in range(max([j.steps for j in jobs], default=0)):
        now = [j for j in jobs if s < j.steps and s * points // j.steps == point]
        for j in now:
            if s > 0:
                j.wait(s - 1)
        for j in now:
            j.start(s)


def finish(jobs):
    for j in jobs:
        if j.steps:
            j.wait(j.steps - 1)


class In:
    def __init__(self, hbm, ref, sem):
        self.ref = ref
        self.copy = pltpu.make_async_copy(hbm, ref, sem)
        self.copy.start()

    def __call__(self):
        if self.copy is not None:
            self.copy.wait()
            self.copy = None
        return self.ref


class Out:
    def __init__(self, hbm, ref, sem):
        self.ref = ref
        self.copy = pltpu.make_async_copy(ref, hbm, sem)
        self.sent = False

    def flush(self):
        if not self.sent:
            self.copy.start()
            self.sent = True


def meet(jobs):
    greet(max(j.plane for j in jobs), max(j.line for j in jobs))


def lazily(body, ins, in_specs, outs, out_specs, scratch):
    lazy = [sp.memory_space != pltpu.SMEM for sp in in_specs]
    bufs = [pltpu.VMEM(x.shape, x.dtype) for x, z in zip(ins, lazy) if z]
    bufs += [pltpu.VMEM(x.shape, x.dtype) for x in outs]
    own = len(scratch)
    count = sum(lazy)

    def wrapped(i, o, s, jobs):
        mine, rest = s[:own], s[own:]
        vm, sin, sout = rest[:-2], rest[-2], rest[-1]
        given = []
        k = 0
        for ref, z in zip(i, lazy):
            if z:
                given.append(In(ref, vm[k], sin.at[k]))
                k += 1
            else:
                given.append(ref)
        results = [Out(ref, vm[count + k], sout.at[k]) for k, ref in enumerate(o)]
        if jobs:
            meet(jobs)
        body(given, results, mine, jobs)
        for x, z in zip(given, lazy):
            if z:
                x()
        for x in results:
            x.flush()
        for x in results:
            x.copy.wait()

    specs = [any_spec()[0] if z else sp for sp, z in zip(in_specs, lazy)]
    return wrapped, specs, any_spec(len(outs)), list(scratch) + bufs + [dma(count), dma(len(outs))]


def run(body, name, ins, in_specs, outs, out_specs, scratch, jobs, cid, flops, nbytes, grid=None):
    late = grid is None and len(ins) > 0
    if late:
        body, in_specs, out_specs, scratch = lazily(body, ins, in_specs, outs, out_specs, scratch)
    cuts = []
    for what in ("ins", "outs", "scratch"):
        own = {"ins": ins, "outs": outs, "scratch": scratch}[what]
        cuts.append([len(own)] + [len(getattr(j, what)) for j in jobs])

    def kernel(*refs):
        at = 0
        groups = []
        for cut in cuts:
            g = []
            for c in cut:
                g.append(refs[at : at + c])
                at += c
            groups.append(g)
        for k, j in enumerate(jobs):
            j.bind(groups[0][k + 1], groups[1][k + 1], groups[2][k + 1])
        if jobs and not late:
            if grid is None:
                meet(jobs)
            else:
                pl.when(pl.program_id(0) == 0)(functools.partial(meet, jobs))
        body(groups[0][0], groups[1][0], groups[2][0], jobs)

    for j in jobs:
        ins, in_specs = list(ins) + j.ins, list(in_specs) + j.in_specs
        outs, out_specs = list(outs) + j.outs, list(out_specs) + j.out_specs
        scratch = list(scratch) + j.scratch
    res = pl.pallas_call(
        kernel,
        out_shape=tuple(outs),
        in_specs=list(in_specs),
        out_specs=tuple(out_specs),
        scratch_shapes=list(scratch),
        compiler_params=params(collective_id=cid, has_side_effects=True) if jobs else params(),
        cost_estimate=cost(flops, nbytes),
        name=name,
        **({} if grid is None else {"grid": grid}),
    )(*ins)
    at = cuts[1][0]
    extra = []
    for c in cuts[1][1:]:
        extra.append(res[at : at + c])
        at += c
    return res[: cuts[1][0]], extra


def only_jobs(ins, outs, scr, jobs):
    for s in range(max(j.steps for j in jobs) + 1):
        for j in jobs:
            if s <= j.steps:
                j.advance()


def transfer(name, jobs, cid):
    return run(only_jobs, name, [], [], [], [], [], jobs, cid, 1, 1 << 24)[1]


def turned(out, tmp, cos, sin):
    for g in range(out.shape[1] // 128):
        sl = slice(g * 128, g * 128 + 128)
        out[:, sl] = turn(tmp[:, sl], cos[...], sin[...]).astype(BF)


def near_bias(info, bias):
    n = bias.shape[0]
    length = info[0]
    noisy = info[1] < 2
    base = info[1] % 2 * n
    j = lax.broadcasted_iota(jnp.int32, (n, n), 0)
    i = lax.broadcasted_iota(jnp.int32, (n, n), 1)
    bi = i // BLK
    bj = j // BLK
    low = jnp.where(noisy, bi, 0)
    seen = (bj <= bi) & (bj >= low) & (j + base < length)
    bias[...] = jnp.where(seen | (i == j), 0.0, NEG)


def far_masks(info, first, second, hot):
    n = hot.shape[1]
    length = info[0]
    noisy = info[1] < 2
    odd = info[1] % 2
    key = lax.broadcasted_iota(jnp.int32, (n, 128), 0)
    block = lax.broadcasted_iota(jnp.int32, (n, 128), 1) % HD
    real = block < n // BLK
    odd_lim = jnp.where(odd == 1, length, 0)
    lim = jnp.where(noisy, length - odd * n, 0)
    first[...] = jnp.where(real & (key >= odd_lim), NEG, 0.0).astype(BF)
    hidden = (key // BLK >= block) | (key >= lim)
    second[...] = jnp.where(real & hidden, NEG, 0.0).astype(BF)
    row = lax.broadcasted_iota(jnp.int32, (128, n), 0) % HD
    query = lax.broadcasted_iota(jnp.int32, (128, n), 1)
    hot[...] = jnp.where(query // BLK == row, 1.0, 0.0).astype(BF)


def half_of(h, shape, axis):
    at = lax.broadcasted_iota(jnp.int32, shape, axis)
    return (at < HD) if h == 0 else (at >= HD)


def attend_body(ins, outs, scr, jobs):
    info, a_in, w_in, cos_in, sin_in, cosf_in, sinf_in, x_in, gain_in = ins
    q_ref, ko_ref, vo_ref, kf_ref, vf_ref, ks_ref, vs_ref, o_ref, lse_ref, xm_ref, m_ref = [
        x.ref for x in outs
    ]
    tmp, bias, mask1, mask2, hot, acc, top, tot = scr
    spread = jobs[0]
    rest = jobs[1:]
    af_ref, as_ref = spread.s[0:2]
    n, d = x_in.ref.shape
    pairs = d // 128
    gather = rest[0]
    line = rest[1:]
    spread.begin()
    gather.advance()
    near_bias(info, bias)
    far_masks(info, mask1, mask2, hot)
    a_ref = a_in()
    w_ref = w_in()
    cos = cos_in()
    sin = sin_in()

    tmp[...] = mm(a_ref[...], w_ref[:, 0:d]) * SCALE
    turned(q_ref, tmp, cos, sin)

    def keys_of(src, kk, vv, c, s):
        av = src[...]
        tmp[...] = mm(av, w_ref[:, d : 2 * d])
        turned(kk, tmp, c, s)
        vv[...] = mm(av, w_ref[:, 2 * d : 3 * d]).astype(BF)

    keys_of(a_ref, ko_ref, vo_ref, cos, sin)
    for k in range(3):
        outs[k].flush()

    def segment(kk, vv, mask, full, first, last):
        def pair(g, carry):
            sl = pl.ds(aligned(g * 128, 128), 128)
            qt = q_ref[:, sl].T
            k2 = kk[:, sl]
            vt = vv[:, sl].T
            other_q = jnp.zeros_like(qt) if mask is None else hot[...]
            other_k = k2 if mask is None else mask[...]
            rows = pl.ds(aligned(g * 128, 128), 128)
            if not first:
                olds = top[g]
                tots = tot[g]
                before = acc[rows, :]
            tops, sums, outs = [], [], []
            chains = [(h, b) for h in range(2) for b in range(n // QB)]
            scores = []
            for h, b in chains:
                qh = jnp.where(half_of(h, qt.shape, 0), qt, other_q)
                kh = jnp.where(half_of(h, k2.shape, 1), k2, other_k)
                width = n if full else (b + 1) * QB
                scores.append(mm(kh[0:width], qh[:, b * QB : b * QB + QB]))
            for (h, b), s in zip(chains, scores):
                cs = slice(b * QB, b * QB + QB)
                width = s.shape[0]
                if mask is None:
                    s = s + bias[0:width, cs]
                mx = jnp.max(s, axis=0, keepdims=True)
                if not first:
                    old = olds[h : h + 1, cs]
                    mx = jnp.maximum(mx, old)
                    scale = jnp.exp(old - mx)
                e = jnp.exp(s - mx)
                total = jnp.sum(e, axis=0, keepdims=True)
                out = mm(vt[h * HD : h * HD + HD, 0:width], e.astype(BF))
                if not first:
                    total = total + tots[h : h + 1, cs] * scale
                    out = out + before[h * HD : h * HD + HD, cs] * scale
                if last:
                    mx = mx + jnp.log(total)
                    out = out / total
                tops.append(mx)
                sums.append(total)
                outs.append(out)
            for (h, b), mx, total, out in zip(chains, tops, sums, outs):
                cs = slice(b * QB, b * QB + QB)
                if last:
                    lse_ref[g, h : h + 1, cs] = mx
                else:
                    top[g, h : h + 1, cs] = mx
                    tot[g, h : h + 1, cs] = total
                    acc[pl.ds(aligned(g * 128 + h * HD, HD), HD), cs] = out
            if last:
                ot = jnp.concatenate(
                    [jnp.concatenate(outs[i : i + n // QB], axis=1) for i in (0, n // QB)], axis=0
                )
                o_ref[:, sl] = ot.T.astype(BF)
            return carry

        return pair

    lax.fori_loop(0, pairs, segment(ko_ref, vo_ref, None, False, True, False), 0)
    gather.advance()
    spread.first()
    keys_of(af_ref, kf_ref, vf_ref, cosf_in(), sinf_in())
    outs[3].flush()
    outs[4].flush()
    lax.fori_loop(0, pairs, segment(kf_ref, vf_ref, mask1, True, False, False), 0)
    spread.second()
    for j in line:
        j.advance()
    keys_of(as_ref, ks_ref, vs_ref, cos, sin)
    outs[5].flush()
    outs[6].flush()
    last = segment(ks_ref, vs_ref, mask2, False, False, True)
    lax.fori_loop(0, pairs // 2, last, 0)
    gather.advance()
    for j in line:
        j.advance()
    lax.fori_loop(pairs // 2, pairs, last, 0)
    for j in line:
        j.advance()
    outs[7].flush()
    outs[8].flush()
    xm = x_in()[...].astype(F32) + mm(o_ref[...], w_ref[:, 3 * d : 4 * d], NT)
    xm_ref[...] = xm
    outs[9].flush()
    xh, _ = norm_stats(xm)
    m_ref[...] = (xh * gain_in()[...]).astype(BF)
    outs[10].flush()
    spread.end()
    gather.complete()
    for j in line:
        j.complete()


def attend(info, x, a, w, cosf, sinf, cos, sin, gain, jobs, cid):
    n, d = x.shape
    sd = jax.ShapeDtypeStruct((n, d), BF)
    heads = (d // 128, 8, n)
    return run(
        attend_body, "attend",
        [info, a, w, cos, sin, cosf, sinf, x, gain], [smem()] + vmem(8),
        [sd] * 8 + [jax.ShapeDtypeStruct(heads, F32), jax.ShapeDtypeStruct((n, d), F32), sd],
        vmem(11),
        [
            pltpu.VMEM((n, d), F32),
            pltpu.VMEM((n, n), F32),
            pltpu.VMEM((n, 128), BF),
            pltpu.VMEM((n, 128), BF),
            pltpu.VMEM((128, n), BF),
            pltpu.VMEM((d, n), F32),
            pltpu.VMEM(heads, F32),
            pltpu.VMEM(heads, F32),
        ],
        [Spread(a)] + jobs, cid,
        16 * n * d * d + 40 * QB * QB * d * 4, 2 * (4 * d * d + 16 * n * d),
    )


MLP_STEPS = 6


def gelu(u):
    return 0.5 * u * (1.0 + jnp.tanh(GC * (u + GA * (u * u * u))))


def grid_steps(jobs):
    step = pl.program_id(0)
    for point in range(MLP_STEPS):
        if any(s * MLP_STEPS // j.steps == point for j in jobs for s in range(j.steps)):
            pl.when(step == point)(functools.partial(steps_at, jobs, point, MLP_STEPS))


def mlp_body(ins, outs, scr, jobs):
    xm_ref, m_ref, up_ref, dn_ref, gain = ins
    x_ref, a_ref, u_ref = outs
    (acc,) = scr
    step = pl.program_id(0)
    grid_steps(jobs)

    @pl.when(step == 0)
    def _():
        acc[...] = xm_ref[...]

    u = mm(m_ref[...], up_ref[...])
    u_ref[...] = u.astype(BF)
    acc[...] += mm(gelu(u).astype(BF), dn_ref[...], NT)

    @pl.when(step == MLP_STEPS - 1)
    def _():
        x = acc[...]
        x_ref[...] = x
        xh, _ = norm_stats(x)
        a_ref[...] = (xh * gain[...]).astype(BF)
        finish(jobs)


def mlp(xm, m, w, gain, jobs, cid):
    n, d = xm.shape
    ff = w.shape[1] // 2
    steps = MLP_STEPS
    fc = ff // steps
    full = pl.BlockSpec((n, d), lambda i: (0, 0))
    return run(
        mlp_body, "mlp",
        [xm, m, w, w, gain],
        [
            full,
            full,
            pl.BlockSpec((d, fc), lambda i: (0, i)),
            pl.BlockSpec((d, fc), lambda i: (0, i + steps)),
            pl.BlockSpec((1, d), lambda i: (0, 0)),
        ],
        [
            jax.ShapeDtypeStruct((n, d), F32),
            jax.ShapeDtypeStruct((n, d), BF),
            jax.ShapeDtypeStruct((n, ff), BF),
        ],
        [full, full, pl.BlockSpec((n, fc), lambda i: (0, i))],
        [pltpu.VMEM((n, d), F32)],
        jobs, cid,
        4 * n * d * ff, 4 * d * ff + 2 * n * ff + 10 * n * d, grid=(steps,),
    )


def mlp_back_body(ins, outs, scr, jobs):
    g_ref, xm_ref, m_ref, u_ref, up_ref, dn_ref, gain = ins
    gm_ref, go_ref, dup_ref, ddn_ref, dgain_ref = outs
    gy, gyt, mt, dm = scr
    step = pl.program_id(0)
    grid_steps(jobs)

    @pl.when(step == 0)
    def _():
        gb = g_ref[...].astype(BF)
        gy[...] = gb
        gyt[...] = gb.T
        mt[...] = m_ref[...].T
        dm[...] = jnp.zeros_like(dm)

    u = u_ref[...].astype(F32)
    dh = mm(gy[...], dn_ref[...])
    u2 = u * u
    th = jnp.tanh(GC * (u + GA * (u2 * u)))
    half = 0.5 * (1.0 + th)
    h = (u * half).astype(BF)
    slope = half + 0.5 * u * (1.0 - th * th) * (GC * (1.0 + 3.0 * GA * u2))
    du = (dh * slope).astype(BF)
    dm[...] += mm(du, up_ref[...], NT)
    dup_ref[...] = mm(mt[...], du).astype(BF)
    ddn_ref[...] = mm(gyt[...], h).astype(BF)

    @pl.when(step == MLP_STEPS - 1)
    def _():
        dz, dgain = norm_back(xm_ref[...], gain[...], dm[...])
        gm = g_ref[...] + dz
        gm_ref[...] = gm
        go_ref[...] = gm.astype(BF)
        dgain_ref[...] = dgain
        finish(jobs)


def mlp_back(g, xm, m, u, w, gain, jobs, cid):
    n, d = xm.shape
    ff = w.shape[1] // 2
    steps = MLP_STEPS
    fc = ff // steps
    full = pl.BlockSpec((n, d), lambda i: (0, 0))
    row = pl.BlockSpec((1, d), lambda i: (0, 0))
    wide = pl.BlockSpec((d, fc), lambda i: (0, i))
    return run(
        mlp_back_body, "mlp_back",
        [g, xm, m, u, w, w, gain],
        [
            full, full, full,
            pl.BlockSpec((n, fc), lambda i: (0, i)),
            wide,
            pl.BlockSpec((d, fc), lambda i: (0, i + steps)),
            row,
        ],
        [
            jax.ShapeDtypeStruct((n, d), F32),
            jax.ShapeDtypeStruct((n, d), BF),
            jax.ShapeDtypeStruct((d, ff), BF),
            jax.ShapeDtypeStruct((d, ff), BF),
            jax.ShapeDtypeStruct((1, d), F32),
        ],
        [full, full, wide, wide, row],
        [
            pltpu.VMEM((n, d), BF),
            pltpu.VMEM((d, n), BF),
            pltpu.VMEM((d, n), BF),
            pltpu.VMEM((n, d), F32),
        ],
        jobs, cid,
        8 * n * d * ff, 8 * d * ff + 2 * n * ff + 16 * n * d, grid=(steps,),
    )


def back_pair(g, segs, q_ref, do_ref, o_ref, lse_ref, hot, dqt, dka, dva):
    n = q_ref.shape[0]
    sl = pl.ds(aligned(g * 128, 128), 128)
    q2 = q_ref[:, sl]
    do2 = do_ref[:, sl]
    qt = q2.T
    dot = do2.T
    prod = dot.astype(F32) * o_ref[:, sl].T.astype(F32)
    for h in range(2):
        hs = slice(h * HD, h * HD + HD)
        low = half_of(h, qt.shape, 0)
        side = half_of(h, q2.shape, 1)
        none = jnp.zeros_like(q2)
        qth = jnp.where(low, qt, jnp.zeros_like(qt) if hot is None else hot[...])
        doth = jnp.where(low, dot, jnp.zeros_like(dot))
        qh = jnp.where(side, q2, none)
        doh = jnp.where(side, do2, none)
        dsum = jnp.sum(prod[hs], axis=0, keepdims=True)
        ls = lse_ref[g, h : h + 1, :]
        for at, (kr, vr, mask, bias, whole, base) in enumerate(segs):
            k2 = kr[:, sl]
            v2 = vr[:, sl]
            kt = k2.T
            kh = jnp.where(side, k2, none if mask is None else mask[...])
            for b in range(n // QB):
                cs = slice(b * QB, b * QB + QB)
                width = n if whole else (b + 1) * QB
                s = mm(kh[0:width], qth[:, cs])
                if bias is not None:
                    s = s + bias[0:width, cs]
                p = jnp.exp(s - ls[:, cs])
                dp = mm(v2[0:width], doth[:, cs])
                ds = (p * (dp - dsum[:, cs])).astype(BF)
                dv = mm(p.astype(BF), doh[cs])
                dk = mm(ds, qh[cs])
                dq = mm(kt[hs, 0:width], ds)
                if h == 0 and b == 0:
                    dva[base : base + width, :] = dv
                    dka[base : base + width, :] = dk
                elif h == 0 and not whole:
                    dva[base : base + width - QB, :] += dv[: width - QB]
                    dka[base : base + width - QB, :] += dk[: width - QB]
                    dva[base + width - QB : base + width, :] = dv[width - QB :]
                    dka[base + width - QB : base + width, :] = dk[width - QB :]
                else:
                    dva[base : base + width, :] += dv
                    dka[base : base + width, :] += dk
                if at == 0:
                    dqt[hs, cs] = dq
                else:
                    dqt[hs, cs] += dq
    return sl


def back_far_body(ins, outs, scr, jobs):
    (
        info, go_in, w_in, q_in, o_in, lse_in, ks_in, vs_in, cos_in, sin_in, kf_in, vf_in, cosf_in, sinf_in,
    ) = ins
    do_ref, dqp_ref, dkf_ref, dvf_ref, dks_ref, dvs_ref, daf_ref = [x.ref for x in outs]
    mask1, mask2, hot, dqt, dka, dva, das = scr
    early = jobs[0]
    rest = jobs[1:]
    n, d = go_in.ref.shape
    pairs = d // 128
    for j in rest:
        j.advance()
    far_masks(info, mask1, mask2, hot)
    go_ref = go_in()
    w_ref = w_in()
    do_ref[...] = mm(go_ref[...], w_ref[:, 3 * d : 4 * d]).astype(BF)
    outs[0].flush()
    wk = w_ref[:, d : 2 * d]
    wv = w_ref[:, 2 * d : 3 * d]

    def part(k_in, v_in, mask, whole, c_in, s_in, dk_ref, dv_ref, begin):
        q_ref, o_ref, lse_ref = q_in(), o_in(), lse_in()
        k_ref, v_ref = k_in(), v_in()
        cos, sin = c_in(), s_in()

        def pair(g, carry):
            segs = ((k_ref, v_ref, mask, None, whole, 0),)
            sl = back_pair(g, segs, q_ref, do_ref, o_ref, lse_ref, hot, dqt, dka, dva)
            if begin:
                dqp_ref[sl, :] = dqt[...]
            else:
                dqp_ref[sl, :] += dqt[...]
            dk_ref[:, sl] = turn(dka[...], cos[...], -sin[...]).astype(BF)
            dv_ref[:, sl] = dva[...].astype(BF)
            return carry

        return pair

    pair = part(ks_in, vs_in, mask2, False, cos_in, sin_in, dks_ref, dvs_ref, True)
    lax.fori_loop(0, pairs, pair, 0)
    for j in rest:
        j.advance()
    das[...] = (mm(dks_ref[...], wk, NT) + mm(dvs_ref[...], wv, NT)).astype(BF)
    early.go(das)
    outs[4].flush()
    outs[5].flush()
    pair = part(kf_in, vf_in, mask1, True, cosf_in, sinf_in, dkf_ref, dvf_ref, False)
    lax.fori_loop(0, pairs, pair, 0)
    outs[1].flush()
    outs[2].flush()
    outs[3].flush()
    daf_ref[...] = (mm(dkf_ref[...], wk, NT) + mm(dvf_ref[...], wv, NT)).astype(BF)
    outs[6].flush()
    for j in rest:
        j.advance()
    early.end(das)
    for j in rest:
        j.complete()


def back_far(info, go, o, lse, q, kf, vf, ks, vs, w, cosf, sinf, cos, sin, jobs, cid):
    n, d = go.shape
    sd = jax.ShapeDtypeStruct((n, d), BF)
    return run(
        back_far_body, "back_far",
        [info, go, w, q, o, lse, ks, vs, cos, sin, kf, vf, cosf, sinf], [smem()] + vmem(13),
        [sd, jax.ShapeDtypeStruct((d, n), F32)] + [sd] * 5, vmem(7),
        [
            pltpu.VMEM((n, 128), BF),
            pltpu.VMEM((n, 128), BF),
            pltpu.VMEM((128, n), BF),
            pltpu.VMEM((128, n), F32),
            pltpu.VMEM((n, 128), F32),
            pltpu.VMEM((n, 128), F32),
            pltpu.VMEM((n, d), BF),
        ],
        [Early((n, d))] + jobs, cid,
        10 * n * d * d + 70 * QB * QB * d * 4, 2 * (4 * d * d + 18 * n * d),
    )


def back_near_body(ins, outs, scr, jobs):
    (
        info, q_in, do_in, o_in, lse_in, ko_in, vo_in, dqp_in, cos_in, sin_in, go_in, af_in, dkf_in, dvf_in,
        as_in, dks_in, dvs_in, ao_in, w_in, x_in, gm_in, gain_in,
    ) = ins
    da_ref, db_ref, g_ref, dgain_ref = [x.ref for x in outs]
    bias, dqt, dka, dva, dq_s, dko_s, dvo_s, dao = scr
    back = jobs[0]
    rest = jobs[1:]
    n, d = do_in.ref.shape
    pairs = d // 128
    back.begin()
    for j in rest:
        j.advance()
    near_bias(info, bias)
    q_ref, do_ref, o_ref, lse_ref = q_in(), do_in(), o_in(), lse_in()
    ko_ref, vo_ref, dqp_ref, cos, sin = ko_in(), vo_in(), dqp_in(), cos_in(), sin_in()

    def pair(g, carry):
        segs = ((ko_ref, vo_ref, None, bias, False, 0),)
        sl = back_pair(g, segs, q_ref, do_ref, o_ref, lse_ref, None, dqt, dka, dva)
        dq = (dqt[...] + dqp_ref[sl, :]).T
        dq_s[:, sl] = turn(dq * SCALE, cos[...], -sin[...]).astype(BF)
        dko_s[:, sl] = turn(dka[...], cos[...], -sin[...]).astype(BF)
        dvo_s[:, sl] = dva[...].astype(BF)
        return carry

    lax.fori_loop(0, pairs, pair, 0)
    for j in rest:
        j.advance()
    db_ref[:, d : 2 * d] = mm(go_in()[...].T, o_ref[...]).astype(BF)
    aot = ao_in()[...].T
    aft = af_in()[...].T
    ast = as_in()[...].T
    db_ref[:, 0:d] = (
        mm(aot, dvo_s[...]) + mm(aft, dvf_in()[...]) + mm(ast, dvs_in()[...])
    ).astype(BF)
    outs[1].flush()
    for j in rest:
        j.advance()
    da_ref[:, 0:d] = mm(aot, dq_s[...]).astype(BF)
    da_ref[:, d : 2 * d] = (
        mm(aot, dko_s[...]) + mm(aft, dkf_in()[...]) + mm(ast, dks_in()[...])
    ).astype(BF)
    outs[0].flush()
    w_ref = w_in()
    dao[...] = (
        mm(dko_s[...], w_ref[:, d : 2 * d], NT)
        + mm(dvo_s[...], w_ref[:, 2 * d : 3 * d], NT)
        + mm(dq_s[...], w_ref[:, 0:d], NT)
    )
    for j in rest:
        j.advance()
    back.end(dao)
    dz, dgain = norm_back(x_in()[...].astype(F32), gain_in()[...], dao[...])
    g_ref[...] = gm_in()[...] + dz
    dgain_ref[...] = dgain
    for j in rest:
        j.complete()


def back_near(ins, daf, got, jobs, cid):
    n, d = ins[1].shape
    wide = jax.ShapeDtypeStruct((d, 2 * d), BF)
    return run(
        back_near_body, "back_near",
        ins, [smem()] + vmem(len(ins) - 1),
        [wide, wide, jax.ShapeDtypeStruct((n, d), F32), jax.ShapeDtypeStruct((1, d), F32)], vmem(4),
        [
            pltpu.VMEM((n, n), F32),
            pltpu.VMEM((128, n), F32),
            pltpu.VMEM((n, 128), F32),
            pltpu.VMEM((n, 128), F32),
            pltpu.VMEM((n, d), BF),
            pltpu.VMEM((n, d), BF),
            pltpu.VMEM((n, d), BF),
            pltpu.VMEM((n, d), F32),
        ],
        [Return(daf, got)] + jobs, cid,
        22 * n * d * d + 30 * QB * QB * d * 4, 2 * (8 * d * d + 24 * n * d),
    )


def first_body(ins, outs, scr, jobs):
    x_in, gain_in = ins
    a_ref = outs[0].ref
    for j in jobs:
        j.advance()
    xh, _ = norm_stats(x_in()[...].astype(F32))
    a_ref[...] = (xh * gain_in()[...]).astype(BF)
    for j in jobs:
        j.complete()


def first(x, gain, jobs, cid):
    n, d = x.shape
    return run(
        first_body, "first", [x, gain], vmem(2), [jax.ShapeDtypeStruct((n, d), BF)], vmem(1), [],
        jobs, cid, 10 * n * d, 4 * n * d,
    )


def layout_body(ins, outs, scr, jobs):
    count = len(ins) // 2
    for k in reversed(range(count)):
        ref = ins[count + k]()
        f = ref.shape[1] // 2
        outs[4].ref[k] = ref[:, 0:f].astype(F32)
        outs[5].ref[k] = ref[:, f : 2 * f].astype(F32).T
    outs[4].flush()
    outs[5].flush()
    for k in reversed(range(count)):
        v = ins[k]()[...].astype(F32)
        w = v.shape[1] // 4
        for i in range(3):
            outs[i].ref[k] = v[:, i * w : i * w + w]
        outs[3].ref[k] = v[:, 3 * w : 4 * w].T
    for i in range(4):
        outs[i].flush()


def layout(att, mlps):
    layers = len(att)
    d = att[0].shape[0]
    w = att[0].shape[1] // 4
    f = mlps[0].shape[1] // 2
    shapes = [(layers, d, w)] * 3 + [(layers, w, d), (layers, d, f), (layers, f, d)]
    return run(
        layout_body, "layout", att + mlps, vmem(2 * layers),
        [jax.ShapeDtypeStruct(x, F32) for x in shapes], vmem(6), [], [], None, 1, 6 * layers * d * (4 * w + 2 * f),
    )[0]


def wide_of(every, widths):
    outs = []
    at = 0
    for w in widths:
        outs += [every[z, :, at : at + w] for z in range(NZ)]
        at += w
    return jnp.concatenate(outs, axis=1)


def by_line(halves, counts):
    n = lax.axis_size("dp")
    cols = []
    for x, c in zip(halves, counts):
        for b in range(BITS, n.bit_length() - 1):
            x = x + lax.ppermute(x, "dp", [(i, i ^ (1 << b)) for i in range(n)])
        w = x.shape[1] // c
        for j in range(c):
            cols.append(x[:, j * w : (j + 1) * w].reshape(x.shape[0], NZ, w // NZ))
    return jnp.concatenate(cols, axis=2).transpose(1, 0, 2)


def on_device(
    tokens, lengths, noise_mask, cotangent, attn_gain, query_weight, key_weight, value_weight,
    out_weight, mlp_gain, up_weight, down_weight,
):
    n, d = tokens.shape
    dp = lax.axis_index("dp")
    t = lax.axis_index("tensor")
    info = jnp.stack([lengths[0], t]).astype(jnp.int32)
    base = (t % 2) * n
    piece_rows = d >> BITS
    at_a = slot_of(dp, ORDERS[0]) * piece_rows
    at_b = slot_of(dp, ORDERS[1]) * piece_rows

    def rows_of(w, at):
        return lax.dynamic_slice_in_dim(w, at, piece_rows, 0)

    def cols_of(w, at):
        return lax.dynamic_slice_in_dim(w, at, piece_rows, 1).T

    pa = []
    pm = []
    for l in range(LAYERS):
        pa.append(
            jnp.concatenate(
                [
                    rows_of(query_weight[l], at_a),
                    rows_of(key_weight[l], at_a),
                    rows_of(value_weight[l], at_b),
                    cols_of(out_weight[l], at_b),
                ],
                axis=1,
            )[None]
        )
        pm.append(jnp.stack([rows_of(up_weight[l], at_a), cols_of(down_weight[l], at_b)]))
    widths = (d // NZ,) * 4

    position = jnp.arange(LMAX, dtype=jnp.int32).astype(F32)
    frequency = jnp.exp(
        -math.log(10000.0) * jnp.arange(HD // 2, dtype=jnp.int32).astype(F32) / (HD // 2)
    )
    angles = position[:, None] * frequency[None, :]
    cos1 = jnp.cos(angles)
    sin1 = jnp.sin(angles)
    cos_all = jnp.concatenate([cos1] * 4, axis=1)
    sin_all = jnp.concatenate([-sin1, sin1] * 2, axis=1)
    cosf, sinf = cos_all[:n], sin_all[:n]
    cos = lax.dynamic_slice_in_dim(cos_all, base, n, 0)
    sin = lax.dynamic_slice_in_dim(sin_all, base, n, 0)

    pos = base + jnp.arange(n, dtype=jnp.int32)
    masked = lax.dynamic_slice_in_dim(noise_mask[0], base, n, 0)
    weight = ((pos < lengths[0]) & ((t >= 2) | (masked == 1))).astype(F32)

    (a,), ((every,),) = first(tokens, attn_gain[0:1], [Line(pa[0], False)], 0)
    piece = wide_of(every[:, 0], widths)
    ((wa,), (wide,)) = transfer("gather_first", [Gather(piece), Line(pm[0], True)], 1)
    was, wms, saved = [], [], []
    x = tokens
    for l in range(LAYERS):
        more = l + 1 < LAYERS
        jobs = [Gather(wide)] + ([Line(pa[l + 1], False)] if more else [])
        res, extra = attend(
            info, x, a, wa, cosf, sinf, cos, sin, mlp_gain[l : l + 1], jobs, 10 + l
        )
        q, ko, vo, kf, vf, ks, vs, o, lse, xm, m = res
        af, as_ = extra[0]
        wm = extra[1][0]
        was.append(wa)
        wms.append(wm)
        jobs = []
        if more:
            piece = wide_of(extra[2][0][:, 0], widths)
            jobs = [Gather(piece), Line(pm[l + 1], True)]
        nxt = min(l + 1, LAYERS - 1)
        (x_next, a_next, u), extra = mlp(xm, m, wm, attn_gain[nxt : nxt + 1], jobs, 20 + l)
        if more:
            wa, wide = extra[0][0], extra[1][0]
        saved.append((x, a, af, as_, q, kf, vf, ks, vs, ko, vo, o, lse, xm, m, u))
        x, a = x_next, a_next
    block_out = x

    g = cotangent.astype(F32) * weight[:, None]
    gains = [None] * (2 * LAYERS)
    att = [None] * LAYERS
    mlps = [None] * LAYERS
    att_grads = mlp_parts = None

    def joined(parts):
        return [jnp.concatenate([p[i] for p in parts], axis=1) for i in (0, 1)]

    for l in reversed(range(LAYERS)):
        x, a, af, as_, q, kf, vf, ks, vs, ko, vo, o, lse, xm, m, u = saved[l]
        above = l + 1 < LAYERS
        jobs = []
        if above:
            jobs = [Reduce(*att_grads), LineSum(by_line(joined(mlp_parts), (1, 1)))]
        res, extra = mlp_back(g, xm, m, u, wms[l], mlp_gain[l : l + 1], jobs, 30 + l)
        gm, go, dup, ddn, gains[LAYERS + l] = res
        jobs = [Reduce(dup, ddn, 0, 2)]
        if above:
            jobs += [LineSum(by_line(extra[0], (2, 2))), Gather(extra[1][0])]
        res, extra = back_far(
            info, go, o, lse, q, kf, vf, ks, vs, was[l], cosf, sinf, cos, sin, jobs, 40 + l
        )
        do, dqp, dkf, dvf, dks, dvs, daf = res
        got = extra[0][0]
        mlp_parts = [extra[1]]
        jobs = [Reduce(dup, ddn, 1, 2)]
        if above:
            mlps[l + 1] = extra[3][0]
            jobs.append(Gather(extra[2][0]))
        res, extra = back_near(
            [
                info, q, do, o, lse, ko, vo, dqp, cos, sin, go, af, dkf, dvf, as_, dks, dvs, a, was[l],
                x, gm, attn_gain[l : l + 1],
            ],
            daf, got, jobs, 50 + l,
        )
        mlp_parts.append(extra[1])
        if above:
            att[l + 1] = extra[2][0]
        att_grads = res[0:2]
        g, gains[l] = res[2:4]

    gain_rows = jnp.concatenate(gains, axis=0)
    (sums, (gain_rows,), (mlp_sum,)) = transfer(
        "reduce_last",
        [Reduce(*att_grads), PlaneSum(gain_rows), LineSum(by_line(joined(mlp_parts), (1, 1)))],
        2,
    )
    for b in range(BITS, lax.axis_size("dp").bit_length() - 1):
        size = lax.axis_size("dp")
        gain_rows = gain_rows + lax.ppermute(
            gain_rows, "dp", [(i, i ^ (1 << b)) for i in range(size)]
        )
    (part,), (gain_sums,), (mlps[0],) = transfer(
        "line_last",
        [
            LineSum(by_line(sums, (2, 2))),
            LineSum(jnp.broadcast_to(gain_rows, (NZ,) + gain_rows.shape)),
            Gather(mlp_sum),
        ],
        3,
    )
    ((att[0],),) = transfer("gather_last", [Gather(part)], 4)
    grads = layout(att, mlps)
    return (
        block_out, g, gain_sums[:LAYERS], grads[0], grads[1], grads[2], grads[3],
        gain_sums[LAYERS:], grads[4], grads[5],
    )


def solution(mesh):
    rows = P(("dp", "tensor"), None)
    cols = P(None, None, "tensor")
    mids = P(None, "tensor", None)
    return jax.shard_map(
        on_device,
        mesh=mesh,
        in_specs=(
            rows, P("dp"), P("dp", None), rows, P(), cols, cols, cols, mids, P(), cols, mids,
        ),
        out_specs=(rows, rows, P(), cols, cols, cols, mids, P(), cols, mids),
        check_vma=False,
    )
```

```python
import functools
import math

import jax
import jax.numpy as jnp
import numpy as np
from jax import lax
from jax.experimental import pallas as pl
from jax.experimental.pallas import tpu as pltpu
from jax.sharding import PartitionSpec as P

HD = 64
BLK = 16
LMAX = 1024
LAYERS = 2
EPS = 1e-05
NEG = -1e30
SCALE = 1.0 / math.sqrt(HD)
GC = math.sqrt(2.0 / math.pi)
GA = 0.044715
F32 = jnp.float32
BF = jnp.bfloat16
QB = 256
VMEM_LIMIT = 56 << 20

NN = (((1,), (0,)), ((), ()))
NT = (((1,), (1,)), ((), ()))
TN = (((0,), (0,)), ((), ()))


def mm(a, b, dims=NN):
    return lax.dot_general(a, b, dims, preferred_element_type=F32)


def norm_stats(x):
    mean = jnp.mean(x, axis=-1, keepdims=True)
    c = x - mean
    var = jnp.mean(c * c, axis=-1, keepdims=True)
    r = lax.rsqrt(var + EPS)
    return c * r, r


def norm_back(x, gain, dy):
    xh, r = norm_stats(x)
    gy = dy * gain
    m1 = jnp.mean(gy, axis=-1, keepdims=True)
    m2 = jnp.mean(gy * xh, axis=-1, keepdims=True)
    dz = r * (gy - m1 - xh * m2)
    return dz, jnp.sum(dy * xh, axis=0, keepdims=True)


def turn(y, cos, sin):
    lane = lax.broadcasted_iota(jnp.int32, y.shape, 1) % HD
    other = jnp.where(
        lane < HD // 2, pltpu.roll(y, 128 - HD // 2, 1), pltpu.roll(y, HD // 2, 1)
    )
    return y * cos + other * sin


def vmem(n):
    return [pl.BlockSpec(memory_space=pltpu.VMEM)] * n


def smem():
    return pl.BlockSpec(memory_space=pltpu.SMEM)


def params(**kw):
    return pltpu.CompilerParams(vmem_limit_bytes=VMEM_LIMIT, **kw)


def cost(flops, nbytes, trans=0):
    return pl.CostEstimate(flops=int(flops), bytes_accessed=int(nbytes), transcendentals=int(trans))


MESH = pl.DeviceIdType.MESH
BITS = 3
ORDERS = ((0, 1, 2), (0, 2, 1))
NZ = 4


def bit_of(dp, b):
    return dp // (1 << b) % 2


def slot_of(dp, order):
    out = 0
    for b in order:
        out = out * 2 + bit_of(dp, b)
    return out


def partner(dp, b):
    return dp + (1 - 2 * bit_of(dp, b)) * (1 << b)


def greet(plane, line):
    dp = lax.axis_index("dp")
    t = lax.axis_index("tensor")
    barrier = pltpu.get_barrier_semaphore()
    if plane:
        for b in range(BITS):
            pl.semaphore_signal(barrier, inc=1, device_id=(partner(dp, b), t), device_id_type=MESH)
    if line:
        for s in range(1, NZ):
            pl.semaphore_signal(barrier, inc=1, device_id=(dp, (t + s) % NZ), device_id_type=MESH)
    pl.semaphore_wait(barrier, BITS * plane + (NZ - 1) * line)


def remote(src, dst, send, recv, dp, t):
    return pltpu.make_async_remote_copy(
        src_ref=src, dst_ref=dst, send_sem=send, recv_sem=recv, device_id=(dp, t), device_id_type=MESH
    )


def aligned(x, n=16):
    return pl.multiple_of(x, n)


def dma(n):
    return pltpu.SemaphoreType.DMA((n,))


def any_spec(n=1):
    return [pl.BlockSpec(memory_space=pl.ANY)] * n


class Job:
    plane = line = 0
    steps = BITS

    def bind(self, ins, outs, scr):
        self.at = 0
        self.i, self.o, self.s = ins, outs, scr
        self.dp = lax.axis_index("dp")
        self.t = lax.axis_index("tensor")

    def wait(self, s):
        pass

    def advance(self):
        if self.at < self.steps:
            if self.at > 0:
                self.wait(self.at - 1)
            self.start(self.at)
            self.at += 1

    def complete(self):
        while self.at < self.steps:
            self.advance()
        if self.steps:
            self.wait(self.steps - 1)


class Gather(Job):
    plane = 1

    def __init__(self, piece):
        self.rows, n = piece.shape
        self.half = n // 2
        self.ins, self.in_specs = [piece], vmem(1)
        self.outs, self.out_specs = [jax.ShapeDtypeStruct((self.rows << BITS, n), BF)], any_spec()
        self.scratch = [dma(2 * BITS), dma(2 * BITS), dma(2)]

    def cols(self, i):
        return pl.ds(i * self.half, self.half)

    def own(self, i):
        at = slot_of(self.dp, ORDERS[i]) * self.rows
        return pltpu.make_async_copy(
            self.i[0].at[:, self.cols(i)],
            self.o[0].at[pl.ds(aligned(at), self.rows), self.cols(i)],
            self.s[2].at[i],
        )

    def copy(self, s, i):
        b = ORDERS[i][BITS - 1 - s]
        size = self.rows << s
        at = slot_of(self.dp, ORDERS[i]) // (1 << s) * size
        there = self.o[0].at[pl.ds(aligned(at), size), self.cols(i)]
        return remote(
            self.i[0].at[:, self.cols(i)] if s == 0 else there, there,
            self.s[0].at[2 * s + i], self.s[1].at[2 * s + i], partner(self.dp, b), self.t,
        )

    def start(self, s):
        for i in range(2):
            self.copy(s, i).start()
            if s == 0:
                self.own(i).start()

    def wait(self, s):
        for i in range(2):
            self.copy(s, i).wait()
            if s == 0:
                self.own(i).wait()


class Reduce(Job):
    plane = 1

    def __init__(self, a, b, part=0, parts=1):
        self.full = a.shape[0]
        widths = (a.shape[1] // parts, b.shape[1] // parts)
        self.cols = [pl.ds(part * w, w) for w in widths]
        self.ins, self.in_specs = [a, b], any_spec(2)
        self.outs = [jax.ShapeDtypeStruct((self.full >> BITS, w), BF) for w in widths]
        self.out_specs = vmem(2)
        self.scratch = [pltpu.VMEM((self.full // 2, w), BF) for w in widths]
        for w in widths:
            self.scratch += [pltpu.VMEM((self.full >> (s + 1), w), BF) for s in range(BITS)]
        self.scratch += [dma(2 * BITS), dma(2 * BITS), dma(2)]

    def got(self, s, i):
        return self.s[2 + i * BITS + s]

    def offset(self, s, i):
        at = 0
        for j in range(1, s):
            at = at + bit_of(self.dp, ORDERS[i][j]) * (self.full >> (j + 1))
        return at

    def copy(self, s, i):
        b = ORDERS[i][s]
        size = self.full >> (s + 1)
        at = (1 - bit_of(self.dp, b)) * size
        if s == 0:
            there = self.i[i].at[pl.ds(aligned(at), size), self.cols[i]]
        else:
            there = self.s[i].at[pl.ds(aligned(self.offset(s, i) + at), size), :]
        send, recv = self.s[2 + 2 * BITS], self.s[3 + 2 * BITS]
        return remote(
            there, self.got(s, i), send.at[2 * s + i], recv.at[2 * s + i], partner(self.dp, b), self.t
        )

    def own(self, i):
        size = self.full // 2
        at = bit_of(self.dp, ORDERS[i][0]) * size
        return pltpu.make_async_copy(
            self.i[i].at[pl.ds(aligned(at), size), self.cols[i]], self.s[i], self.s[4 + 2 * BITS].at[i]
        )

    def start(self, s):
        for i in range(2):
            self.copy(s, i).start()
            if s == 0:
                self.own(i).start()

    def wait(self, s):
        for i in range(2):
            self.copy(s, i).wait()
            if s == 0:
                self.own(i).wait()
            size = self.full >> (s + 1)
            base = self.offset(s + 1, i)
            keep, got, out = self.s[i], self.got(s, i), self.o[i]
            last = s == BITS - 1
            step = 48 if size % 48 == 0 else size

            def add(j, carry):
                rows = pl.ds(aligned(base + j * step), step)
                here = pl.ds(aligned(j * step), step)
                total = (keep[rows, :].astype(F32) + got[here, :].astype(F32)).astype(BF)
                if last:
                    out[here, :] = total
                else:
                    keep[rows, :] = total
                return carry

            lax.fori_loop(0, size // step, add, 0)


class Line(Job):
    line = 1
    steps = NZ - 1

    def __init__(self, parts, wide, shape=None):
        self.count, self.rows, self.w = shape if parts is None else parts.shape
        self.wide = wide
        self.src = None
        self.ins, self.in_specs = ([], []) if parts is None else ([parts], vmem(1))
        if wide:
            shape = (self.rows, self.count * NZ * self.w)
        else:
            shape = (NZ, self.count, self.rows, self.w)
        self.outs, self.out_specs = [jax.ShapeDtypeStruct(shape, BF)], any_spec()
        m = self.count * 2 * self.steps
        self.scratch = [dma(m), dma(m), dma(self.count)]

    def place(self, p, z):
        if self.wide:
            at = (p * NZ + z) * self.w
            return self.o[0].at[:, pl.ds(aligned(at, 128), self.w)]
        return self.o[0].at[z, p]

    def copy(self, s, p, way):
        z = (self.t - way * s) % NZ
        k = (s * 2 + (way > 0)) * self.count + p
        there = self.place(p, z)
        return remote(
            self.source().at[p] if s == 0 else there, there, self.s[0].at[k], self.s[1].at[k],
            self.dp, (self.t + way) % NZ,
        )

    def source(self):
        return self.i[0] if self.src is None else self.src

    def inside(self, s, way, receiver):
        t = self.t
        if receiver:
            return (t - way * (s + 1) >= 0) & (t - way * (s + 1) < NZ)
        return (t - way * s >= 0) & (t - way * s < NZ) & (t + way >= 0) & (t + way < NZ)

    def own(self, p):
        return pltpu.make_async_copy(self.source().at[p], self.place(p, self.t), self.s[2].at[p])

    def start(self, s):
        for way in (1, -1):

            @pl.when(self.inside(s, way, False))
            def _(way=way):
                for p in range(self.count):
                    self.copy(s, p, way).start()

        if s == 0:
            for p in range(self.count):
                self.own(p).start()

    def wait(self, s):
        for way in (1, -1):

            @pl.when(self.inside(s, way, True))
            def _(way=way):
                for p in range(self.count):
                    self.copy(s, p, way).wait_recv()

            @pl.when(self.inside(s, way, False))
            def _(way=way):
                for p in range(self.count):
                    self.copy(s, p, way).wait_send()

        if s == 0:
            for p in range(self.count):
                self.own(p).wait()


class LineSum(Job):
    line = 1
    steps = 1

    def __init__(self, parts):
        shape = parts.shape[1:]
        self.ins, self.in_specs = [parts], vmem(1)
        self.outs, self.out_specs = [jax.ShapeDtypeStruct(shape, parts.dtype)], vmem(1)
        self.scratch = [pltpu.VMEM((NZ - 1,) + shape, parts.dtype), dma(3), dma(3)]

    def copies(self):
        for s in (1, 2, 3):
            z = (self.t + s) % NZ
            yield remote(
                self.i[0].at[z], self.s[0].at[s - 1], self.s[1].at[s - 1], self.s[2].at[s - 1], self.dp, z
            )

    def start(self, s):
        for c in self.copies():
            c.start()

    def wait(self, s):
        for c in self.copies():
            c.wait()
        got = self.s[0]
        total = self.i[0][self.t].astype(F32)
        for k in range(NZ - 1):
            total = total + got[k].astype(F32)
        self.o[0][...] = total.astype(self.o[0].dtype)


class PlaneSum(Job):
    plane = 1

    def __init__(self, x):
        self.ins, self.in_specs = [x], vmem(1)
        self.outs, self.out_specs = [jax.ShapeDtypeStruct(x.shape, F32)], vmem(1)
        self.scratch = [pltpu.VMEM((BITS,) + x.shape, F32), dma(BITS), dma(BITS)]

    def copy(self, s):
        return remote(
            self.i[0] if s == 0 else self.o[0], self.s[0].at[s], self.s[1].at[s], self.s[2].at[s],
            partner(self.dp, s), self.t,
        )

    def start(self, s):
        self.copy(s).start()

    def wait(self, s):
        self.copy(s).wait()
        self.o[0][...] = (self.i[0] if s == 0 else self.o[0])[...] + self.s[0][s]


class Spread(Job):
    line = 1
    steps = 0

    def __init__(self, a):
        self.ins, self.in_specs = [a], any_spec()
        self.outs, self.out_specs = [jax.ShapeDtypeStruct(a.shape, BF)] * 2, any_spec(2)
        self.scratch = [pltpu.VMEM(a.shape, BF), pltpu.VMEM(a.shape, BF), dma(2), dma(2), dma(2)]

    def put(self, src, which, to, k):
        return remote(src, self.s[which], self.s[2].at[k], self.s[3].at[which], self.dp, to)

    def save(self, which):
        return pltpu.make_async_copy(self.s[which], self.o[which], self.s[4].at[which])

    def begin(self):
        a, t = self.i[0], self.t

        @pl.when(t == 2)
        def _():
            self.put(a, 0, 1, 0).start()
            self.put(a, 0, 3, 1).start()

        @pl.when(t % 2 == 0)
        def _():
            self.s[0][...] = jnp.zeros_like(self.s[0])

        @pl.when(t >= 2)
        def _():
            self.s[1][...] = jnp.zeros_like(self.s[1])

    def first(self):
        a, t = self.i[0], self.t

        @pl.when(t % 2 == 1)
        def _():
            self.put(a, 0, 1, 0).wait_recv()

        @pl.when(t == 1)
        def _():
            self.put(self.s[0], 1, 0, 0).start()

        @pl.when(t == 3)
        def _():
            self.put(a, 1, 1, 0).start()

        self.save(0).start()

    def second(self):
        @pl.when(self.t < 2)
        def _():
            self.put(self.i[0], 1, 1, 0).wait_recv()

        self.save(1).start()

    def end(self):
        a, t = self.i[0], self.t

        @pl.when(t >= 1)
        def _():
            self.put(a, 0, 1, 0).wait_send()

        @pl.when(t == 2)
        def _():
            self.put(a, 0, 3, 1).wait_send()

        self.save(0).wait()
        self.save(1).wait()


class Early(Job):
    line = 1
    steps = 0

    def __init__(self, shape):
        self.ins, self.in_specs = [], []
        self.outs, self.out_specs = [jax.ShapeDtypeStruct(shape, BF)], any_spec()
        self.scratch = [dma(1), dma(1)]

    def put(self, src, to):
        return remote(src, self.o[0], self.s[0].at[0], self.s[1].at[0], self.dp, to)

    def go(self, das):
        @pl.when(self.t < 2)
        def _():
            self.put(das, 2 * self.t + 1).start()

    def end(self, das):
        @pl.when(self.t < 2)
        def _():
            self.put(das, 1).wait_send()

        @pl.when(self.t % 2 == 1)
        def _():
            self.put(das, 1).wait_recv()


class Return(Job):
    line = 1
    steps = 0

    def __init__(self, daf, got):
        self.ins, self.in_specs = [daf, got], vmem(2)
        self.outs, self.out_specs = [], []
        sd = pltpu.VMEM(daf.shape, BF)
        self.scratch = [sd, sd, sd, dma(1), dma(2)]

    def put(self, src, which):
        return remote(src, self.s[which], self.s[3].at[0], self.s[4].at[which], self.dp, 2)

    def begin(self):
        daf, got = self.i

        @pl.when(self.t == 1)
        def _():
            self.s[2][...] = (daf[...].astype(F32) + got[...].astype(F32)).astype(BF)
            self.put(self.s[2], 0).start()

        @pl.when(self.t == 3)
        def _():
            self.put(daf, 1).start()

    def end(self, acc):
        daf, got = self.i

        @pl.when(self.t == 2)
        def _():
            self.put(daf, 0).wait_recv()
            self.put(daf, 1).wait_recv()
            acc[...] += self.s[0][...].astype(F32) + self.s[1][...].astype(F32)

        @pl.when(self.t == 3)
        def _():
            acc[...] += got[...].astype(F32)

        @pl.when(self.t % 2 == 1)
        def _():
            self.put(daf, 0).wait_send()


def steps_at(jobs, point, points):
    for s in range(max([j.steps for j in jobs], default=0)):
        now = [j for j in jobs if s < j.steps and s * points // j.steps == point]
        for j in now:
            if s > 0:
                j.wait(s - 1)
        for j in now:
            j.start(s)


def finish(jobs):
    for j in jobs:
        if j.steps:
            j.wait(j.steps - 1)


class In:
    def __init__(self, hbm, ref, sem):
        self.ref = ref
        self.copy = pltpu.make_async_copy(hbm, ref, sem)
        self.copy.start()

    def __call__(self):
        if self.copy is not None:
            self.copy.wait()
            self.copy = None
        return self.ref


class Out:
    def __init__(self, hbm, ref, sem):
        self.ref = ref
        self.copy = pltpu.make_async_copy(ref, hbm, sem)
        self.sent = False

    def flush(self):
        if not self.sent:
            self.copy.start()
            self.sent = True


def meet(jobs):
    greet(max(j.plane for j in jobs), max(j.line for j in jobs))


def lazily(body, ins, in_specs, outs, out_specs, scratch):
    lazy = [sp.memory_space == pltpu.VMEM for sp in in_specs]
    picks = [x[1] if isinstance(x, tuple) else None for x in ins]
    ins = [x[0] if isinstance(x, tuple) else x for x in ins]
    bufs = [
        pltpu.VMEM(x.shape if p is None else x.shape[1:], x.dtype)
        for x, z, p in zip(ins, lazy, picks)
        if z
    ]
    bufs += [pltpu.VMEM(x.shape, x.dtype) for x in outs]
    own = len(scratch)
    count = sum(lazy)

    def wrapped(i, o, s, jobs):
        mine, rest = s[:own], s[own:]
        vm, sin, sout = rest[:-2], rest[-2], rest[-1]
        given = []
        k = 0
        for ref, z, p in zip(i, lazy, picks):
            if z:
                if p is not None:
                    ref = ref.at[lax.axis_index("tensor") % 2 if p else 0]
                given.append(In(ref, vm[k], sin.at[k]))
                k += 1
            else:
                given.append(ref)
        results = [Out(ref, vm[count + k], sout.at[k]) for k, ref in enumerate(o)]
        if jobs:
            meet(jobs)
        body(given, results, mine, jobs)
        for x, z in zip(given, lazy):
            if z:
                x()
        for x in results:
            x.flush()
        for x in results:
            x.copy.wait()

    specs = [any_spec()[0] if z else sp for sp, z in zip(in_specs, lazy)]
    return wrapped, ins, specs, any_spec(len(outs)), list(scratch) + bufs + [dma(count), dma(len(outs))]


def run(body, name, ins, in_specs, outs, out_specs, scratch, jobs, cid, flops, nbytes, grid=None):
    late = grid is None and len(ins) > 0
    if late:
        body, ins, in_specs, out_specs, scratch = lazily(body, ins, in_specs, outs, out_specs, scratch)
    cuts = []
    for what in ("ins", "outs", "scratch"):
        own = {"ins": ins, "outs": outs, "scratch": scratch}[what]
        cuts.append([len(own)] + [len(getattr(j, what)) for j in jobs])

    def kernel(*refs):
        at = 0
        groups = []
        for cut in cuts:
            g = []
            for c in cut:
                g.append(refs[at : at + c])
                at += c
            groups.append(g)
        for k, j in enumerate(jobs):
            j.bind(groups[0][k + 1], groups[1][k + 1], groups[2][k + 1])
        if jobs and not late:
            if grid is None:
                meet(jobs)
            else:
                pl.when(pl.program_id(0) == 0)(functools.partial(meet, jobs))
        body(groups[0][0], groups[1][0], groups[2][0], jobs)

    for j in jobs:
        ins, in_specs = list(ins) + j.ins, list(in_specs) + j.in_specs
        outs, out_specs = list(outs) + j.outs, list(out_specs) + j.out_specs
        scratch = list(scratch) + j.scratch
    res = pl.pallas_call(
        kernel,
        out_shape=tuple(outs),
        in_specs=list(in_specs),
        out_specs=tuple(out_specs),
        scratch_shapes=list(scratch),
        compiler_params=params(collective_id=cid, has_side_effects=True) if jobs else params(),
        cost_estimate=cost(flops, nbytes),
        name=name,
        **({} if grid is None else {"grid": grid}),
    )(*ins)
    at = cuts[1][0]
    extra = []
    for c in cuts[1][1:]:
        extra.append(res[at : at + c])
        at += c
    return res[: cuts[1][0]], extra


def only_jobs(ins, outs, scr, jobs):
    for s in range(max(j.steps for j in jobs)):
        for j in jobs:
            j.advance()
    for j in jobs:
        j.complete()


def transfer(name, jobs, cid):
    return run(only_jobs, name, [], [], [], [], [], jobs, cid, 1, 1 << 24)[1]


def turned(out, tmp, cos, sin):
    for g in range(out.shape[1] // 128):
        sl = slice(g * 128, g * 128 + 128)
        out[:, sl] = turn(tmp[:, sl], cos[...], sin[...]).astype(BF)


def near_bias(info, bias):
    n = bias.shape[0]
    length = info[0]
    t = lax.axis_index("tensor")
    noisy = t < 2
    base = t % 2 * n
    j = lax.broadcasted_iota(jnp.int32, (n, n), 0)
    i = lax.broadcasted_iota(jnp.int32, (n, n), 1)
    bi = i // BLK
    bj = j // BLK
    low = jnp.where(noisy, bi, 0)
    seen = (bj <= bi) & (bj >= low) & (j + base < length)
    bias[...] = jnp.where(seen | (i == j), 0.0, NEG)


def far_masks(info, first, second, hot):
    n = hot.shape[1]
    length = info[0]
    t = lax.axis_index("tensor")
    noisy = t < 2
    odd = t % 2
    key = lax.broadcasted_iota(jnp.int32, (n, 128), 0)
    block = lax.broadcasted_iota(jnp.int32, (n, 128), 1) % HD
    real = block < n // BLK
    odd_lim = jnp.where(odd == 1, length, 0)
    lim = jnp.where(noisy, length - odd * n, 0)
    first[...] = jnp.where(real & (key >= odd_lim), NEG, 0.0).astype(BF)
    hidden = (key // BLK >= block) | (key >= lim)
    second[...] = jnp.where(real & hidden, NEG, 0.0).astype(BF)
    row = lax.broadcasted_iota(jnp.int32, (128, n), 0) % HD
    query = lax.broadcasted_iota(jnp.int32, (128, n), 1)
    hot[...] = jnp.where(query // BLK == row, 1.0, 0.0).astype(BF)


def half_of(h, shape, axis):
    at = lax.broadcasted_iota(jnp.int32, shape, axis)
    return (at < HD) if h == 0 else (at >= HD)


def attend_body(row, ins, outs, scr, jobs):
    info, a_in, w_in, cos_in, sin_in, cosf_in, sinf_in, x_in, gain_in = ins
    q_ref, ko_ref, vo_ref, kf_ref, vf_ref, ks_ref, vs_ref, o_ref, lse_ref, xm_ref, m_ref = [
        x.ref for x in outs
    ]
    tmp, bias, mask1, mask2, hot, acc, top, tot = scr
    spread = jobs[0]
    rest = jobs[1:]
    af_ref, as_ref = spread.s[0:2]
    n, d = x_in.ref.shape
    pairs = d // 128
    gather = rest[0]
    line = rest[1:]
    spread.begin()
    gather.advance()
    near_bias(info, bias)
    far_masks(info, mask1, mask2, hot)
    a_ref = a_in()
    w_ref = w_in()
    cos = cos_in()
    sin = sin_in()

    tmp[...] = mm(a_ref[...], w_ref[:, 0:d]) * SCALE
    turned(q_ref, tmp, cos, sin)

    def keys_of(src, kk, vv, c, s):
        av = src[...]
        tmp[...] = mm(av, w_ref[:, d : 2 * d])
        turned(kk, tmp, c, s)
        vv[...] = mm(av, w_ref[:, 2 * d : 3 * d]).astype(BF)

    keys_of(a_ref, ko_ref, vo_ref, cos, sin)
    for k in range(3):
        outs[k].flush()

    def segment(kk, vv, mask, full, first, last):
        def pair(g, carry):
            sl = pl.ds(aligned(g * 128, 128), 128)
            qt = q_ref[:, sl].T
            k2 = kk[:, sl]
            vt = vv[:, sl].T
            other_q = jnp.zeros_like(qt) if mask is None else hot[...]
            other_k = k2 if mask is None else mask[...]
            rows = pl.ds(aligned(g * 128, 128), 128)
            if not first:
                olds = top[g]
                tots = tot[g]
                before = acc[rows, :]
            tops, sums, outs = [], [], []
            chains = [(h, b) for h in range(2) for b in range(n // QB)]
            scores = []
            for h, b in chains:
                qh = jnp.where(half_of(h, qt.shape, 0), qt, other_q)
                kh = jnp.where(half_of(h, k2.shape, 1), k2, other_k)
                width = n if full else (b + 1) * QB
                scores.append(mm(kh[0:width], qh[:, b * QB : b * QB + QB]))
            for (h, b), s in zip(chains, scores):
                cs = slice(b * QB, b * QB + QB)
                width = s.shape[0]
                if mask is None:
                    s = s + bias[0:width, cs]
                mx = jnp.max(s, axis=0, keepdims=True)
                if not first:
                    old = olds[h : h + 1, cs]
                    mx = jnp.maximum(mx, old)
                    scale = jnp.exp(old - mx)
                e = jnp.exp(s - mx)
                total = jnp.sum(e, axis=0, keepdims=True)
                out = mm(vt[h * HD : h * HD + HD, 0:width], e.astype(BF))
                if not first:
                    total = total + tots[h : h + 1, cs] * scale
                    out = out + before[h * HD : h * HD + HD, cs] * scale
                if last:
                    mx = mx + jnp.log(total)
                    out = out / total
                tops.append(mx)
                sums.append(total)
                outs.append(out)
            for (h, b), mx, total, out in zip(chains, tops, sums, outs):
                cs = slice(b * QB, b * QB + QB)
                if last:
                    lse_ref[g, h : h + 1, cs] = mx
                else:
                    top[g, h : h + 1, cs] = mx
                    tot[g, h : h + 1, cs] = total
                    acc[pl.ds(aligned(g * 128 + h * HD, HD), HD), cs] = out
            if last:
                ot = jnp.concatenate(
                    [jnp.concatenate(outs[i : i + n // QB], axis=1) for i in (0, n // QB)], axis=0
                )
                o_ref[:, sl] = ot.T.astype(BF)
            return carry

        return pair

    lax.fori_loop(0, pairs, segment(ko_ref, vo_ref, None, False, True, False), 0)
    gather.advance()
    spread.first()
    keys_of(af_ref, kf_ref, vf_ref, cosf_in(), sinf_in())
    outs[3].flush()
    outs[4].flush()
    lax.fori_loop(0, pairs, segment(kf_ref, vf_ref, mask1, True, False, False), 0)
    spread.second()
    for j in line:
        j.advance()
    keys_of(as_ref, ks_ref, vs_ref, cos, sin)
    outs[5].flush()
    outs[6].flush()
    last = segment(ks_ref, vs_ref, mask2, False, False, True)
    lax.fori_loop(0, pairs // 2, last, 0)
    gather.advance()
    for j in line:
        j.advance()
    lax.fori_loop(pairs // 2, pairs, last, 0)
    for j in line:
        j.advance()
    outs[7].flush()
    outs[8].flush()
    xm = x_in()[...].astype(F32) + mm(o_ref[...], w_ref[:, 3 * d : 4 * d], NT)
    xm_ref[...] = xm
    outs[9].flush()
    xh, _ = norm_stats(xm)
    m_ref[...] = (xh * gain_in()[row : row + 1]).astype(BF)
    outs[10].flush()
    spread.end()
    gather.complete()
    for j in line:
        j.complete()


def attend(info, x, a, w, cosf, sinf, cos, sin, gain, row, jobs, cid):
    n, d = x.shape
    sd = jax.ShapeDtypeStruct((n, d), BF)
    heads = (d // 128, 8, n)
    return run(
        functools.partial(attend_body, row), "attend",
        [info, a, w, cos, sin, cosf, sinf, x, gain], [smem()] + vmem(8),
        [sd] * 8 + [jax.ShapeDtypeStruct(heads, F32), jax.ShapeDtypeStruct((n, d), F32), sd],
        vmem(11),
        [
            pltpu.VMEM((n, d), F32),
            pltpu.VMEM((n, n), F32),
            pltpu.VMEM((n, 128), BF),
            pltpu.VMEM((n, 128), BF),
            pltpu.VMEM((128, n), BF),
            pltpu.VMEM((d, n), F32),
            pltpu.VMEM(heads, F32),
            pltpu.VMEM(heads, F32),
        ],
        [Spread(a)] + jobs, cid,
        16 * n * d * d + 40 * QB * QB * d * 4, 2 * (4 * d * d + 16 * n * d),
    )


MLP_STEPS = 6
SPLIT = 2
SPLITB = 2


def gelu(u):
    return u * (0.5 * jnp.tanh(u * (GC + (GC * GA) * (u * u))) + 0.5)


def grid_steps(jobs):
    step = pl.program_id(0)
    for point in range(MLP_STEPS):
        if any(s * MLP_STEPS // j.steps == point for j in jobs for s in range(j.steps)):
            pl.when(step == point)(functools.partial(steps_at, jobs, point, MLP_STEPS))


def mlp_body(row, ins, outs, scr, jobs):
    xm_ref, m_ref, up_ref, dn_ref, gain = ins
    x_ref, a_ref, u_ref = outs
    (acc,) = scr
    step = pl.program_id(0)
    grid_steps(jobs)

    @pl.when(step == 0)
    def _():
        acc[...] = xm_ref[...]

    up = up_ref[...]
    dn = dn_ref[...]
    cut = m_ref.shape[0] // SPLIT
    us = [mm(m_ref[i * cut : (i + 1) * cut], up) for i in range(SPLIT)]
    for i, u in enumerate(us):
        rows = slice(i * cut, (i + 1) * cut)
        u_ref[rows] = u.astype(BF)
        acc[rows] += mm(gelu(u).astype(BF), dn, NT)

    @pl.when(step == pl.num_programs(0) - 1)
    def _():
        x = acc[...]
        x_ref[...] = x
        xh, _ = norm_stats(x)
        a_ref[...] = (xh * gain[row : row + 1]).astype(BF)
        finish(jobs)


def mlp(xm, m, w, gain, row, jobs, cid):
    n, d = xm.shape
    ff = w.shape[1] // 2
    steps = MLP_STEPS if jobs else MLP_STEPS // 2
    fc = ff // steps
    full = pl.BlockSpec((n, d), lambda i: (0, 0))
    return run(
        functools.partial(mlp_body, row), "mlp",
        [xm, m, w, w, gain],
        [
            full,
            full,
            pl.BlockSpec((d, fc), lambda i: (0, i)),
            pl.BlockSpec((d, fc), lambda i: (0, i + steps)),
            pl.BlockSpec(gain.shape, lambda i: (0, 0)),
        ],
        [
            jax.ShapeDtypeStruct((n, d), F32),
            jax.ShapeDtypeStruct((n, d), BF),
            jax.ShapeDtypeStruct((n, ff), BF),
        ],
        [full, full, pl.BlockSpec((n, fc), lambda i: (0, i))],
        [pltpu.VMEM((n, d), F32)],
        jobs, cid,
        4 * n * d * ff, 4 * d * ff + 2 * n * ff + 10 * n * d, grid=(steps,),
    )


def mlp_back_body(at, ins, outs, scr, jobs):
    g_ref, xm_ref, m_ref, u_ref, up_ref, dn_ref, gain = ins[:7]
    gm_ref, go_ref, dup_ref, ddn_ref, dgain_ref = outs
    gy, gyt, mt, dm = scr[:4]
    step = pl.program_id(0)
    grid_steps(jobs)
    if len(ins) > 7:
        counted, info = ins[7:]
        cot_ref, g_ref = g_ref, scr[4]

        @pl.when(step == 0)
        def _():
            n = cot_ref.shape[0]
            t = lax.axis_index("tensor")
            base = t % 2 * n
            masked = counted[:, pl.ds(aligned(base, 128), n)]
            pos = base + lax.broadcasted_iota(jnp.int32, (1, n), 1)
            live = (pos < info[0]) & ((t >= 2) | (masked == 1))
            col = jnp.broadcast_to(jnp.where(live, 1.0, 0.0), (8, n)).T[:, 0:1]
            g_ref[...] = cot_ref[...].astype(F32) * col

    @pl.when(step == 0)
    def _():
        gb = g_ref[...].astype(BF)
        gy[...] = gb
        gyt[...] = gb.T
        mt[...] = m_ref[...].T
        dm[...] = jnp.zeros_like(dm)

    cut = u_ref.shape[1] // SPLITB
    gyv, gytv, mtv = gy[...], gyt[...], mt[...]
    parts = [slice(i * cut, (i + 1) * cut) for i in range(SPLITB)]
    dhs = [mm(gyv, dn_ref[:, c]) for c in parts]
    add = None
    for c, dh in zip(parts, dhs):
        u = u_ref[:, c].astype(F32)
        u2 = u * u
        th = jnp.tanh(u * (GC + (GC * GA) * u2))
        half = 0.5 * th + 0.5
        h = (u * half).astype(BF)
        slope = half + (u * (1.0 - th * th)) * ((0.5 * GC) + (1.5 * GC * GA) * u2)
        du = (dh * slope).astype(BF)
        more = mm(du, up_ref[:, c], NT)
        add = more if add is None else add + more
        dup_ref[:, c] = mm(mtv, du).astype(BF)
        ddn_ref[:, c] = mm(gytv, h).astype(BF)
    dm[...] += add

    @pl.when(step == MLP_STEPS - 1)
    def _():
        dz, dgain = norm_back(xm_ref[...], gain[at : at + 1], dm[...])
        gm = g_ref[...] + dz
        gm_ref[...] = gm
        go_ref[...] = gm.astype(BF)
        dgain_ref[...] = dgain
        finish(jobs)


def mlp_back(g, xm, m, u, w, gain, at, top, jobs, cid):
    n, d = xm.shape
    ff = w.shape[1] // 2
    steps = MLP_STEPS
    fc = ff // steps
    full = pl.BlockSpec((n, d), lambda i: (0, 0))
    row = pl.BlockSpec((1, d), lambda i: (0, 0))
    wide = pl.BlockSpec((d, fc), lambda i: (0, i))
    return run(
        functools.partial(mlp_back_body, at), "mlp_back",
        [g, xm, m, u, w, w, gain] + top,
        [
            full, full, full,
            pl.BlockSpec((n, fc), lambda i: (0, i)),
            wide,
            pl.BlockSpec((d, fc), lambda i: (0, i + steps)),
            pl.BlockSpec(gain.shape, lambda i: (0, 0)),
        ]
        + ([pl.BlockSpec(top[0].shape, lambda i: (0, 0)), smem()] if top else []),
        [
            jax.ShapeDtypeStruct((n, d), F32),
            jax.ShapeDtypeStruct((n, d), BF),
            jax.ShapeDtypeStruct((d, ff), BF),
            jax.ShapeDtypeStruct((d, ff), BF),
            jax.ShapeDtypeStruct((1, d), F32),
        ],
        [full, full, wide, wide, row],
        [
            pltpu.VMEM((n, d), BF),
            pltpu.VMEM((d, n), BF),
            pltpu.VMEM((d, n), BF),
            pltpu.VMEM((n, d), F32),
        ]
        + ([pltpu.VMEM((n, d), F32)] if top else []),
        jobs, cid,
        8 * n * d * ff, 8 * d * ff + 2 * n * ff + 16 * n * d, grid=(steps,),
    )


def back_pair(g, segs, q_ref, do_ref, o_ref, lse_ref, hot, dqt, dka, dva):
    n = q_ref.shape[0]
    sl = pl.ds(aligned(g * 128, 128), 128)
    q2 = q_ref[:, sl]
    do2 = do_ref[:, sl]
    qt = q2.T
    dot = do2.T
    prod = dot.astype(F32) * o_ref[:, sl].T.astype(F32)
    for h in range(2):
        hs = slice(h * HD, h * HD + HD)
        low = half_of(h, qt.shape, 0)
        side = half_of(h, q2.shape, 1)
        none = jnp.zeros_like(q2)
        qth = jnp.where(low, qt, jnp.zeros_like(qt) if hot is None else hot[...])
        doth = jnp.where(low, dot, jnp.zeros_like(dot))
        qh = jnp.where(side, q2, none)
        doh = jnp.where(side, do2, none)
        dsum = jnp.sum(prod[hs], axis=0, keepdims=True)
        ls = lse_ref[g, h : h + 1, :]
        for at, (kr, vr, mask, bias, whole, base) in enumerate(segs):
            k2 = kr[:, sl]
            v2 = vr[:, sl]
            kt = k2.T
            kh = jnp.where(side, k2, none if mask is None else mask[...])
            for b in range(n // QB):
                cs = slice(b * QB, b * QB + QB)
                width = n if whole else (b + 1) * QB
                s = mm(kh[0:width], qth[:, cs])
                if bias is not None:
                    s = s + bias[0:width, cs]
                p = jnp.exp(s - ls[:, cs])
                dp = mm(v2[0:width], doth[:, cs])
                ds = (p * (dp - dsum[:, cs])).astype(BF)
                dv = mm(p.astype(BF), doh[cs])
                dk = mm(ds, qh[cs])
                dq = mm(kt[hs, 0:width], ds)
                if h == 0 and b == 0:
                    dva[base : base + width, :] = dv
                    dka[base : base + width, :] = dk
                elif h == 0 and not whole:
                    dva[base : base + width - QB, :] += dv[: width - QB]
                    dka[base : base + width - QB, :] += dk[: width - QB]
                    dva[base + width - QB : base + width, :] = dv[width - QB :]
                    dka[base + width - QB : base + width, :] = dk[width - QB :]
                else:
                    dva[base : base + width, :] += dv
                    dka[base : base + width, :] += dk
                if at == 0:
                    dqt[hs, cs] = dq
                else:
                    dqt[hs, cs] += dq
    return sl


def back_far_body(ins, outs, scr, jobs):
    (
        info, go_in, w_in, q_in, o_in, lse_in, ks_in, vs_in, cos_in, sin_in, kf_in, vf_in, cosf_in, sinf_in,
    ) = ins
    do_ref, dqp_ref, dkf_ref, dvf_ref, dks_ref, dvs_ref, daf_ref = [x.ref for x in outs]
    mask1, mask2, hot, dqt, dka, dva, das = scr
    early = jobs[0]
    rest = jobs[1:]
    n, d = go_in.ref.shape
    pairs = d // 128
    for j in rest:
        j.advance()
    far_masks(info, mask1, mask2, hot)
    go_ref = go_in()
    w_ref = w_in()
    do_ref[...] = mm(go_ref[...], w_ref[:, 3 * d : 4 * d]).astype(BF)
    outs[0].flush()
    for j in rest:
        j.advance()
    wk = w_ref[:, d : 2 * d]
    wv = w_ref[:, 2 * d : 3 * d]

    def part(k_in, v_in, mask, whole, c_in, s_in, dk_ref, dv_ref, begin):
        q_ref, o_ref, lse_ref = q_in(), o_in(), lse_in()
        k_ref, v_ref = k_in(), v_in()
        cos, sin = c_in(), s_in()

        def pair(g, carry):
            segs = ((k_ref, v_ref, mask, None, whole, 0),)
            sl = back_pair(g, segs, q_ref, do_ref, o_ref, lse_ref, hot, dqt, dka, dva)
            if begin:
                dqp_ref[sl, :] = dqt[...]
            else:
                dqp_ref[sl, :] += dqt[...]
            dk_ref[:, sl] = turn(dka[...], cos[...], -sin[...]).astype(BF)
            dv_ref[:, sl] = dva[...].astype(BF)
            return carry

        return pair

    pair = part(ks_in, vs_in, mask2, False, cos_in, sin_in, dks_ref, dvs_ref, True)
    lax.fori_loop(0, pairs, pair, 0)
    das[...] = (mm(dks_ref[...], wk, NT) + mm(dvs_ref[...], wv, NT)).astype(BF)
    early.go(das)
    outs[4].flush()
    outs[5].flush()
    pair = part(kf_in, vf_in, mask1, True, cosf_in, sinf_in, dkf_ref, dvf_ref, False)
    lax.fori_loop(0, pairs // 3, pair, 0)
    for j in rest:
        j.advance()
    lax.fori_loop(pairs // 3, pairs, pair, 0)
    outs[1].flush()
    outs[2].flush()
    outs[3].flush()
    daf_ref[...] = (mm(dkf_ref[...], wk, NT) + mm(dvf_ref[...], wv, NT)).astype(BF)
    outs[6].flush()
    early.end(das)
    for j in rest:
        j.complete()


def back_far(info, go, o, lse, q, kf, vf, ks, vs, w, cosf, sinf, cos, sin, jobs, cid):
    n, d = go.shape
    sd = jax.ShapeDtypeStruct((n, d), BF)
    return run(
        back_far_body, "back_far",
        [info, go, w, q, o, lse, ks, vs, cos, sin, kf, vf, cosf, sinf], [smem()] + vmem(13),
        [sd, jax.ShapeDtypeStruct((d, n), F32)] + [sd] * 5, vmem(7),
        [
            pltpu.VMEM((n, 128), BF),
            pltpu.VMEM((n, 128), BF),
            pltpu.VMEM((128, n), BF),
            pltpu.VMEM((128, n), F32),
            pltpu.VMEM((n, 128), F32),
            pltpu.VMEM((n, 128), F32),
            pltpu.VMEM((n, d), BF),
        ],
        [Early((n, d))] + jobs, cid,
        10 * n * d * d + 70 * QB * QB * d * 4, 2 * (4 * d * d + 18 * n * d),
    )


def back_near_body(row, ins, outs, scr, jobs):
    (
        info, q_in, do_in, o_in, lse_in, ko_in, vo_in, dqp_in, cos_in, sin_in, go_in, af_in, dkf_in, dvf_in,
        as_in, dks_in, dvs_in, ao_in, w_in, x_in, gm_in, gain_in,
    ) = ins
    da_ref, db_ref, g_ref, dgain_ref = [x.ref for x in outs]
    bias, dqt, dka, dva, dq_s, dko_s, dvo_s, dao = scr
    back = jobs[0]
    rest = jobs[1:]
    n, d = do_in.ref.shape
    pairs = d // 128
    back.begin()
    for j in rest:
        j.advance()
    near_bias(info, bias)
    q_ref, do_ref, o_ref, lse_ref = q_in(), do_in(), o_in(), lse_in()
    ko_ref, vo_ref, dqp_ref, cos, sin = ko_in(), vo_in(), dqp_in(), cos_in(), sin_in()

    def pair(g, carry):
        segs = ((ko_ref, vo_ref, None, bias, False, 0),)
        sl = back_pair(g, segs, q_ref, do_ref, o_ref, lse_ref, None, dqt, dka, dva)
        dq = (dqt[...] + dqp_ref[sl, :]).T
        dq_s[:, sl] = turn(dq * SCALE, cos[...], -sin[...]).astype(BF)
        dko_s[:, sl] = turn(dka[...], cos[...], -sin[...]).astype(BF)
        dvo_s[:, sl] = dva[...].astype(BF)
        return carry

    lax.fori_loop(0, pairs // 2, pair, 0)
    for j in rest:
        j.advance()
    lax.fori_loop(pairs // 2, pairs, pair, 0)
    db_ref[:, d : 2 * d] = mm(go_in()[...].T, o_ref[...]).astype(BF)
    aot = ao_in()[...].T
    aft = af_in()[...].T
    ast = as_in()[...].T
    db_ref[:, 0:d] = (
        mm(aot, dvo_s[...]) + mm(aft, dvf_in()[...]) + mm(ast, dvs_in()[...])
    ).astype(BF)
    outs[1].flush()
    da_ref[:, 0:d] = mm(aot, dq_s[...]).astype(BF)
    da_ref[:, d : 2 * d] = (
        mm(aot, dko_s[...]) + mm(aft, dkf_in()[...]) + mm(ast, dks_in()[...])
    ).astype(BF)
    outs[0].flush()
    for j in rest:
        j.advance()
    w_ref = w_in()
    dao[...] = (
        mm(dko_s[...], w_ref[:, d : 2 * d], NT)
        + mm(dvo_s[...], w_ref[:, 2 * d : 3 * d], NT)
        + mm(dq_s[...], w_ref[:, 0:d], NT)
    )
    back.end(dao)
    dz, dgain = norm_back(x_in()[...].astype(F32), gain_in()[row : row + 1], dao[...])
    g_ref[...] = gm_in()[...] + dz
    dgain_ref[...] = dgain
    for j in rest:
        j.complete()


def back_near(row, ins, daf, got, jobs, cid):
    n, d = ins[1].shape
    wide = jax.ShapeDtypeStruct((d, 2 * d), BF)
    return run(
        functools.partial(back_near_body, row), "back_near",
        ins, [smem()] + vmem(len(ins) - 1),
        [wide, wide, jax.ShapeDtypeStruct((n, d), F32), jax.ShapeDtypeStruct((1, d), F32)], vmem(4),
        [
            pltpu.VMEM((n, n), F32),
            pltpu.VMEM((128, n), F32),
            pltpu.VMEM((n, 128), F32),
            pltpu.VMEM((n, 128), F32),
            pltpu.VMEM((n, d), BF),
            pltpu.VMEM((n, d), BF),
            pltpu.VMEM((n, d), BF),
            pltpu.VMEM((n, d), F32),
        ],
        [Return(daf, got)] + jobs, cid,
        22 * n * d * d + 30 * QB * QB * d * 4, 2 * (8 * d * d + 24 * n * d),
    )


def first_body(ins, outs, scr, jobs):
    x_in, gain_in = ins[0:2]
    narrow, (up, down) = ins[2:6], ins[6:8]
    layers, d = up.shape[0:2]
    pa0, ob, db, ot, dt, sem = scr
    rows = pa0.shape[1]
    pas = [pa0] + [x.ref for x in outs[1:layers]]
    pms = [x.ref for x in outs[layers:]]
    dp = lax.axis_index("dp")
    at_a = pl.ds(aligned(slot_of(dp, ORDERS[0]) * rows), rows)
    at_b = pl.ds(aligned(slot_of(dp, ORDERS[1]) * rows), rows)
    copies = []
    for l in range(layers):
        for i, (src, dst) in enumerate(
            [(x.at[l], ob.at[l, p]) for p, x in enumerate(narrow)]
            + [(down.at[l], db.at[l]), (up.at[l, at_a, :], pms[l].at[0])]
        ):
            copies.append(pltpu.make_async_copy(src, dst, sem.at[l * 6 + i]))
            copies[-1].start()

    def narrow_parts(l):
        for p in range(4):
            ot[p] = ob[l, p].T
            pas[l][p] = ot[p, at_a if p < 2 else at_b, :]

    for c in copies[0:4]:
        c.wait()
    narrow_parts(0)
    line = jobs[0]
    line.src = pa0
    line.advance()
    xh, _ = norm_stats(x_in()[...].astype(F32))
    outs[0].ref[...] = (xh * gain_in()[0:1]).astype(BF)
    outs[0].flush()
    line.advance()
    for c in copies[4:]:
        c.wait()
    for l in range(layers):
        dt[...] = db[l].T
        pms[l][1] = dt[at_b, :]
    line.advance()
    for l in range(1, layers):
        narrow_parts(l)
    line.complete()


def first(x, gain, weights, cid):
    n, d = x.shape
    q, up = weights[0], weights[4]
    layers, rows = q.shape[0], d >> BITS
    w, f = q.shape[1], up.shape[2]
    pa = jax.ShapeDtypeStruct((4, rows, w), BF)
    pm = jax.ShapeDtypeStruct((2, rows, d), BF)
    assert f == d
    return run(
        first_body, "first", [x, gain] + list(weights), vmem(2) + any_spec(6),
        [jax.ShapeDtypeStruct((n, d), BF)] + [pa] * (layers - 1) + [pm] * layers, vmem(2 * layers),
        [
            pltpu.VMEM((4, rows, w), BF),
            pltpu.VMEM((layers, 4, w, d), BF),
            pltpu.VMEM((layers, f, d), BF),
            pltpu.VMEM((4, d, w), BF),
            pltpu.VMEM((d, f), BF),
            dma(6 * layers),
        ],
        [Line(None, False, (4, rows, w))], cid, 10 * n * d, 4 * n * d,
    )


def layout_body(ins, outs, scr, jobs):
    count = len(ins) // 2
    for k in reversed(range(count)):
        ref = ins[count + k]()
        f = ref.shape[1] // 2
        outs[4].ref[k] = ref[:, 0:f].astype(F32)
        outs[5].ref[k] = ref[:, f : 2 * f].astype(F32).T
    outs[4].flush()
    outs[5].flush()
    for k in reversed(range(count)):
        v = ins[k]()[...].astype(F32)
        w = v.shape[1] // 4
        vt = v.T
        for i in range(4):
            outs[i].ref[k] = vt[i * w : i * w + w]
    for i in range(4):
        outs[i].flush()


def layout(att, mlps):
    layers = len(att)
    d = att[0].shape[0]
    w = att[0].shape[1] // 4
    f = mlps[0].shape[1] // 2
    shapes = [(layers, w, d)] * 4 + [(layers, d, f), (layers, f, d)]
    return run(
        layout_body, "layout", att + mlps, vmem(2 * layers),
        [jax.ShapeDtypeStruct(x, F32) for x in shapes], vmem(6), [], [], None, 1, 6 * layers * d * (4 * w + 2 * f),
    )[0]


def wide_of(every):
    return jnp.concatenate(
        [every[z, p] for p in range(every.shape[1]) for z in range(NZ)], axis=1
    )


def turning(n):
    position = np.arange(LMAX, dtype=np.float32)
    frequency = np.exp(
        (-math.log(10000.0) * np.arange(HD // 2, dtype=np.float32) / (HD // 2)).astype(np.float32)
    )
    angles = (position[:, None] * frequency[None, :]).astype(np.float32).astype(np.float64)
    cos = np.concatenate([np.cos(angles)] * 4, axis=1)
    sin = np.concatenate([-np.sin(angles), np.sin(angles)] * 2, axis=1)
    return [jnp.asarray(x.astype(np.float32).reshape(LMAX // n, n, 128)) for x in (cos, sin)]


def by_line(halves, counts):
    n = lax.axis_size("dp")
    cols = []
    for x, c in zip(halves, counts):
        for b in range(BITS, n.bit_length() - 1):
            x = x + lax.ppermute(x, "dp", [(i, i ^ (1 << b)) for i in range(n)])
        w = x.shape[1] // c
        for j in range(c):
            cols.append(x[:, j * w : (j + 1) * w].reshape(x.shape[0], NZ, w // NZ))
    return jnp.concatenate(cols, axis=2).transpose(1, 0, 2)


def on_device(
    tokens, lengths, noise_mask, cotangent, attn_gain, query_weight, key_weight, value_weight,
    out_weight, mlp_gain, up_weight, down_weight,
):
    n, d = tokens.shape
    info = lengths
    cos_t, sin_t = turning(n)
    cosf, sinf, cos, sin = (cos_t, 0), (sin_t, 0), (cos_t, 1), (sin_t, 1)

    res, ((every,),) = first(
        tokens, attn_gain,
        [x.transpose(0, 2, 1) for x in (query_weight, key_weight, value_weight)]
        + [out_weight, up_weight, down_weight],
        0,
    )
    a = res[0]
    pa = [None] + list(res[1:LAYERS])
    pm = res[LAYERS:]
    ((wa,), (wide,)) = transfer("gather_first", [Gather(wide_of(every)), Line(pm[0], True)], 1)
    was, wms, saved = [], [], []
    x = tokens
    for l in range(LAYERS):
        more = l + 1 < LAYERS
        jobs = [Gather(wide)] + ([Line(pa[l + 1], False)] if more else [])
        res, extra = attend(
            info, x, a, wa, cosf, sinf, cos, sin, mlp_gain, l, jobs, 10 + l
        )
        q, ko, vo, kf, vf, ks, vs, o, lse, xm, m = res
        af, as_ = extra[0]
        wm = extra[1][0]
        was.append(wa)
        wms.append(wm)
        jobs = []
        if more:
            piece = wide_of(extra[2][0])
            jobs = [Gather(piece), Line(pm[l + 1], True)]
        nxt = min(l + 1, LAYERS - 1)
        (x_next, a_next, u), extra = mlp(xm, m, wm, attn_gain, nxt, jobs, 20 + l)
        if more:
            wa, wide = extra[0][0], extra[1][0]
        saved.append((x, a, af, as_, q, kf, vf, ks, vs, ko, vo, o, lse, xm, m, u))
        x, a = x_next, a_next
    block_out = x

    g = cotangent
    top = [noise_mask, info]
    gains = [None] * (2 * LAYERS)
    att = [None] * LAYERS
    mlps = [None] * LAYERS
    att_grads = mlp_parts = None

    def joined(parts):
        return [jnp.concatenate([p[i] for p in parts], axis=1) for i in (0, 1)]

    for l in reversed(range(LAYERS)):
        x, a, af, as_, q, kf, vf, ks, vs, ko, vo, o, lse, xm, m, u = saved[l]
        above = l + 1 < LAYERS
        jobs = []
        if above:
            jobs = [Reduce(*att_grads), LineSum(by_line(joined(mlp_parts), (1, 1)))]
        res, extra = mlp_back(g, xm, m, u, wms[l], mlp_gain, l, top, jobs, 30 + l)
        top = []
        gm, go, dup, ddn, gains[LAYERS + l] = res
        jobs = [Reduce(dup, ddn, 0, 2)]
        if above:
            jobs += [LineSum(by_line(extra[0], (2, 2))), Gather(extra[1][0])]
        res, extra = back_far(
            info, go, o, lse, q, kf, vf, ks, vs, was[l], cosf, sinf, cos, sin, jobs, 40 + l
        )
        do, dqp, dkf, dvf, dks, dvs, daf = res
        got = extra[0][0]
        mlp_parts = [extra[1]]
        jobs = [Reduce(dup, ddn, 1, 2)]
        if above:
            mlps[l + 1] = extra[3][0]
            jobs.append(Gather(extra[2][0]))
        res, extra = back_near(
            l,
            [
                info, q, do, o, lse, ko, vo, dqp, cos, sin, go, af, dkf, dvf, as_, dks, dvs, a, was[l],
                x, gm, attn_gain,
            ],
            daf, got, jobs, 50 + l,
        )
        mlp_parts.append(extra[1])
        if above:
            att[l + 1] = extra[2][0]
        att_grads = res[0:2]
        g, gains[l] = res[2:4]

    gain_rows = jnp.concatenate(gains, axis=0)
    (sums, (gain_rows,), (mlp_sum,)) = transfer(
        "reduce_last",
        [Reduce(*att_grads), PlaneSum(gain_rows), LineSum(by_line(joined(mlp_parts), (1, 1)))],
        2,
    )
    for b in range(BITS, lax.axis_size("dp").bit_length() - 1):
        size = lax.axis_size("dp")
        gain_rows = gain_rows + lax.ppermute(
            gain_rows, "dp", [(i, i ^ (1 << b)) for i in range(size)]
        )
    (part,), (gain_sums,), (mlps[0],) = transfer(
        "line_last",
        [
            LineSum(by_line(sums, (2, 2))),
            LineSum(jnp.broadcast_to(gain_rows, (NZ,) + gain_rows.shape)),
            Gather(mlp_sum),
        ],
        3,
    )
    ((att[0],),) = transfer("gather_last", [Gather(part)], 4)
    grads = layout(att, mlps)
    return (
        block_out, g, gain_sums[:LAYERS], *[x.transpose(0, 2, 1) for x in grads[:3]], grads[3],
        gain_sums[LAYERS:], grads[4], grads[5],
    )


def solution(mesh):
    rows = P(("dp", "tensor"), None)
    cols = P(None, None, "tensor")
    mids = P(None, "tensor", None)
    return jax.shard_map(
        on_device,
        mesh=mesh,
        in_specs=(
            rows, P("dp"), P("dp", None), rows, P(), cols, cols, cols, mids, P(), cols, mids,
        ),
        out_specs=(rows, rows, P(), cols, cols, cols, mids, P(), cols, mids),
        check_vma=False,
    )
```

```python
import functools
import math

import jax
import jax.numpy as jnp
import numpy as np
from jax import lax
from jax.experimental import pallas as pl
from jax.experimental.pallas import tpu as pltpu
from jax.sharding import PartitionSpec as P

HD = 64
BLK = 16
LMAX = 1024
LAYERS = 2
EPS = 1e-05
NEG = -1e30
SCALE = 1.0 / math.sqrt(HD)
GC = math.sqrt(2.0 / math.pi)
GA = 0.044715
F32 = jnp.float32
BF = jnp.bfloat16
QB = 256
VMEM_LIMIT = 56 << 20

NN = (((1,), (0,)), ((), ()))
NT = (((1,), (1,)), ((), ()))
TN = (((0,), (0,)), ((), ()))


def mm(a, b, dims=NN):
    return lax.dot_general(a, b, dims, preferred_element_type=F32)


def norm_stats(x):
    mean = jnp.mean(x, axis=-1, keepdims=True)
    c = x - mean
    var = jnp.mean(c * c, axis=-1, keepdims=True)
    r = lax.rsqrt(var + EPS)
    return c * r, r


def norm_back(x, gain, dy):
    xh, r = norm_stats(x)
    gy = dy * gain
    m1 = jnp.mean(gy, axis=-1, keepdims=True)
    m2 = jnp.mean(gy * xh, axis=-1, keepdims=True)
    dz = r * (gy - m1 - xh * m2)
    return dz, jnp.sum(dy * xh, axis=0, keepdims=True)


def turn(y, cos, sin):
    lane = lax.broadcasted_iota(jnp.int32, y.shape, 1) % HD
    other = jnp.where(
        lane < HD // 2, pltpu.roll(y, 128 - HD // 2, 1), pltpu.roll(y, HD // 2, 1)
    )
    return y * cos + other * sin


def vmem(n):
    return [pl.BlockSpec(memory_space=pltpu.VMEM)] * n


def smem():
    return pl.BlockSpec(memory_space=pltpu.SMEM)


def params(**kw):
    return pltpu.CompilerParams(vmem_limit_bytes=VMEM_LIMIT, **kw)


def cost(flops, nbytes, trans=0):
    return pl.CostEstimate(flops=int(flops), bytes_accessed=int(nbytes), transcendentals=int(trans))


MESH = pl.DeviceIdType.MESH
BITS = 3
ORDERS = ((0, 1, 2), (0, 2, 1))
NZ = 4


def bit_of(dp, b):
    return dp // (1 << b) % 2


def slot_of(dp, order):
    out = 0
    for b in order:
        out = out * 2 + bit_of(dp, b)
    return out


def partner(dp, b):
    return dp + (1 - 2 * bit_of(dp, b)) * (1 << b)


def greet(plane, line):
    dp = lax.axis_index("dp")
    t = lax.axis_index("tensor")
    barrier = pltpu.get_barrier_semaphore()
    if plane:
        for b in range(BITS):
            pl.semaphore_signal(barrier, inc=1, device_id=(partner(dp, b), t), device_id_type=MESH)
    if line:
        for s in range(1, NZ):
            pl.semaphore_signal(barrier, inc=1, device_id=(dp, (t + s) % NZ), device_id_type=MESH)
    pl.semaphore_wait(barrier, BITS * plane + (NZ - 1) * line)


def remote(src, dst, send, recv, dp, t):
    return pltpu.make_async_remote_copy(
        src_ref=src, dst_ref=dst, send_sem=send, recv_sem=recv, device_id=(dp, t), device_id_type=MESH
    )


def aligned(x, n=16):
    return pl.multiple_of(x, n)


def dma(n):
    return pltpu.SemaphoreType.DMA((n,))


def any_spec(n=1):
    return [pl.BlockSpec(memory_space=pl.ANY)] * n


class Job:
    plane = line = 0
    steps = BITS

    def bind(self, ins, outs, scr):
        self.at = 0
        self.i, self.o, self.s = ins, outs, scr
        self.dp = lax.axis_index("dp")
        self.t = lax.axis_index("tensor")

    def wait(self, s):
        pass

    def advance(self):
        if self.at < self.steps:
            if self.at > 0:
                self.wait(self.at - 1)
            self.start(self.at)
            self.at += 1

    def complete(self):
        while self.at < self.steps:
            self.advance()
        if self.steps:
            self.wait(self.steps - 1)


class Gather(Job):
    plane = 1

    def __init__(self, piece, shape=None):
        self.rows, n = shape if piece is None else piece.shape
        self.half = n // 2
        self.src = None
        self.ins, self.in_specs = ([], []) if piece is None else ([piece], vmem(1))
        self.outs, self.out_specs = [jax.ShapeDtypeStruct((self.rows << BITS, n), BF)], any_spec()
        self.scratch = [dma(2 * BITS), dma(2 * BITS), dma(2)]

    def cols(self, i):
        return pl.ds(i * self.half, self.half)

    def source(self):
        return self.i[0] if self.src is None else self.src

    def own(self, i):
        at = slot_of(self.dp, ORDERS[i]) * self.rows
        return pltpu.make_async_copy(
            self.source().at[:, self.cols(i)],
            self.o[0].at[pl.ds(aligned(at), self.rows), self.cols(i)],
            self.s[2].at[i],
        )

    def copy(self, s, i):
        b = ORDERS[i][BITS - 1 - s]
        size = self.rows << s
        at = slot_of(self.dp, ORDERS[i]) // (1 << s) * size
        there = self.o[0].at[pl.ds(aligned(at), size), self.cols(i)]
        return remote(
            self.source().at[:, self.cols(i)] if s == 0 else there, there,
            self.s[0].at[2 * s + i], self.s[1].at[2 * s + i], partner(self.dp, b), self.t,
        )

    def start(self, s):
        for i in range(2):
            self.copy(s, i).start()
            if s == 0:
                self.own(i).start()

    def wait(self, s):
        for i in range(2):
            self.copy(s, i).wait()
            if s == 0:
                self.own(i).wait()


class Reduce(Job):
    plane = 1

    def __init__(self, a, b, part=0, parts=1):
        self.full = a.shape[0]
        widths = (a.shape[1] // parts, b.shape[1] // parts)
        self.cols = [pl.ds(part * w, w) for w in widths]
        self.ins, self.in_specs = [a, b], any_spec(2)
        self.outs = [jax.ShapeDtypeStruct((self.full >> BITS, w), BF) for w in widths]
        self.out_specs = vmem(2)
        self.scratch = [pltpu.VMEM((self.full // 2, w), BF) for w in widths]
        for w in widths:
            self.scratch += [pltpu.VMEM((self.full >> (s + 1), w), BF) for s in range(BITS)]
        self.scratch += [dma(2 * BITS), dma(2 * BITS), dma(2)]

    def got(self, s, i):
        return self.s[2 + i * BITS + s]

    def offset(self, s, i):
        at = 0
        for j in range(1, s):
            at = at + bit_of(self.dp, ORDERS[i][j]) * (self.full >> (j + 1))
        return at

    def copy(self, s, i):
        b = ORDERS[i][s]
        size = self.full >> (s + 1)
        at = (1 - bit_of(self.dp, b)) * size
        if s == 0:
            there = self.i[i].at[pl.ds(aligned(at), size), self.cols[i]]
        else:
            there = self.s[i].at[pl.ds(aligned(self.offset(s, i) + at), size), :]
        send, recv = self.s[2 + 2 * BITS], self.s[3 + 2 * BITS]
        return remote(
            there, self.got(s, i), send.at[2 * s + i], recv.at[2 * s + i], partner(self.dp, b), self.t
        )

    def own(self, i):
        size = self.full // 2
        at = bit_of(self.dp, ORDERS[i][0]) * size
        return pltpu.make_async_copy(
            self.i[i].at[pl.ds(aligned(at), size), self.cols[i]], self.s[i], self.s[4 + 2 * BITS].at[i]
        )

    def start(self, s):
        for i in range(2):
            self.copy(s, i).start()
            if s == 0:
                self.own(i).start()

    def wait(self, s):
        for i in range(2):
            self.copy(s, i).wait()
            if s == 0:
                self.own(i).wait()
            size = self.full >> (s + 1)
            base = self.offset(s + 1, i)
            keep, got, out = self.s[i], self.got(s, i), self.o[i]
            last = s == BITS - 1
            step = 48 if size % 48 == 0 else size

            def add(j, carry):
                rows = pl.ds(aligned(base + j * step), step)
                here = pl.ds(aligned(j * step), step)
                total = (keep[rows, :].astype(F32) + got[here, :].astype(F32)).astype(BF)
                if last:
                    out[here, :] = total
                else:
                    keep[rows, :] = total
                return carry

            lax.fori_loop(0, size // step, add, 0)


class Line(Job):
    line = 1
    steps = NZ - 1

    def __init__(self, parts, wide, shape=None):
        self.count, self.rows, self.w = shape if parts is None else parts.shape
        self.wide = wide
        self.src = None
        self.ins, self.in_specs = ([], []) if parts is None else ([parts], vmem(1))
        if wide:
            shape = (self.rows, self.count * NZ * self.w)
        else:
            shape = (NZ, self.count, self.rows, self.w)
        self.outs, self.out_specs = [jax.ShapeDtypeStruct(shape, BF)], any_spec()
        m = self.count * 2 * self.steps
        self.scratch = [dma(m), dma(m), dma(self.count)]

    def place(self, p, z):
        if self.wide:
            at = (p * NZ + z) * self.w
            return self.o[0].at[:, pl.ds(aligned(at, 128), self.w)]
        return self.o[0].at[z, p]

    def copy(self, s, p, way):
        z = (self.t - way * s) % NZ
        k = (s * 2 + (way > 0)) * self.count + p
        there = self.place(p, z)
        return remote(
            self.source().at[p] if s == 0 else there, there, self.s[0].at[k], self.s[1].at[k],
            self.dp, (self.t + way) % NZ,
        )

    def source(self):
        return self.i[0] if self.src is None else self.src

    def inside(self, s, way, receiver):
        t = self.t
        if receiver:
            return (t - way * (s + 1) >= 0) & (t - way * (s + 1) < NZ)
        return (t - way * s >= 0) & (t - way * s < NZ) & (t + way >= 0) & (t + way < NZ)

    def own(self, p):
        return pltpu.make_async_copy(self.source().at[p], self.place(p, self.t), self.s[2].at[p])

    def start(self, s):
        for way in (1, -1):

            @pl.when(self.inside(s, way, False))
            def _(way=way):
                for p in range(self.count):
                    self.copy(s, p, way).start()

        if s == 0:
            for p in range(self.count):
                self.own(p).start()

    def wait(self, s):
        for way in (1, -1):

            @pl.when(self.inside(s, way, True))
            def _(way=way):
                for p in range(self.count):
                    self.copy(s, p, way).wait_recv()

            @pl.when(self.inside(s, way, False))
            def _(way=way):
                for p in range(self.count):
                    self.copy(s, p, way).wait_send()

        if s == 0:
            for p in range(self.count):
                self.own(p).wait()


class LineSum(Job):
    line = 1
    steps = 1

    def __init__(self, parts, shape=None, kind=BF, same=False):
        shape = parts.shape[1:] if shape is None else shape
        self.same = same
        self.src = self.dst = None
        self.outs = self.out_specs = []
        self.ins, self.in_specs = ([], []) if parts is None else ([parts], vmem(1))
        if parts is not None:
            kind = parts.dtype
            self.outs, self.out_specs = [jax.ShapeDtypeStruct(shape, kind)], vmem(1)
        self.scratch = [pltpu.VMEM((NZ - 1,) + tuple(shape), kind), dma(3), dma(3)]

    def source(self, z):
        ref = self.i[0] if self.src is None else self.src
        return ref if self.same else ref.at[z]

    def copies(self):
        for s in (1, 2, 3):
            z = (self.t + s) % NZ
            yield remote(
                self.source(z), self.s[0].at[s - 1], self.s[1].at[s - 1], self.s[2].at[s - 1],
                self.dp, z,
            )

    def start(self, s):
        for c in self.copies():
            c.start()

    def wait(self, s):
        for c in self.copies():
            c.wait()
        got = self.s[0]
        total = self.source(self.t)[...].astype(F32)
        for k in range(NZ - 1):
            total = total + got[k].astype(F32)
        out = self.o[0] if self.dst is None else self.dst
        out[...] = total.astype(out.dtype)


class LineSumWide(Job):
    line = 1
    steps = 1

    def __init__(self, arrays):
        self.w = arrays[0].shape[1] // 2
        self.ins, self.in_specs = list(arrays), vmem(4)
        shape = arrays[0].shape
        self.outs, self.out_specs = [jax.ShapeDtypeStruct(shape, BF)], vmem(1)
        self.scratch = [pltpu.VMEM((NZ - 1,) + shape, BF), dma(6), dma(6)]

    def part(self, kind, half, z):
        return self.i[2 * kind + half].at[:, pl.ds(aligned(z % 2 * self.w, 128), self.w)]

    def copy(self, s, kind, half):
        z = (self.t + s) % NZ
        k = (s - 1) * 2 + kind
        return remote(
            self.part(kind, half, z), self.s[0].at[s - 1, :, pl.ds(kind * self.w, self.w)],
            self.s[1].at[k], self.s[2].at[k], self.dp, z,
        )

    def start(self, step):
        for s in (1, 2, 3):
            for half in (0, 1):

                @pl.when((self.t + s) % NZ // 2 == half)
                def _(s=s, half=half):
                    for kind in (0, 1):
                        self.copy(s, kind, half).start()

    def wait(self, step):
        for s in (1, 2, 3):
            for kind in (0, 1):
                self.copy(s, kind, 0).wait()
        got, out = self.s[0], self.o[0]
        for half in (0, 1):

            @pl.when(self.t // 2 == half)
            def _(half=half):
                for kind in (0, 1):
                    at = slice(kind * self.w, (kind + 1) * self.w)
                    total = self.part(kind, half, self.t)[...].astype(F32)
                    for k in range(NZ - 1):
                        total = total + got[k, :, at].astype(F32)
                    out[:, at] = total.astype(BF)


class PlaneSum(Job):
    plane = 1

    def __init__(self, x):
        self.ins, self.in_specs = [x], vmem(1)
        self.outs, self.out_specs = [jax.ShapeDtypeStruct(x.shape, F32)], vmem(1)
        self.scratch = [pltpu.VMEM((BITS,) + x.shape, F32), dma(BITS), dma(BITS)]

    def copy(self, s):
        return remote(
            self.i[0] if s == 0 else self.o[0], self.s[0].at[s], self.s[1].at[s], self.s[2].at[s],
            partner(self.dp, s), self.t,
        )

    def start(self, s):
        self.copy(s).start()

    def wait(self, s):
        self.copy(s).wait()
        self.o[0][...] = (self.i[0] if s == 0 else self.o[0])[...] + self.s[0][s]


class Spread(Job):
    line = 1
    steps = 0

    def __init__(self, a):
        self.ins, self.in_specs = [a], any_spec()
        self.outs, self.out_specs = [jax.ShapeDtypeStruct(a.shape, BF)] * 2, any_spec(2)
        self.scratch = [pltpu.VMEM(a.shape, BF), pltpu.VMEM(a.shape, BF), dma(2), dma(2), dma(2)]

    def put(self, src, which, to, k):
        return remote(src, self.s[which], self.s[2].at[k], self.s[3].at[which], self.dp, to)

    def save(self, which):
        return pltpu.make_async_copy(self.s[which], self.o[which], self.s[4].at[which])

    def begin(self):
        a, t = self.i[0], self.t

        @pl.when(t == 2)
        def _():
            self.put(a, 0, 1, 0).start()
            self.put(a, 0, 3, 1).start()

        @pl.when(t % 2 == 0)
        def _():
            self.s[0][...] = jnp.zeros_like(self.s[0])

        @pl.when(t >= 2)
        def _():
            self.s[1][...] = jnp.zeros_like(self.s[1])

    def first(self):
        a, t = self.i[0], self.t

        @pl.when(t % 2 == 1)
        def _():
            self.put(a, 0, 1, 0).wait_recv()

        @pl.when(t == 1)
        def _():
            self.put(self.s[0], 1, 0, 0).start()

        @pl.when(t == 3)
        def _():
            self.put(a, 1, 1, 0).start()

        self.save(0).start()

    def second(self):
        @pl.when(self.t < 2)
        def _():
            self.put(self.i[0], 1, 1, 0).wait_recv()

        self.save(1).start()

    def end(self):
        a, t = self.i[0], self.t

        @pl.when(t >= 1)
        def _():
            self.put(a, 0, 1, 0).wait_send()

        @pl.when(t == 2)
        def _():
            self.put(a, 0, 3, 1).wait_send()

        self.save(0).wait()
        self.save(1).wait()


class Early(Job):
    line = 1
    steps = 0

    def __init__(self, shape):
        self.ins, self.in_specs = [], []
        self.outs, self.out_specs = [jax.ShapeDtypeStruct(shape, BF)], any_spec()
        self.scratch = [dma(1), dma(1)]

    def put(self, src, to):
        return remote(src, self.o[0], self.s[0].at[0], self.s[1].at[0], self.dp, to)

    def go(self, das):
        @pl.when(self.t < 2)
        def _():
            self.put(das, 2 * self.t + 1).start()

    def end(self, das):
        @pl.when(self.t < 2)
        def _():
            self.put(das, 1).wait_send()

        @pl.when(self.t % 2 == 1)
        def _():
            self.put(das, 1).wait_recv()


class Return(Job):
    line = 1
    steps = 0

    def __init__(self, daf, got):
        self.ins, self.in_specs = [daf, got], vmem(2)
        self.outs, self.out_specs = [], []
        sd = pltpu.VMEM(daf.shape, BF)
        self.scratch = [sd, sd, sd, dma(1), dma(2)]

    def put(self, src, which):
        return remote(src, self.s[which], self.s[3].at[0], self.s[4].at[which], self.dp, 2)

    def begin(self):
        daf, got = self.i

        @pl.when(self.t == 1)
        def _():
            self.s[2][...] = (daf[...].astype(F32) + got[...].astype(F32)).astype(BF)
            self.put(self.s[2], 0).start()

        @pl.when(self.t == 3)
        def _():
            self.put(daf, 1).start()

    def end(self, acc):
        daf, got = self.i

        @pl.when(self.t == 2)
        def _():
            self.put(daf, 0).wait_recv()
            self.put(daf, 1).wait_recv()
            acc[...] += self.s[0][...].astype(F32) + self.s[1][...].astype(F32)

        @pl.when(self.t == 3)
        def _():
            acc[...] += got[...].astype(F32)

        @pl.when(self.t % 2 == 1)
        def _():
            self.put(daf, 0).wait_send()


def at_points(j, points):
    return points.get(type(j).__name__, (0,) * j.steps)


def steps_at(jobs, point, points):
    for j in jobs:
        for s in range(j.steps):
            if at_points(j, points)[s] == point:
                if s > 0:
                    j.wait(s - 1)
                j.start(s)


def finish(jobs, points):
    steps_at(jobs, -1, points)
    for j in jobs:
        if j.steps:
            j.wait(j.steps - 1)


class In:
    def __init__(self, hbm, ref, sem):
        self.ref = ref
        self.copy = pltpu.make_async_copy(hbm, ref, sem)
        self.copy.start()

    def __call__(self):
        if self.copy is not None:
            self.copy.wait()
            self.copy = None
        return self.ref


class Out:
    def __init__(self, hbm, ref, sem):
        self.ref = ref
        self.copy = pltpu.make_async_copy(ref, hbm, sem)
        self.sent = False

    def flush(self):
        if not self.sent:
            self.copy.start()
            self.sent = True


def meet(jobs):
    greet(max(j.plane for j in jobs), max(j.line for j in jobs))


def lazily(body, ins, in_specs, outs, out_specs, scratch):
    lazy = [sp.memory_space == pltpu.VMEM for sp in in_specs]
    picks = [x[1] if isinstance(x, tuple) else None for x in ins]
    ins = [x[0] if isinstance(x, tuple) else x for x in ins]
    bufs = [
        pltpu.VMEM(x.shape if p is None else x.shape[1:], x.dtype)
        for x, z, p in zip(ins, lazy, picks)
        if z
    ]
    bufs += [pltpu.VMEM(x.shape, x.dtype) for x in outs]
    own = len(scratch)
    count = sum(lazy)

    def wrapped(i, o, s, jobs):
        mine, rest = s[:own], s[own:]
        vm, sin, sout = rest[:-2], rest[-2], rest[-1]
        given = []
        k = 0
        for ref, z, p in zip(i, lazy, picks):
            if z:
                if p is not None:
                    ref = ref.at[lax.axis_index("tensor") % 2 if p else 0]
                given.append(In(ref, vm[k], sin.at[k]))
                k += 1
            else:
                given.append(ref)
        results = [Out(ref, vm[count + k], sout.at[k]) for k, ref in enumerate(o)]
        if jobs:
            meet(jobs)
        body(given, results, mine, jobs)
        for x, z in zip(given, lazy):
            if z:
                x()
        for x in results:
            x.flush()
        for x in results:
            x.copy.wait()

    specs = [any_spec()[0] if z else sp for sp, z in zip(in_specs, lazy)]
    return wrapped, ins, specs, any_spec(len(outs)), list(scratch) + bufs + [dma(count), dma(len(outs))]


def run(body, name, ins, in_specs, outs, out_specs, scratch, jobs, cid, flops, nbytes, grid=None):
    late = grid is None and len(ins) > 0
    if late:
        body, ins, in_specs, out_specs, scratch = lazily(body, ins, in_specs, outs, out_specs, scratch)
    cuts = []
    for what in ("ins", "outs", "scratch"):
        own = {"ins": ins, "outs": outs, "scratch": scratch}[what]
        cuts.append([len(own)] + [len(getattr(j, what)) for j in jobs])

    def kernel(*refs):
        at = 0
        groups = []
        for cut in cuts:
            g = []
            for c in cut:
                g.append(refs[at : at + c])
                at += c
            groups.append(g)
        for k, j in enumerate(jobs):
            j.bind(groups[0][k + 1], groups[1][k + 1], groups[2][k + 1])
        if jobs and not late:
            if grid is None:
                meet(jobs)
            else:
                pl.when(pl.program_id(0) == 0)(functools.partial(meet, jobs))
        body(groups[0][0], groups[1][0], groups[2][0], jobs)

    for j in jobs:
        ins, in_specs = list(ins) + j.ins, list(in_specs) + j.in_specs
        outs, out_specs = list(outs) + j.outs, list(out_specs) + j.out_specs
        scratch = list(scratch) + j.scratch
    res = pl.pallas_call(
        kernel,
        out_shape=tuple(outs),
        in_specs=list(in_specs),
        out_specs=tuple(out_specs),
        scratch_shapes=list(scratch),
        compiler_params=params(collective_id=cid, has_side_effects=True) if jobs else params(),
        cost_estimate=cost(flops, nbytes),
        name=name,
        **({} if grid is None else {"grid": grid}),
    )(*ins)
    at = cuts[1][0]
    extra = []
    for c in cuts[1][1:]:
        extra.append(res[at : at + c])
        at += c
    return res[: cuts[1][0]], extra


def only_jobs(ins, outs, scr, jobs):
    for s in range(max(j.steps for j in jobs)):
        for j in jobs:
            j.advance()
    for j in jobs:
        j.complete()


def transfer(name, jobs, cid):
    return run(only_jobs, name, [], [], [], [], [], jobs, cid, 1, 1 << 24)[1]


def turned(out, tmp, cos, sin):
    for g in range(out.shape[1] // 128):
        sl = slice(g * 128, g * 128 + 128)
        out[:, sl] = turn(tmp[:, sl], cos[...], sin[...]).astype(BF)


def near_bias(info, bias):
    n = bias.shape[0]
    length = info[0]
    t = lax.axis_index("tensor")
    noisy = t < 2
    base = t % 2 * n
    j = lax.broadcasted_iota(jnp.int32, (n, n), 0)
    i = lax.broadcasted_iota(jnp.int32, (n, n), 1)
    bi = i // BLK
    bj = j // BLK
    low = jnp.where(noisy, bi, 0)
    seen = (bj <= bi) & (bj >= low) & (j + base < length)
    bias[...] = jnp.where(seen | (i == j), 0.0, NEG)


def far_masks(info, first, second, hot):
    n = hot.shape[1]
    length = info[0]
    t = lax.axis_index("tensor")
    noisy = t < 2
    odd = t % 2
    key = lax.broadcasted_iota(jnp.int32, (n, 128), 0)
    block = lax.broadcasted_iota(jnp.int32, (n, 128), 1) % HD
    real = block < n // BLK
    odd_lim = jnp.where(odd == 1, length, 0)
    lim = jnp.where(noisy, length - odd * n, 0)
    first[...] = jnp.where(real & (key >= odd_lim), NEG, 0.0).astype(BF)
    hidden = (key // BLK >= block) | (key >= lim)
    second[...] = jnp.where(real & hidden, NEG, 0.0).astype(BF)
    row = lax.broadcasted_iota(jnp.int32, (128, n), 0) % HD
    query = lax.broadcasted_iota(jnp.int32, (128, n), 1)
    hot[...] = jnp.where(query // BLK == row, 1.0, 0.0).astype(BF)


def half_of(h, shape, axis):
    at = lax.broadcasted_iota(jnp.int32, shape, axis)
    return (at < HD) if h == 0 else (at >= HD)


def attend_body(row, ins, outs, scr, jobs):
    info, a_in, w_in, cos_in, sin_in, cosf_in, sinf_in, x_in, gain_in = ins
    q_ref, ko_ref, vo_ref, kf_ref, vf_ref, ks_ref, vs_ref, o_ref, lse_ref, xm_ref, m_ref = [
        x.ref for x in outs
    ]
    tmp, bias, mask1, mask2, hot, acc, top, tot = scr
    spread = jobs[0]
    rest = jobs[1:]
    af_ref, as_ref = spread.s[0:2]
    n, d = x_in.ref.shape
    pairs = d // 128
    gather = rest[0]
    line = rest[1:]
    spread.begin()
    gather.advance()
    near_bias(info, bias)
    far_masks(info, mask1, mask2, hot)
    a_ref = a_in()
    w_ref = w_in()
    cos = cos_in()
    sin = sin_in()

    tmp[...] = mm(a_ref[...], w_ref[:, 0:d]) * SCALE
    turned(q_ref, tmp, cos, sin)

    def keys_of(src, kk, vv, c, s):
        av = src[...]
        tmp[...] = mm(av, w_ref[:, d : 2 * d])
        turned(kk, tmp, c, s)
        vv[...] = mm(av, w_ref[:, 2 * d : 3 * d]).astype(BF)

    keys_of(a_ref, ko_ref, vo_ref, cos, sin)
    for k in range(3):
        outs[k].flush()

    def segment(kk, vv, mask, full, first, last):
        def pair(g, carry):
            sl = pl.ds(aligned(g * 128, 128), 128)
            qt = q_ref[:, sl].T
            k2 = kk[:, sl]
            vt = vv[:, sl].T
            other_q = jnp.zeros_like(qt) if mask is None else hot[...]
            other_k = k2 if mask is None else mask[...]
            rows = pl.ds(aligned(g * 128, 128), 128)
            if not first:
                olds = top[g]
                tots = tot[g]
                before = acc[rows, :]
            tops, sums, outs = [], [], []
            chains = [(h, b) for h in range(2) for b in range(n // QB)]
            scores = []
            for h, b in chains:
                qh = jnp.where(half_of(h, qt.shape, 0), qt, other_q)
                kh = jnp.where(half_of(h, k2.shape, 1), k2, other_k)
                width = n if full else (b + 1) * QB
                scores.append(mm(kh[0:width], qh[:, b * QB : b * QB + QB]))
            for (h, b), s in zip(chains, scores):
                cs = slice(b * QB, b * QB + QB)
                width = s.shape[0]
                if mask is None:
                    s = s + bias[0:width, cs]
                mx = jnp.max(s, axis=0, keepdims=True)
                if not first:
                    old = olds[h : h + 1, cs]
                    mx = jnp.maximum(mx, old)
                    scale = jnp.exp(old - mx)
                e = jnp.exp(s - mx)
                total = jnp.sum(e, axis=0, keepdims=True)
                out = mm(vt[h * HD : h * HD + HD, 0:width], e.astype(BF))
                if not first:
                    total = total + tots[h : h + 1, cs] * scale
                    out = out + before[h * HD : h * HD + HD, cs] * scale
                if last:
                    mx = mx + jnp.log(total)
                    out = out / total
                tops.append(mx)
                sums.append(total)
                outs.append(out)
            for (h, b), mx, total, out in zip(chains, tops, sums, outs):
                cs = slice(b * QB, b * QB + QB)
                if last:
                    lse_ref[g, h : h + 1, cs] = mx
                else:
                    top[g, h : h + 1, cs] = mx
                    tot[g, h : h + 1, cs] = total
                    acc[pl.ds(aligned(g * 128 + h * HD, HD), HD), cs] = out
            if last:
                ot = jnp.concatenate(
                    [jnp.concatenate(outs[i : i + n // QB], axis=1) for i in (0, n // QB)], axis=0
                )
                o_ref[:, sl] = ot.T.astype(BF)
            return carry

        return pair

    lax.fori_loop(0, pairs, segment(ko_ref, vo_ref, None, False, True, False), 0)
    gather.advance()
    spread.first()
    keys_of(af_ref, kf_ref, vf_ref, cosf_in(), sinf_in())
    outs[3].flush()
    outs[4].flush()
    lax.fori_loop(0, pairs, segment(kf_ref, vf_ref, mask1, True, False, False), 0)
    spread.second()
    for j in line:
        j.advance()
    keys_of(as_ref, ks_ref, vs_ref, cos, sin)
    outs[5].flush()
    outs[6].flush()
    last = segment(ks_ref, vs_ref, mask2, False, False, True)
    lax.fori_loop(0, pairs // 2, last, 0)
    gather.advance()
    for j in line:
        j.advance()
    lax.fori_loop(pairs // 2, pairs, last, 0)
    for j in line:
        j.advance()
    outs[7].flush()
    outs[8].flush()
    xm = x_in()[...].astype(F32) + mm(o_ref[...], w_ref[:, 3 * d : 4 * d], NT)
    xm_ref[...] = xm
    outs[9].flush()
    xh, _ = norm_stats(xm)
    m_ref[...] = (xh * gain_in()[row : row + 1]).astype(BF)
    outs[10].flush()
    spread.end()
    gather.complete()
    for j in line:
        j.complete()


def attend(info, x, a, w, cosf, sinf, cos, sin, gain, row, jobs, cid):
    n, d = x.shape
    sd = jax.ShapeDtypeStruct((n, d), BF)
    heads = (d // 128, 8, n)
    return run(
        functools.partial(attend_body, row), "attend",
        [info, a, w, cos, sin, cosf, sinf, x, gain], [smem()] + vmem(8),
        [sd] * 8 + [jax.ShapeDtypeStruct(heads, F32), jax.ShapeDtypeStruct((n, d), F32), sd],
        vmem(11),
        [
            pltpu.VMEM((n, d), F32),
            pltpu.VMEM((n, n), F32),
            pltpu.VMEM((n, 128), BF),
            pltpu.VMEM((n, 128), BF),
            pltpu.VMEM((128, n), BF),
            pltpu.VMEM((d, n), F32),
            pltpu.VMEM(heads, F32),
            pltpu.VMEM(heads, F32),
        ],
        [Spread(a)] + jobs, cid,
        16 * n * d * d + 40 * QB * QB * d * 4, 2 * (4 * d * d + 16 * n * d),
    )


MLP_STEPS = 6
SPLIT = 2
SPLITB = 2


def gelu(u):
    return u * (0.5 * jnp.tanh(u * (GC + (GC * GA) * (u * u))) + 0.5)


FORWARD = {"Gather": (0, 2, -1), "Line": (0, 3, -1)}
BACKWARD = {"Reduce": (0, 1, 5)}


def grid_steps(jobs, points):
    step = pl.program_id(0)
    for point in range(MLP_STEPS):
        if any(point in at_points(j, points) for j in jobs):
            pl.when(step == point)(functools.partial(steps_at, jobs, point, points))


def mlp_body(row, ins, outs, scr, jobs):
    xm_ref, m_ref, up_ref, dn_ref, gain = ins
    x_ref, a_ref, u_ref = outs
    (acc,) = scr
    step = pl.program_id(0)
    grid_steps(jobs, FORWARD)

    @pl.when(step == 0)
    def _():
        acc[...] = xm_ref[...]

    up = up_ref[...]
    dn = dn_ref[...]
    cut = m_ref.shape[0] // SPLIT
    us = [mm(m_ref[i * cut : (i + 1) * cut], up) for i in range(SPLIT)]
    for i, u in enumerate(us):
        rows = slice(i * cut, (i + 1) * cut)
        u_ref[rows] = u.astype(BF)
        acc[rows] += mm(gelu(u).astype(BF), dn, NT)

    @pl.when(step == pl.num_programs(0) - 1)
    def _():
        x = acc[...]
        x_ref[...] = x
        xh, _ = norm_stats(x)
        a_ref[...] = (xh * gain[row : row + 1]).astype(BF)
        finish(jobs, FORWARD)


def mlp(xm, m, w, gain, row, jobs, cid):
    n, d = xm.shape
    ff = w.shape[1] // 2
    steps = MLP_STEPS if jobs else MLP_STEPS // 2
    fc = ff // steps
    full = pl.BlockSpec((n, d), lambda i: (0, 0))
    return run(
        functools.partial(mlp_body, row), "mlp",
        [xm, m, w, w, gain],
        [
            full,
            full,
            pl.BlockSpec((d, fc), lambda i: (0, i)),
            pl.BlockSpec((d, fc), lambda i: (0, i + steps)),
            pl.BlockSpec(gain.shape, lambda i: (0, 0)),
        ],
        [
            jax.ShapeDtypeStruct((n, d), F32),
            jax.ShapeDtypeStruct((n, d), BF),
            jax.ShapeDtypeStruct((n, ff), BF),
        ],
        [full, full, pl.BlockSpec((n, fc), lambda i: (0, i))],
        [pltpu.VMEM((n, d), F32)],
        jobs, cid,
        4 * n * d * ff, 4 * d * ff + 2 * n * ff + 10 * n * d, grid=(steps,),
    )


def mlp_back_body(at, ins, outs, scr, jobs):
    g_ref, xm_ref, m_ref, u_ref, up_ref, dn_ref, gain = ins[:7]
    gm_ref, go_ref, dup_ref, ddn_ref, dgain_ref = outs
    gy, gyt, mt, dm = scr[:4]
    step = pl.program_id(0)
    grid_steps(jobs, BACKWARD)
    if len(ins) > 7:
        counted, info = ins[7:]
        cot_ref, g_ref = g_ref, scr[4]

        @pl.when(step == 0)
        def _():
            n = cot_ref.shape[0]
            t = lax.axis_index("tensor")
            base = t % 2 * n
            masked = counted[:, pl.ds(aligned(base, 128), n)]
            pos = base + lax.broadcasted_iota(jnp.int32, (1, n), 1)
            live = (pos < info[0]) & ((t >= 2) | (masked == 1))
            col = jnp.broadcast_to(jnp.where(live, 1.0, 0.0), (8, n)).T[:, 0:1]
            g_ref[...] = cot_ref[...].astype(F32) * col

    @pl.when(step == 0)
    def _():
        gb = g_ref[...].astype(BF)
        gy[...] = gb
        gyt[...] = gb.T
        mt[...] = m_ref[...].T
        dm[...] = jnp.zeros_like(dm)

    cut = u_ref.shape[1] // SPLITB
    gyv, gytv, mtv = gy[...], gyt[...], mt[...]
    parts = [slice(i * cut, (i + 1) * cut) for i in range(SPLITB)]
    dhs = [mm(gyv, dn_ref[:, c]) for c in parts]
    add = None
    for c, dh in zip(parts, dhs):
        u = u_ref[:, c].astype(F32)
        u2 = u * u
        th = jnp.tanh(u * (GC + (GC * GA) * u2))
        half = 0.5 * th + 0.5
        h = (u * half).astype(BF)
        slope = half + (u * (1.0 - th * th)) * ((0.5 * GC) + (1.5 * GC * GA) * u2)
        du = (dh * slope).astype(BF)
        more = mm(du, up_ref[:, c], NT)
        add = more if add is None else add + more
        dup_ref[:, c] = mm(mtv, du).astype(BF)
        ddn_ref[:, c] = mm(gytv, h).astype(BF)
    dm[...] += add

    @pl.when(step == MLP_STEPS - 1)
    def _():
        dz, dgain = norm_back(xm_ref[...], gain[at : at + 1], dm[...])
        gm = g_ref[...] + dz
        gm_ref[...] = gm
        go_ref[...] = gm.astype(BF)
        dgain_ref[...] = dgain
        finish(jobs, BACKWARD)


def mlp_back(g, xm, m, u, w, gain, at, top, jobs, cid):
    n, d = xm.shape
    ff = w.shape[1] // 2
    steps = MLP_STEPS
    fc = ff // steps
    full = pl.BlockSpec((n, d), lambda i: (0, 0))
    row = pl.BlockSpec((1, d), lambda i: (0, 0))
    wide = pl.BlockSpec((d, fc), lambda i: (0, i))
    return run(
        functools.partial(mlp_back_body, at), "mlp_back",
        [g, xm, m, u, w, w, gain] + top,
        [
            full, full, full,
            pl.BlockSpec((n, fc), lambda i: (0, i)),
            wide,
            pl.BlockSpec((d, fc), lambda i: (0, i + steps)),
            pl.BlockSpec(gain.shape, lambda i: (0, 0)),
        ]
        + ([pl.BlockSpec(top[0].shape, lambda i: (0, 0)), smem()] if top else []),
        [
            jax.ShapeDtypeStruct((n, d), F32),
            jax.ShapeDtypeStruct((n, d), BF),
            jax.ShapeDtypeStruct((d, ff), BF),
            jax.ShapeDtypeStruct((d, ff), BF),
            jax.ShapeDtypeStruct((1, d), F32),
        ],
        [full, full, wide, wide, row],
        [
            pltpu.VMEM((n, d), BF),
            pltpu.VMEM((d, n), BF),
            pltpu.VMEM((d, n), BF),
            pltpu.VMEM((n, d), F32),
        ]
        + ([pltpu.VMEM((n, d), F32)] if top else []),
        jobs, cid,
        8 * n * d * ff, 8 * d * ff + 2 * n * ff + 16 * n * d, grid=(steps,),
    )


def back_pair(g, segs, q_ref, do_ref, o_ref, lse_ref, hot, dqt, dka, dva):
    n = q_ref.shape[0]
    sl = pl.ds(aligned(g * 128, 128), 128)
    q2 = q_ref[:, sl]
    do2 = do_ref[:, sl]
    qt = q2.T
    dot = do2.T
    prod = dot.astype(F32) * o_ref[:, sl].T.astype(F32)
    for h in range(2):
        hs = slice(h * HD, h * HD + HD)
        low = half_of(h, qt.shape, 0)
        side = half_of(h, q2.shape, 1)
        none = jnp.zeros_like(q2)
        qth = jnp.where(low, qt, jnp.zeros_like(qt) if hot is None else hot[...])
        doth = jnp.where(low, dot, jnp.zeros_like(dot))
        qh = jnp.where(side, q2, none)
        doh = jnp.where(side, do2, none)
        dsum = jnp.sum(prod[hs], axis=0, keepdims=True)
        ls = lse_ref[g, h : h + 1, :]
        for at, (kr, vr, mask, bias, whole, base) in enumerate(segs):
            k2 = kr[:, sl]
            v2 = vr[:, sl]
            kt = k2.T
            kh = jnp.where(side, k2, none if mask is None else mask[...])
            for b in range(n // QB):
                cs = slice(b * QB, b * QB + QB)
                width = n if whole else (b + 1) * QB
                s = mm(kh[0:width], qth[:, cs])
                if bias is not None:
                    s = s + bias[0:width, cs]
                p = jnp.exp(s - ls[:, cs])
                dp = mm(v2[0:width], doth[:, cs])
                ds = (p * (dp - dsum[:, cs])).astype(BF)
                dv = mm(p.astype(BF), doh[cs])
                dk = mm(ds, qh[cs])
                dq = mm(kt[hs, 0:width], ds)
                if h == 0 and b == 0:
                    dva[base : base + width, :] = dv
                    dka[base : base + width, :] = dk
                elif h == 0 and not whole:
                    dva[base : base + width - QB, :] += dv[: width - QB]
                    dka[base : base + width - QB, :] += dk[: width - QB]
                    dva[base + width - QB : base + width, :] = dv[width - QB :]
                    dka[base + width - QB : base + width, :] = dk[width - QB :]
                else:
                    dva[base : base + width, :] += dv
                    dka[base : base + width, :] += dk
                if at == 0:
                    dqt[hs, cs] = dq
                else:
                    dqt[hs, cs] += dq
    return sl


def back_far_body(ins, outs, scr, jobs):
    (
        info, go_in, w_in, q_in, o_in, lse_in, ks_in, vs_in, cos_in, sin_in, kf_in, vf_in, cosf_in, sinf_in,
    ) = ins
    do_ref, dqp_ref, dkf_ref, dvf_ref, dks_ref, dvs_ref, daf_ref = [x.ref for x in outs]
    mask1, mask2, hot, dqt, dka, dva, das = scr
    early = jobs[0]
    rest = jobs[1:]
    n, d = go_in.ref.shape
    pairs = d // 128
    for j in rest:
        j.advance()
    far_masks(info, mask1, mask2, hot)
    go_ref = go_in()
    w_ref = w_in()
    do_ref[...] = mm(go_ref[...], w_ref[:, 3 * d : 4 * d]).astype(BF)
    outs[0].flush()
    for j in rest:
        j.advance()
    wk = w_ref[:, d : 2 * d]
    wv = w_ref[:, 2 * d : 3 * d]

    def part(k_in, v_in, mask, whole, c_in, s_in, dk_ref, dv_ref, begin):
        q_ref, o_ref, lse_ref = q_in(), o_in(), lse_in()
        k_ref, v_ref = k_in(), v_in()
        cos, sin = c_in(), s_in()

        def pair(g, carry):
            segs = ((k_ref, v_ref, mask, None, whole, 0),)
            sl = back_pair(g, segs, q_ref, do_ref, o_ref, lse_ref, hot, dqt, dka, dva)
            if begin:
                dqp_ref[sl, :] = dqt[...]
            else:
                dqp_ref[sl, :] += dqt[...]
            dk_ref[:, sl] = turn(dka[...], cos[...], -sin[...]).astype(BF)
            dv_ref[:, sl] = dva[...].astype(BF)
            return carry

        return pair

    pair = part(ks_in, vs_in, mask2, False, cos_in, sin_in, dks_ref, dvs_ref, True)
    lax.fori_loop(0, pairs, pair, 0)
    das[...] = (mm(dks_ref[...], wk, NT) + mm(dvs_ref[...], wv, NT)).astype(BF)
    early.go(das)
    outs[4].flush()
    outs[5].flush()
    pair = part(kf_in, vf_in, mask1, True, cosf_in, sinf_in, dkf_ref, dvf_ref, False)
    lax.fori_loop(0, pairs // 3, pair, 0)
    for j in rest:
        j.advance()
    lax.fori_loop(pairs // 3, pairs, pair, 0)
    outs[1].flush()
    outs[2].flush()
    outs[3].flush()
    daf_ref[...] = (mm(dkf_ref[...], wk, NT) + mm(dvf_ref[...], wv, NT)).astype(BF)
    outs[6].flush()
    early.end(das)
    for j in rest:
        j.complete()


def back_far(info, go, o, lse, q, kf, vf, ks, vs, w, cosf, sinf, cos, sin, jobs, cid):
    n, d = go.shape
    sd = jax.ShapeDtypeStruct((n, d), BF)
    return run(
        back_far_body, "back_far",
        [info, go, w, q, o, lse, ks, vs, cos, sin, kf, vf, cosf, sinf], [smem()] + vmem(13),
        [sd, jax.ShapeDtypeStruct((d, n), F32)] + [sd] * 5, vmem(7),
        [
            pltpu.VMEM((n, 128), BF),
            pltpu.VMEM((n, 128), BF),
            pltpu.VMEM((128, n), BF),
            pltpu.VMEM((128, n), F32),
            pltpu.VMEM((n, 128), F32),
            pltpu.VMEM((n, 128), F32),
            pltpu.VMEM((n, d), BF),
        ],
        [Early((n, d))] + jobs, cid,
        10 * n * d * d + 70 * QB * QB * d * 4, 2 * (4 * d * d + 18 * n * d),
    )


def back_near_body(row, ins, outs, scr, jobs):
    (
        info, q_in, do_in, o_in, lse_in, ko_in, vo_in, dqp_in, cos_in, sin_in, go_in, af_in, dkf_in, dvf_in,
        as_in, dks_in, dvs_in, ao_in, w_in, x_in, gm_in, gain_in,
    ) = ins
    da_ref, db_ref, g_ref, dgain_ref = [x.ref for x in outs]
    bias, dqt, dka, dva, dq_s, dko_s, dvo_s, dao = scr
    back = jobs[0]
    rest = jobs[1:]
    n, d = do_in.ref.shape
    pairs = d // 128
    back.begin()
    for j in rest:
        j.advance()
    near_bias(info, bias)
    q_ref, do_ref, o_ref, lse_ref = q_in(), do_in(), o_in(), lse_in()
    ko_ref, vo_ref, dqp_ref, cos, sin = ko_in(), vo_in(), dqp_in(), cos_in(), sin_in()

    def pair(g, carry):
        segs = ((ko_ref, vo_ref, None, bias, False, 0),)
        sl = back_pair(g, segs, q_ref, do_ref, o_ref, lse_ref, None, dqt, dka, dva)
        dq = (dqt[...] + dqp_ref[sl, :]).T
        dq_s[:, sl] = turn(dq * SCALE, cos[...], -sin[...]).astype(BF)
        dko_s[:, sl] = turn(dka[...], cos[...], -sin[...]).astype(BF)
        dvo_s[:, sl] = dva[...].astype(BF)
        return carry

    lax.fori_loop(0, pairs // 2, pair, 0)
    for j in rest:
        j.advance()
    lax.fori_loop(pairs // 2, pairs, pair, 0)
    db_ref[:, d : 2 * d] = mm(go_in()[...].T, o_ref[...]).astype(BF)
    aot = ao_in()[...].T
    aft = af_in()[...].T
    ast = as_in()[...].T
    db_ref[:, 0:d] = (
        mm(aot, dvo_s[...]) + mm(aft, dvf_in()[...]) + mm(ast, dvs_in()[...])
    ).astype(BF)
    outs[1].flush()
    da_ref[:, 0:d] = mm(aot, dq_s[...]).astype(BF)
    da_ref[:, d : 2 * d] = (
        mm(aot, dko_s[...]) + mm(aft, dkf_in()[...]) + mm(ast, dks_in()[...])
    ).astype(BF)
    outs[0].flush()
    for j in rest:
        j.advance()
    w_ref = w_in()
    dao[...] = (
        mm(dko_s[...], w_ref[:, d : 2 * d], NT)
        + mm(dvo_s[...], w_ref[:, 2 * d : 3 * d], NT)
        + mm(dq_s[...], w_ref[:, 0:d], NT)
    )
    back.end(dao)
    dz, dgain = norm_back(x_in()[...].astype(F32), gain_in()[row : row + 1], dao[...])
    g_ref[...] = gm_in()[...] + dz
    dgain_ref[...] = dgain
    for j in rest:
        j.complete()


def back_near(row, ins, daf, got, jobs, cid):
    n, d = ins[1].shape
    wide = jax.ShapeDtypeStruct((d, 2 * d), BF)
    return run(
        functools.partial(back_near_body, row), "back_near",
        ins, [smem()] + vmem(len(ins) - 1),
        [wide, wide, jax.ShapeDtypeStruct((n, d), F32), jax.ShapeDtypeStruct((1, d), F32)], vmem(4),
        [
            pltpu.VMEM((n, n), F32),
            pltpu.VMEM((128, n), F32),
            pltpu.VMEM((n, 128), F32),
            pltpu.VMEM((n, 128), F32),
            pltpu.VMEM((n, d), BF),
            pltpu.VMEM((n, d), BF),
            pltpu.VMEM((n, d), BF),
            pltpu.VMEM((n, d), F32),
        ],
        [Return(daf, got)] + jobs, cid,
        22 * n * d * d + 30 * QB * QB * d * 4, 2 * (8 * d * d + 24 * n * d),
    )


def first_body(ins, outs, scr, jobs):
    x_in, gain_in = ins[0:2]
    narrow, (up, down) = ins[2:6], ins[6:8]
    layers, d = up.shape[0:2]
    pa0, ob, db, ot, dt, sem = scr
    rows = pa0.shape[1]
    pas = [pa0] + [x.ref for x in outs[1:layers]]
    pms = [x.ref for x in outs[layers:]]
    dp = lax.axis_index("dp")
    at_a = pl.ds(aligned(slot_of(dp, ORDERS[0]) * rows), rows)
    at_b = pl.ds(aligned(slot_of(dp, ORDERS[1]) * rows), rows)
    copies = []
    for l in range(layers):
        for i, (src, dst) in enumerate(
            [(x.at[l], ob.at[l, p]) for p, x in enumerate(narrow)]
            + [(down.at[l], db.at[l]), (up.at[l, at_a, :], pms[l].at[0])]
        ):
            copies.append(pltpu.make_async_copy(src, dst, sem.at[l * 6 + i]))
            copies[-1].start()

    def narrow_parts(l):
        for p in range(4):
            ot[p] = ob[l, p].T
            pas[l][p] = ot[p, at_a if p < 2 else at_b, :]

    for c in copies[0:4]:
        c.wait()
    narrow_parts(0)
    line = jobs[0]
    line.src = pa0
    line.advance()
    xh, _ = norm_stats(x_in()[...].astype(F32))
    outs[0].ref[...] = (xh * gain_in()[0:1]).astype(BF)
    outs[0].flush()
    line.advance()
    for c in copies[4:]:
        c.wait()
    for l in range(layers):
        dt[...] = db[l].T
        pms[l][1] = dt[at_b, :]
    line.advance()
    for l in range(1, layers):
        narrow_parts(l)
    line.complete()


def first(x, gain, weights, cid):
    n, d = x.shape
    q, up = weights[0], weights[4]
    layers, rows = q.shape[0], d >> BITS
    w, f = q.shape[1], up.shape[2]
    pa = jax.ShapeDtypeStruct((4, rows, w), BF)
    pm = jax.ShapeDtypeStruct((2, rows, d), BF)
    assert f == d
    return run(
        first_body, "first", [x, gain] + list(weights), vmem(2) + any_spec(6),
        [jax.ShapeDtypeStruct((n, d), BF)] + [pa] * (layers - 1) + [pm] * layers, vmem(2 * layers),
        [
            pltpu.VMEM((4, rows, w), BF),
            pltpu.VMEM((layers, 4, w, d), BF),
            pltpu.VMEM((layers, f, d), BF),
            pltpu.VMEM((4, d, w), BF),
            pltpu.VMEM((d, f), BF),
            dma(6 * layers),
        ],
        [Line(None, False, (4, rows, w))], cid, 10 * n * d, 4 * n * d,
    )


def layout_body(ins, outs, scr, jobs):
    count = len(ins) // 2
    for k in reversed(range(count)):
        ref = ins[count + k]()
        f = ref.shape[1] // 2
        outs[4].ref[k] = ref[:, 0:f].astype(F32)
        outs[5].ref[k] = ref[:, f : 2 * f].astype(F32).T
    outs[4].flush()
    outs[5].flush()
    for k in reversed(range(count)):
        v = ins[k]()[...].astype(F32)
        w = v.shape[1] // 4
        vt = v.T
        for i in range(4):
            outs[i].ref[k] = vt[i * w : i * w + w]
    for i in range(4):
        outs[i].flush()


def layout(att, mlps):
    layers = len(att)
    d = att[0].shape[0]
    w = att[0].shape[1] // 4
    f = mlps[0].shape[1] // 2
    shapes = [(layers, w, d)] * 4 + [(layers, d, f), (layers, f, d)]
    return run(
        layout_body, "layout", att + mlps, vmem(2 * layers),
        [jax.ShapeDtypeStruct(x, F32) for x in shapes], vmem(6), [], [], None, 1, 6 * layers * d * (4 * w + 2 * f),
    )[0]


def wide_of(every):
    return jnp.concatenate(
        [every[z, p] for p in range(every.shape[1]) for z in range(NZ)], axis=1
    )


def turning(n):
    position = np.arange(LMAX, dtype=np.float32)
    frequency = np.exp(
        (-math.log(10000.0) * np.arange(HD // 2, dtype=np.float32) / (HD // 2)).astype(np.float32)
    )
    angles = (position[:, None] * frequency[None, :]).astype(np.float32).astype(np.float64)
    cos = np.concatenate([np.cos(angles)] * 4, axis=1)
    sin = np.concatenate([-np.sin(angles), np.sin(angles)] * 2, axis=1)
    return [jnp.asarray(x.astype(np.float32).reshape(LMAX // n, n, 128)) for x in (cos, sin)]


def over_rest(arrays):
    n = lax.axis_size("dp")
    for b in range(BITS, n.bit_length() - 1):
        arrays = [x + lax.ppermute(x, "dp", [(i, i ^ (1 << b)) for i in range(n)]) for x in arrays]
    return arrays


def tail_body(ins, outs, scr, jobs):
    red, gains, wide, gain_line, att_line, wide_gather, att_gather = jobs
    every, part, total = scr
    for j in (red, gains, wide):
        j.advance()
    red.advance()
    gains.advance()
    red.advance()
    gains.advance()
    wide.complete()
    wide_gather.src = wide.o[0]
    gains.complete()
    gain_line.src, gain_line.dst = gains.o[0], total
    gain_line.advance()
    red.complete()
    a = red.o[0][...].astype(F32)
    b = red.o[1][...].astype(F32)
    w = a.shape[1] // 2
    c = w // NZ
    for z in range(NZ):
        cols = [x[:, k * w + z * c : k * w + z * c + c] for x in (a, b) for k in (0, 1)]
        every[z] = jnp.concatenate(cols, axis=1).astype(BF)
    att_line.src, att_line.dst = every, part
    att_line.advance()
    wide_gather.advance()
    wide_gather.advance()
    att_line.complete()
    att_gather.src = part
    att_gather.advance()
    wide_gather.advance()
    att_gather.advance()
    wide_gather.complete()
    att_gather.advance()
    gain_line.complete()
    outs[0].ref[...] = total[...]
    att_gather.complete()


def tail(att_grads, gain_rows, mlp_arrays, cid):
    rows = att_grads[0].shape[0] >> BITS
    w = att_grads[0].shape[1] // 2
    wide = LineSumWide(mlp_arrays)
    jobs = [
        Reduce(*att_grads), PlaneSum(gain_rows), wide,
        LineSum(None, gain_rows.shape, F32, True), LineSum(None, (rows, w)),
        Gather(None, wide.outs[0].shape), Gather(None, (rows, w)),
    ]
    res, extra = run(
        tail_body, "tail", [gain_rows], vmem(1), [jax.ShapeDtypeStruct(gain_rows.shape, F32)], vmem(1),
        [pltpu.VMEM((NZ, rows, w), BF), pltpu.VMEM((rows, w), BF), pltpu.VMEM(gain_rows.shape, F32)],
        jobs, cid, 1, 1 << 24,
    )
    return res[0], extra[5][0], extra[6][0]


def by_line(halves, counts):
    n = lax.axis_size("dp")
    cols = []
    for x, c in zip(halves, counts):
        for b in range(BITS, n.bit_length() - 1):
            x = x + lax.ppermute(x, "dp", [(i, i ^ (1 << b)) for i in range(n)])
        w = x.shape[1] // c
        for j in range(c):
            cols.append(x[:, j * w : (j + 1) * w].reshape(x.shape[0], NZ, w // NZ))
    return jnp.concatenate(cols, axis=2).transpose(1, 0, 2)


def on_device(
    tokens, lengths, noise_mask, cotangent, attn_gain, query_weight, key_weight, value_weight,
    out_weight, mlp_gain, up_weight, down_weight,
):
    n, d = tokens.shape
    info = lengths
    cos_t, sin_t = turning(n)
    cosf, sinf, cos, sin = (cos_t, 0), (sin_t, 0), (cos_t, 1), (sin_t, 1)

    res, ((every,),) = first(
        tokens, attn_gain,
        [x.transpose(0, 2, 1) for x in (query_weight, key_weight, value_weight)]
        + [out_weight, up_weight, down_weight],
        0,
    )
    a = res[0]
    pa = [None] + list(res[1:LAYERS])
    pm = res[LAYERS:]
    (wa,), (wide,) = transfer("gather_first", [Gather(wide_of(every)), Line(pm[0], True)], 1)
    was, wms, saved = [], [], []
    x = tokens
    for l in range(LAYERS):
        more = l + 1 < LAYERS
        jobs = [Gather(wide)] + ([Line(pa[l + 1], False)] if more else [])
        res, extra = attend(
            info, x, a, wa, cosf, sinf, cos, sin, mlp_gain, l, jobs, 10 + l
        )
        q, ko, vo, kf, vf, ks, vs, o, lse, xm, m = res
        af, as_ = extra[0]
        wm = extra[1][0]
        was.append(wa)
        wms.append(wm)
        jobs = []
        if more:
            piece = wide_of(extra[2][0])
            jobs = [Line(pm[l + 1], True), Gather(piece)]
        nxt = min(l + 1, LAYERS - 1)
        (x_next, a_next, u), extra = mlp(xm, m, wm, attn_gain, nxt, jobs, 20 + l)
        if more:
            wide, wa = extra[0][0], extra[1][0]
        saved.append((x, a, af, as_, q, kf, vf, ks, vs, ko, vo, o, lse, xm, m, u))
        x, a = x_next, a_next
    block_out = x

    g = cotangent
    top = [noise_mask, info]
    gains = [None] * (2 * LAYERS)
    att = [None] * LAYERS
    mlps = [None] * LAYERS
    att_grads = mlp_parts = mlp_arrays = None

    for l in reversed(range(LAYERS)):
        x, a, af, as_, q, kf, vf, ks, vs, ko, vo, o, lse, xm, m, u = saved[l]
        above = l + 1 < LAYERS
        jobs = []
        if above:
            jobs = [Reduce(*att_grads), LineSumWide(mlp_arrays)]
        res, extra = mlp_back(g, xm, m, u, wms[l], mlp_gain, l, top, jobs, 30 + l)
        top = []
        gm, go, dup, ddn, gains[LAYERS + l] = res
        jobs = [Reduce(dup, ddn, 0, 2)]
        if above:
            jobs += [LineSum(by_line(extra[0], (2, 2))), Gather(extra[1][0])]
        res, extra = back_far(
            info, go, o, lse, q, kf, vf, ks, vs, was[l], cosf, sinf, cos, sin, jobs, 40 + l
        )
        do, dqp, dkf, dvf, dks, dvs, daf = res
        got = extra[0][0]
        mlp_parts = [extra[1]]
        jobs = [Reduce(dup, ddn, 1, 2)]
        if above:
            mlps[l + 1] = extra[3][0]
            jobs.append(Gather(extra[2][0]))
        res, extra = back_near(
            l,
            [
                info, q, do, o, lse, ko, vo, dqp, cos, sin, go, af, dkf, dvf, as_, dks, dvs, a, was[l],
                x, gm, attn_gain,
            ],
            daf, got, jobs, 50 + l,
        )
        mlp_parts.append(extra[1])
        mlp_arrays = over_rest([p[i] for i in (0, 1) for p in mlp_parts])
        if above:
            att[l + 1] = extra[2][0]
        att_grads = res[0:2]
        g, gains[l] = res[2:4]

    gain_rows = jnp.concatenate(gains, axis=0)
    if lax.axis_size("dp") == 1 << BITS:
        gain_sums, mlps[0], att[0] = tail(att_grads, gain_rows, mlp_arrays, 2)
    else:
        (sums, (gain_rows,), (mlp_sum,)) = transfer(
            "reduce_last",
            [Reduce(*att_grads), PlaneSum(gain_rows), LineSumWide(mlp_arrays)],
            2,
        )
        for b in range(BITS, lax.axis_size("dp").bit_length() - 1):
            size = lax.axis_size("dp")
            gain_rows = gain_rows + lax.ppermute(
                gain_rows, "dp", [(i, i ^ (1 << b)) for i in range(size)]
            )
        (part,), (gain_sums,), (mlps[0],) = transfer(
            "line_last",
            [
                LineSum(by_line(sums, (2, 2))),
                LineSum(jnp.broadcast_to(gain_rows, (NZ,) + gain_rows.shape)),
                Gather(mlp_sum),
            ],
            3,
        )
        ((att[0],),) = transfer("gather_last", [Gather(part)], 4)
    grads = layout(att, mlps)
    return (
        block_out, g, gain_sums[:LAYERS], *[x.transpose(0, 2, 1) for x in grads[:3]], grads[3],
        gain_sums[LAYERS:], grads[4], grads[5],
    )


def solution(mesh):
    rows = P(("dp", "tensor"), None)
    cols = P(None, None, "tensor")
    mids = P(None, "tensor", None)
    return jax.shard_map(
        on_device,
        mesh=mesh,
        in_specs=(
            rows, P("dp"), P("dp", None), rows, P(), cols, cols, cols, mids, P(), cols, mids,
        ),
        out_specs=(rows, rows, P(), cols, cols, cols, mids, P(), cols, mids),
        check_vma=False,
    )
```

```python
import functools
import math

import jax
import jax.numpy as jnp
import numpy as np
from jax import lax
from jax.experimental import pallas as pl
from jax.experimental.pallas import tpu as pltpu
from jax.sharding import PartitionSpec as P

HD = 64
BLK = 16
LMAX = 1024
LAYERS = 2
EPS = 1e-05
NEG = -1e30
SCALE = 1.0 / math.sqrt(HD)
GC = math.sqrt(2.0 / math.pi)
GA = 0.044715
F32 = jnp.float32
BF = jnp.bfloat16
QB = 256
VMEM_LIMIT = 56 << 20

NN = (((1,), (0,)), ((), ()))
NT = (((1,), (1,)), ((), ()))
TN = (((0,), (0,)), ((), ()))


def mm(a, b, dims=NN):
    return lax.dot_general(a, b, dims, preferred_element_type=F32)


def norm_stats(x):
    mean = jnp.mean(x, axis=-1, keepdims=True)
    c = x - mean
    var = jnp.mean(c * c, axis=-1, keepdims=True)
    r = lax.rsqrt(var + EPS)
    return c * r, r


def norm_back(x, gain, dy):
    xh, r = norm_stats(x)
    gy = dy * gain
    m1 = jnp.mean(gy, axis=-1, keepdims=True)
    m2 = jnp.mean(gy * xh, axis=-1, keepdims=True)
    dz = r * (gy - m1 - xh * m2)
    return dz, jnp.sum(dy * xh, axis=0, keepdims=True)


def turn(y, cos, sin):
    lane = lax.broadcasted_iota(jnp.int32, y.shape, 1) % HD
    other = jnp.where(
        lane < HD // 2, pltpu.roll(y, 128 - HD // 2, 1), pltpu.roll(y, HD // 2, 1)
    )
    return y * cos + other * sin


def vmem(n):
    return [pl.BlockSpec(memory_space=pltpu.VMEM)] * n


def smem():
    return pl.BlockSpec(memory_space=pltpu.SMEM)


def params(**kw):
    return pltpu.CompilerParams(vmem_limit_bytes=VMEM_LIMIT, **kw)


def cost(flops, nbytes, trans=0):
    return pl.CostEstimate(flops=int(flops), bytes_accessed=int(nbytes), transcendentals=int(trans))


MESH = pl.DeviceIdType.MESH
BITS = 3
ORDERS = ((0, 1, 2), (0, 2, 1))
NZ = 4


def bit_of(dp, b):
    return dp // (1 << b) % 2


def slot_of(dp, order):
    out = 0
    for b in order:
        out = out * 2 + bit_of(dp, b)
    return out


def partner(dp, b):
    return dp + (1 - 2 * bit_of(dp, b)) * (1 << b)


def greet(plane, line):
    dp = lax.axis_index("dp")
    t = lax.axis_index("tensor")
    barrier = pltpu.get_barrier_semaphore()
    if plane:
        for b in range(BITS):
            pl.semaphore_signal(barrier, inc=1, device_id=(partner(dp, b), t), device_id_type=MESH)
    if line:
        for s in range(1, NZ):
            pl.semaphore_signal(barrier, inc=1, device_id=(dp, (t + s) % NZ), device_id_type=MESH)
    pl.semaphore_wait(barrier, BITS * plane + (NZ - 1) * line)


def remote(src, dst, send, recv, dp, t):
    return pltpu.make_async_remote_copy(
        src_ref=src, dst_ref=dst, send_sem=send, recv_sem=recv, device_id=(dp, t), device_id_type=MESH
    )


def aligned(x, n=16):
    return pl.multiple_of(x, n)


def dma(n):
    return pltpu.SemaphoreType.DMA((n,))


def any_spec(n=1):
    return [pl.BlockSpec(memory_space=pl.ANY)] * n


class Job:
    plane = line = 0
    steps = BITS

    def bind(self, ins, outs, scr):
        self.at = 0
        self.i, self.o, self.s = ins, outs, scr
        self.dp = lax.axis_index("dp")
        self.t = lax.axis_index("tensor")

    def wait(self, s):
        pass

    def advance(self):
        if self.at < self.steps:
            if self.at > 0:
                self.wait(self.at - 1)
            self.start(self.at)
            self.at += 1

    def complete(self):
        while self.at < self.steps:
            self.advance()
        if self.steps:
            self.wait(self.steps - 1)


class Gather(Job):
    plane = 1

    def __init__(self, piece, shape=None, early=False):
        self.early = early
        self.rows, n = shape if piece is None else piece.shape
        self.half = n // 2
        self.src = None
        self.ins, self.in_specs = ([], []) if piece is None else ([piece], vmem(1))
        self.outs, self.out_specs = [jax.ShapeDtypeStruct((self.rows << BITS, n), BF)], any_spec()
        self.scratch = [dma(4 * BITS), dma(4 * BITS), dma(2)]

    def cols(self, i):
        return pl.ds(i * self.half, self.half)

    def source(self):
        return self.i[0] if self.src is None else self.src

    def own(self, i):
        at = slot_of(self.dp, ORDERS[i]) * self.rows
        return pltpu.make_async_copy(
            self.source().at[:, self.cols(i)],
            self.o[0].at[pl.ds(aligned(at), self.rows), self.cols(i)],
            self.s[2].at[i],
        )

    def copy(self, s, i):
        b = ORDERS[i][BITS - 1 - s]
        size = self.rows << s
        at = slot_of(self.dp, ORDERS[i]) // (1 << s) * size
        there = self.o[0].at[pl.ds(aligned(at), size), self.cols(i)]
        return remote(
            self.source().at[:, self.cols(i)] if s == 0 else there, there,
            self.s[0].at[2 * s + i], self.s[1].at[2 * s + i], partner(self.dp, b), self.t,
        )

    def across(self, s, i):
        slot = slot_of(self.dp, ORDERS[i])
        level = max(s - 1, 0)
        block = slot // (1 << level)
        if s > 0:
            block = block + 1 - 2 * (block % 2)
        size = self.rows << level
        there = self.o[0].at[pl.ds(aligned(block * size), size), self.cols(i)]
        k = 2 * BITS + 2 * s + i
        return remote(
            self.source().at[:, self.cols(i)] if s == 0 else there, there,
            self.s[0].at[k], self.s[1].at[k], partner(self.dp, ORDERS[i][0]), self.t,
        )

    def start(self, s):
        for i in range(2):
            if s < BITS - 1 or not self.early:
                self.copy(s, i).start()
            if self.early:
                self.across(s, i).start()
            if s == 0:
                self.own(i).start()

    def wait(self, s):
        for i in range(2):
            if s < BITS - 1 or not self.early:
                self.copy(s, i).wait()
            else:
                for k in range(BITS):
                    self.across(k, i).wait()
            if s == 0:
                self.own(i).wait()


class Reduce(Job):
    plane = 1

    def __init__(self, a, b, part=0, parts=1):
        self.full = a.shape[0]
        widths = (a.shape[1] // parts, b.shape[1] // parts)
        self.cols = [pl.ds(part * w, w) for w in widths]
        self.ins, self.in_specs = [a, b], any_spec(2)
        self.outs = [jax.ShapeDtypeStruct((self.full >> BITS, w), BF) for w in widths]
        self.out_specs = vmem(2)
        self.scratch = [pltpu.VMEM((self.full // 2, w), BF) for w in widths]
        for w in widths:
            self.scratch += [pltpu.VMEM((self.full >> (s + 1), w), BF) for s in range(BITS)]
        self.scratch += [dma(2 * BITS), dma(2 * BITS), dma(2)]

    def got(self, s, i):
        return self.s[2 + i * BITS + s]

    def offset(self, s, i):
        at = 0
        for j in range(1, s):
            at = at + bit_of(self.dp, ORDERS[i][j]) * (self.full >> (j + 1))
        return at

    def copy(self, s, i):
        b = ORDERS[i][s]
        size = self.full >> (s + 1)
        at = (1 - bit_of(self.dp, b)) * size
        if s == 0:
            there = self.i[i].at[pl.ds(aligned(at), size), self.cols[i]]
        else:
            there = self.s[i].at[pl.ds(aligned(self.offset(s, i) + at), size), :]
        send, recv = self.s[2 + 2 * BITS], self.s[3 + 2 * BITS]
        return remote(
            there, self.got(s, i), send.at[2 * s + i], recv.at[2 * s + i], partner(self.dp, b), self.t
        )

    def own(self, i):
        size = self.full // 2
        at = bit_of(self.dp, ORDERS[i][0]) * size
        return pltpu.make_async_copy(
            self.i[i].at[pl.ds(aligned(at), size), self.cols[i]], self.s[i], self.s[4 + 2 * BITS].at[i]
        )

    def start(self, s):
        for i in range(2):
            self.copy(s, i).start()
            if s == 0:
                self.own(i).start()

    def wait(self, s):
        for i in range(2):
            self.copy(s, i).wait()
            if s == 0:
                self.own(i).wait()
            size = self.full >> (s + 1)
            base = self.offset(s + 1, i)
            keep, got, out = self.s[i], self.got(s, i), self.o[i]
            last = s == BITS - 1
            step = 48 if size % 48 == 0 else size

            def add(j, carry):
                rows = pl.ds(aligned(base + j * step), step)
                here = pl.ds(aligned(j * step), step)
                total = (keep[rows, :].astype(F32) + got[here, :].astype(F32)).astype(BF)
                if last:
                    out[here, :] = total
                else:
                    keep[rows, :] = total
                return carry

            lax.fori_loop(0, size // step, add, 0)


class Line(Job):
    line = 1
    steps = NZ - 1

    def __init__(self, parts, wide, shape=None):
        self.count, self.rows, self.w = shape if parts is None else parts.shape
        self.wide = wide
        self.src = None
        self.ins, self.in_specs = ([], []) if parts is None else ([parts], vmem(1))
        if wide:
            shape = (self.rows, self.count * NZ * self.w)
        else:
            shape = (NZ, self.count, self.rows, self.w)
        self.outs, self.out_specs = [jax.ShapeDtypeStruct(shape, BF)], any_spec()
        m = self.count * 2 * self.steps
        self.scratch = [dma(m), dma(m), dma(self.count)]

    def place(self, p, z):
        if self.wide:
            at = (p * NZ + z) * self.w
            return self.o[0].at[:, pl.ds(aligned(at, 128), self.w)]
        return self.o[0].at[z, p]

    def copy(self, s, p, way):
        z = (self.t - way * s) % NZ
        k = (s * 2 + (way > 0)) * self.count + p
        there = self.place(p, z)
        return remote(
            self.source().at[p] if s == 0 else there, there, self.s[0].at[k], self.s[1].at[k],
            self.dp, (self.t + way) % NZ,
        )

    def source(self):
        return self.i[0] if self.src is None else self.src

    def inside(self, s, way, receiver):
        t = self.t
        if receiver:
            return (t - way * (s + 1) >= 0) & (t - way * (s + 1) < NZ)
        return (t - way * s >= 0) & (t - way * s < NZ) & (t + way >= 0) & (t + way < NZ)

    def own(self, p):
        return pltpu.make_async_copy(self.source().at[p], self.place(p, self.t), self.s[2].at[p])

    def start(self, s):
        for way in (1, -1):

            @pl.when(self.inside(s, way, False))
            def _(way=way):
                for p in range(self.count):
                    self.copy(s, p, way).start()

        if s == 0:
            for p in range(self.count):
                self.own(p).start()

    def wait(self, s):
        for way in (1, -1):

            @pl.when(self.inside(s, way, True))
            def _(way=way):
                for p in range(self.count):
                    self.copy(s, p, way).wait_recv()

            @pl.when(self.inside(s, way, False))
            def _(way=way):
                for p in range(self.count):
                    self.copy(s, p, way).wait_send()

        if s == 0:
            for p in range(self.count):
                self.own(p).wait()


class LineSum(Job):
    line = 1
    steps = 1

    def __init__(self, parts, shape=None, kind=BF, same=False):
        shape = parts.shape[1:] if shape is None else shape
        self.same = same
        self.src = self.dst = None
        self.outs = self.out_specs = []
        self.ins, self.in_specs = ([], []) if parts is None else ([parts], vmem(1))
        if parts is not None:
            kind = parts.dtype
            self.outs, self.out_specs = [jax.ShapeDtypeStruct(shape, kind)], vmem(1)
        self.scratch = [pltpu.VMEM((NZ - 1,) + tuple(shape), kind), dma(3), dma(3)]

    def source(self, z):
        ref = self.i[0] if self.src is None else self.src
        return ref if self.same else ref.at[z]

    def copies(self):
        for s in (1, 2, 3):
            z = (self.t + s) % NZ
            yield remote(
                self.source(z), self.s[0].at[s - 1], self.s[1].at[s - 1], self.s[2].at[s - 1],
                self.dp, z,
            )

    def start(self, s):
        for c in self.copies():
            c.start()

    def wait(self, s):
        for c in self.copies():
            c.wait()
        got = self.s[0]
        total = self.source(self.t)[...].astype(F32)
        for k in range(NZ - 1):
            total = total + got[k].astype(F32)
        out = self.o[0] if self.dst is None else self.dst
        out[...] = total.astype(out.dtype)


class LineSumWide(Job):
    line = 1
    steps = 1

    def __init__(self, arrays):
        self.w = arrays[0].shape[1] // 2
        self.ins, self.in_specs = list(arrays), vmem(4)
        shape = arrays[0].shape
        self.outs, self.out_specs = [jax.ShapeDtypeStruct(shape, BF)], vmem(1)
        self.scratch = [pltpu.VMEM((NZ - 1,) + shape, BF), dma(6), dma(6)]

    def part(self, kind, half, z):
        return self.i[2 * kind + half].at[:, pl.ds(aligned(z % 2 * self.w, 128), self.w)]

    def copy(self, s, kind, half):
        z = (self.t + s) % NZ
        k = (s - 1) * 2 + kind
        return remote(
            self.part(kind, half, z), self.s[0].at[s - 1, :, pl.ds(kind * self.w, self.w)],
            self.s[1].at[k], self.s[2].at[k], self.dp, z,
        )

    def start(self, step):
        for s in (1, 2, 3):
            for half in (0, 1):

                @pl.when((self.t + s) % NZ // 2 == half)
                def _(s=s, half=half):
                    for kind in (0, 1):
                        self.copy(s, kind, half).start()

    def wait(self, step):
        for s in (1, 2, 3):
            for kind in (0, 1):
                self.copy(s, kind, 0).wait()
        got, out = self.s[0], self.o[0]
        for half in (0, 1):

            @pl.when(self.t // 2 == half)
            def _(half=half):
                for kind in (0, 1):
                    at = slice(kind * self.w, (kind + 1) * self.w)
                    total = self.part(kind, half, self.t)[...].astype(F32)
                    for k in range(NZ - 1):
                        total = total + got[k, :, at].astype(F32)
                    out[:, at] = total.astype(BF)


class PlaneSum(Job):
    plane = 1

    def __init__(self, x):
        self.ins, self.in_specs = [x], vmem(1)
        self.outs, self.out_specs = [jax.ShapeDtypeStruct(x.shape, F32)], vmem(1)
        self.scratch = [pltpu.VMEM((BITS,) + x.shape, F32), dma(BITS), dma(BITS)]

    def copy(self, s):
        return remote(
            self.i[0] if s == 0 else self.o[0], self.s[0].at[s], self.s[1].at[s], self.s[2].at[s],
            partner(self.dp, s), self.t,
        )

    def start(self, s):
        self.copy(s).start()

    def wait(self, s):
        self.copy(s).wait()
        self.o[0][...] = (self.i[0] if s == 0 else self.o[0])[...] + self.s[0][s]


class Spread(Job):
    line = 1
    steps = 0

    def __init__(self, a):
        self.ins, self.in_specs = [a], any_spec()
        self.outs, self.out_specs = [jax.ShapeDtypeStruct(a.shape, BF)] * 2, any_spec(2)
        self.scratch = [pltpu.VMEM(a.shape, BF), pltpu.VMEM(a.shape, BF), dma(2), dma(2), dma(2)]

    def put(self, src, which, to, k):
        return remote(src, self.s[which], self.s[2].at[k], self.s[3].at[which], self.dp, to)

    def save(self, which):
        return pltpu.make_async_copy(self.s[which], self.o[which], self.s[4].at[which])

    def begin(self):
        a, t = self.i[0], self.t

        @pl.when(t == 2)
        def _():
            self.put(a, 0, 1, 0).start()
            self.put(a, 0, 3, 1).start()

        @pl.when(t % 2 == 0)
        def _():
            self.s[0][...] = jnp.zeros_like(self.s[0])

        @pl.when(t >= 2)
        def _():
            self.s[1][...] = jnp.zeros_like(self.s[1])

    def first(self):
        a, t = self.i[0], self.t

        @pl.when(t % 2 == 1)
        def _():
            self.put(a, 0, 1, 0).wait_recv()

        @pl.when(t == 1)
        def _():
            self.put(self.s[0], 1, 0, 0).start()

        @pl.when(t == 3)
        def _():
            self.put(a, 1, 1, 0).start()

        self.save(0).start()

    def second(self):
        @pl.when(self.t < 2)
        def _():
            self.put(self.i[0], 1, 1, 0).wait_recv()

        self.save(1).start()

    def end(self):
        a, t = self.i[0], self.t

        @pl.when(t >= 1)
        def _():
            self.put(a, 0, 1, 0).wait_send()

        @pl.when(t == 2)
        def _():
            self.put(a, 0, 3, 1).wait_send()

        self.save(0).wait()
        self.save(1).wait()


class Early(Job):
    line = 1
    steps = 0

    def __init__(self, shape):
        self.ins, self.in_specs = [], []
        self.outs, self.out_specs = [jax.ShapeDtypeStruct(shape, BF)], any_spec()
        self.scratch = [dma(1), dma(1)]

    def put(self, src, to):
        return remote(src, self.o[0], self.s[0].at[0], self.s[1].at[0], self.dp, to)

    def go(self, das):
        @pl.when(self.t < 2)
        def _():
            self.put(das, 2 * self.t + 1).start()

    def end(self, das):
        @pl.when(self.t < 2)
        def _():
            self.put(das, 1).wait_send()

        @pl.when(self.t % 2 == 1)
        def _():
            self.put(das, 1).wait_recv()


class Return(Job):
    line = 1
    steps = 0

    def __init__(self, daf, got):
        self.ins, self.in_specs = [daf, got], vmem(2)
        self.outs, self.out_specs = [], []
        sd = pltpu.VMEM(daf.shape, BF)
        self.scratch = [sd, sd, sd, dma(1), dma(2)]

    def put(self, src, which):
        return remote(src, self.s[which], self.s[3].at[0], self.s[4].at[which], self.dp, 2)

    def begin(self):
        daf, got = self.i

        @pl.when(self.t == 1)
        def _():
            self.s[2][...] = (daf[...].astype(F32) + got[...].astype(F32)).astype(BF)
            self.put(self.s[2], 0).start()

        @pl.when(self.t == 3)
        def _():
            self.put(daf, 1).start()

    def end(self, acc):
        daf, got = self.i

        @pl.when(self.t == 2)
        def _():
            self.put(daf, 0).wait_recv()
            self.put(daf, 1).wait_recv()
            acc[...] += self.s[0][...].astype(F32) + self.s[1][...].astype(F32)

        @pl.when(self.t == 3)
        def _():
            acc[...] += got[...].astype(F32)

        @pl.when(self.t % 2 == 1)
        def _():
            self.put(daf, 0).wait_send()


def at_points(j, points):
    return points.get(type(j).__name__, (0,) * j.steps)


def steps_at(jobs, point, points):
    for j in jobs:
        for s in range(j.steps):
            if at_points(j, points)[s] == point:
                if s > 0:
                    j.wait(s - 1)
                j.start(s)


def finish(jobs, points):
    steps_at(jobs, -1, points)
    for j in jobs:
        if j.steps:
            j.wait(j.steps - 1)


class In:
    def __init__(self, hbm, ref, sem):
        self.ref = ref
        self.copy = pltpu.make_async_copy(hbm, ref, sem)
        self.copy.start()

    def __call__(self):
        if self.copy is not None:
            self.copy.wait()
            self.copy = None
        return self.ref


class Out:
    def __init__(self, hbm, ref, sem):
        self.ref = ref
        self.copy = pltpu.make_async_copy(ref, hbm, sem)
        self.sent = False

    def flush(self):
        if not self.sent:
            self.copy.start()
            self.sent = True


def meet(jobs):
    greet(max(j.plane for j in jobs), max(j.line for j in jobs))


def lazily(body, ins, in_specs, outs, out_specs, scratch):
    lazy = [sp.memory_space == pltpu.VMEM for sp in in_specs]
    picks = [x[1] if isinstance(x, tuple) else None for x in ins]
    ins = [x[0] if isinstance(x, tuple) else x for x in ins]
    bufs = [
        pltpu.VMEM(x.shape if p is None else x.shape[1:], x.dtype)
        for x, z, p in zip(ins, lazy, picks)
        if z
    ]
    bufs += [pltpu.VMEM(x.shape, x.dtype) for x in outs]
    own = len(scratch)
    count = sum(lazy)

    def wrapped(i, o, s, jobs):
        mine, rest = s[:own], s[own:]
        vm, sin, sout = rest[:-2], rest[-2], rest[-1]
        given = []
        k = 0
        for ref, z, p in zip(i, lazy, picks):
            if z:
                if p is not None:
                    ref = ref.at[lax.axis_index("tensor") % 2 if p else 0]
                given.append(In(ref, vm[k], sin.at[k]))
                k += 1
            else:
                given.append(ref)
        results = [Out(ref, vm[count + k], sout.at[k]) for k, ref in enumerate(o)]
        if jobs:
            meet(jobs)
        body(given, results, mine, jobs)
        for x, z in zip(given, lazy):
            if z:
                x()
        for x in results:
            x.flush()
        for x in results:
            x.copy.wait()

    specs = [any_spec()[0] if z else sp for sp, z in zip(in_specs, lazy)]
    return wrapped, ins, specs, any_spec(len(outs)), list(scratch) + bufs + [dma(count), dma(len(outs))]


def run(body, name, ins, in_specs, outs, out_specs, scratch, jobs, cid, flops, nbytes, grid=None):
    late = grid is None and len(ins) > 0
    if late:
        body, ins, in_specs, out_specs, scratch = lazily(body, ins, in_specs, outs, out_specs, scratch)
    cuts = []
    for what in ("ins", "outs", "scratch"):
        own = {"ins": ins, "outs": outs, "scratch": scratch}[what]
        cuts.append([len(own)] + [len(getattr(j, what)) for j in jobs])

    def kernel(*refs):
        at = 0
        groups = []
        for cut in cuts:
            g = []
            for c in cut:
                g.append(refs[at : at + c])
                at += c
            groups.append(g)
        for k, j in enumerate(jobs):
            j.bind(groups[0][k + 1], groups[1][k + 1], groups[2][k + 1])
        if jobs and not late:
            if grid is None:
                meet(jobs)
            else:
                pl.when(pl.program_id(0) == 0)(functools.partial(meet, jobs))
        body(groups[0][0], groups[1][0], groups[2][0], jobs)

    for j in jobs:
        ins, in_specs = list(ins) + j.ins, list(in_specs) + j.in_specs
        outs, out_specs = list(outs) + j.outs, list(out_specs) + j.out_specs
        scratch = list(scratch) + j.scratch
    res = pl.pallas_call(
        kernel,
        out_shape=tuple(outs),
        in_specs=list(in_specs),
        out_specs=tuple(out_specs),
        scratch_shapes=list(scratch),
        compiler_params=params(collective_id=cid, has_side_effects=True) if jobs else params(),
        cost_estimate=cost(flops, nbytes),
        name=name,
        **({} if grid is None else {"grid": grid}),
    )(*ins)
    at = cuts[1][0]
    extra = []
    for c in cuts[1][1:]:
        extra.append(res[at : at + c])
        at += c
    return res[: cuts[1][0]], extra


def only_jobs(ins, outs, scr, jobs):
    for s in range(max(j.steps for j in jobs)):
        for j in jobs:
            j.advance()
    for j in jobs:
        j.complete()


def transfer(name, jobs, cid):
    return run(only_jobs, name, [], [], [], [], [], jobs, cid, 1, 1 << 24)[1]


def turned(out, tmp, cos, sin):
    for g in range(out.shape[1] // 128):
        sl = slice(g * 128, g * 128 + 128)
        out[:, sl] = turn(tmp[:, sl], cos[...], sin[...]).astype(BF)


def near_bias(info, bias):
    n = bias.shape[0]
    length = info[0]
    t = lax.axis_index("tensor")
    noisy = t < 2
    base = t % 2 * n
    j = lax.broadcasted_iota(jnp.int32, (n, n), 0)
    i = lax.broadcasted_iota(jnp.int32, (n, n), 1)
    bi = i // BLK
    bj = j // BLK
    low = jnp.where(noisy, bi, 0)
    seen = (bj <= bi) & (bj >= low) & (j + base < length)
    bias[...] = jnp.where(seen | (i == j), 0.0, NEG)


def far_masks(info, first, second, hot):
    n = hot.shape[1]
    length = info[0]
    t = lax.axis_index("tensor")
    noisy = t < 2
    odd = t % 2
    key = lax.broadcasted_iota(jnp.int32, (n, 128), 0)
    block = lax.broadcasted_iota(jnp.int32, (n, 128), 1) % HD
    real = block < n // BLK
    odd_lim = jnp.where(odd == 1, length, 0)
    lim = jnp.where(noisy, length - odd * n, 0)
    first[...] = jnp.where(real & (key >= odd_lim), NEG, 0.0).astype(BF)
    hidden = (key // BLK >= block) | (key >= lim)
    second[...] = jnp.where(real & hidden, NEG, 0.0).astype(BF)
    row = lax.broadcasted_iota(jnp.int32, (128, n), 0) % HD
    query = lax.broadcasted_iota(jnp.int32, (128, n), 1)
    hot[...] = jnp.where(query // BLK == row, 1.0, 0.0).astype(BF)


def half_of(h, shape, axis):
    at = lax.broadcasted_iota(jnp.int32, shape, axis)
    return (at < HD) if h == 0 else (at >= HD)


def attend_body(row, ins, outs, scr, jobs):
    info, a_in, w_in, cos_in, sin_in, cosf_in, sinf_in, x_in, gain_in = ins
    q_ref, ko_ref, vo_ref, kf_ref, vf_ref, ks_ref, vs_ref, o_ref, lse_ref, xm_ref, m_ref = [
        x.ref for x in outs
    ]
    tmp, bias, mask1, mask2, hot, acc, top, tot = scr
    spread = jobs[0]
    rest = jobs[1:]
    af_ref, as_ref = spread.s[0:2]
    n, d = x_in.ref.shape
    pairs = d // 128
    gather = rest[0]
    line = rest[1:]
    spread.begin()
    gather.advance()
    near_bias(info, bias)
    far_masks(info, mask1, mask2, hot)
    a_ref = a_in()
    w_ref = w_in()
    cos = cos_in()
    sin = sin_in()

    tmp[...] = mm(a_ref[...], w_ref[:, 0:d]) * SCALE
    turned(q_ref, tmp, cos, sin)

    def keys_of(src, kk, vv, c, s):
        av = src[...]
        tmp[...] = mm(av, w_ref[:, d : 2 * d])
        turned(kk, tmp, c, s)
        vv[...] = mm(av, w_ref[:, 2 * d : 3 * d]).astype(BF)

    keys_of(a_ref, ko_ref, vo_ref, cos, sin)
    for k in range(3):
        outs[k].flush()

    def segment(kk, vv, mask, full, first, last):
        def pair(g, carry):
            sl = pl.ds(aligned(g * 128, 128), 128)
            qt = q_ref[:, sl].T
            k2 = kk[:, sl]
            vt = vv[:, sl].T
            other_q = jnp.zeros_like(qt) if mask is None else hot[...]
            other_k = k2 if mask is None else mask[...]
            rows = pl.ds(aligned(g * 128, 128), 128)
            if not first:
                olds = top[g]
                tots = tot[g]
                before = acc[rows, :]
            tops, sums, outs = [], [], []
            chains = [(h, b) for h in range(2) for b in range(n // QB)]
            scores = []
            for h, b in chains:
                qh = jnp.where(half_of(h, qt.shape, 0), qt, other_q)
                kh = jnp.where(half_of(h, k2.shape, 1), k2, other_k)
                width = n if full else (b + 1) * QB
                scores.append(mm(kh[0:width], qh[:, b * QB : b * QB + QB]))
            for (h, b), s in zip(chains, scores):
                cs = slice(b * QB, b * QB + QB)
                width = s.shape[0]
                if mask is None:
                    s = s + bias[0:width, cs]
                mx = jnp.max(s, axis=0, keepdims=True)
                if not first:
                    old = olds[h : h + 1, cs]
                    mx = jnp.maximum(mx, old)
                    scale = jnp.exp(old - mx)
                e = jnp.exp(s - mx)
                total = jnp.sum(e, axis=0, keepdims=True)
                out = mm(vt[h * HD : h * HD + HD, 0:width], e.astype(BF))
                if not first:
                    total = total + tots[h : h + 1, cs] * scale
                    out = out + before[h * HD : h * HD + HD, cs] * scale
                if last:
                    mx = mx + jnp.log(total)
                    out = out / total
                tops.append(mx)
                sums.append(total)
                outs.append(out)
            for (h, b), mx, total, out in zip(chains, tops, sums, outs):
                cs = slice(b * QB, b * QB + QB)
                if last:
                    lse_ref[g, h : h + 1, cs] = mx
                else:
                    top[g, h : h + 1, cs] = mx
                    tot[g, h : h + 1, cs] = total
                    acc[pl.ds(aligned(g * 128 + h * HD, HD), HD), cs] = out
            if last:
                ot = jnp.concatenate(
                    [jnp.concatenate(outs[i : i + n // QB], axis=1) for i in (0, n // QB)], axis=0
                )
                o_ref[:, sl] = ot.T.astype(BF)
            return carry

        return pair

    lax.fori_loop(0, pairs, segment(ko_ref, vo_ref, None, False, True, False), 0)
    gather.advance()
    spread.first()
    keys_of(af_ref, kf_ref, vf_ref, cosf_in(), sinf_in())
    outs[3].flush()
    outs[4].flush()
    lax.fori_loop(0, pairs, segment(kf_ref, vf_ref, mask1, True, False, False), 0)
    spread.second()
    for j in line:
        j.advance()
    keys_of(as_ref, ks_ref, vs_ref, cos, sin)
    outs[5].flush()
    outs[6].flush()
    last = segment(ks_ref, vs_ref, mask2, False, False, True)
    lax.fori_loop(0, pairs // 2, last, 0)
    gather.advance()
    for j in line:
        j.advance()
    lax.fori_loop(pairs // 2, pairs, last, 0)
    for j in line:
        j.advance()
    outs[7].flush()
    outs[8].flush()
    xm = x_in()[...].astype(F32) + mm(o_ref[...], w_ref[:, 3 * d : 4 * d], NT)
    xm_ref[...] = xm
    outs[9].flush()
    xh, _ = norm_stats(xm)
    m_ref[...] = (xh * gain_in()[row : row + 1]).astype(BF)
    outs[10].flush()
    spread.end()
    gather.complete()
    for j in line:
        j.complete()


def attend(info, x, a, w, cosf, sinf, cos, sin, gain, row, jobs, cid):
    n, d = x.shape
    sd = jax.ShapeDtypeStruct((n, d), BF)
    heads = (d // 128, 8, n)
    return run(
        functools.partial(attend_body, row), "attend",
        [info, a, w, cos, sin, cosf, sinf, x, gain], [smem()] + vmem(8),
        [sd] * 8 + [jax.ShapeDtypeStruct(heads, F32), jax.ShapeDtypeStruct((n, d), F32), sd],
        vmem(11),
        [
            pltpu.VMEM((n, d), F32),
            pltpu.VMEM((n, n), F32),
            pltpu.VMEM((n, 128), BF),
            pltpu.VMEM((n, 128), BF),
            pltpu.VMEM((128, n), BF),
            pltpu.VMEM((d, n), F32),
            pltpu.VMEM(heads, F32),
            pltpu.VMEM(heads, F32),
        ],
        [Spread(a)] + jobs, cid,
        16 * n * d * d + 40 * QB * QB * d * 4, 2 * (4 * d * d + 16 * n * d),
    )


MLP_STEPS = 6
SPLIT = 2
SPLITB = 2


def gelu(u):
    return u * (0.5 * jnp.tanh(u * (GC + (GC * GA) * (u * u))) + 0.5)


FORWARD = {"Gather": (0, 2, -1), "Line": (0, 3, -1)}
BACKWARD = {"Reduce": (0, 1, 5)}


def grid_steps(jobs, points):
    step = pl.program_id(0)
    for point in range(MLP_STEPS):
        if any(point in at_points(j, points) for j in jobs):
            pl.when(step == point)(functools.partial(steps_at, jobs, point, points))


def mlp_body(row, ins, outs, scr, jobs):
    xm_ref, m_ref, up_ref, dn_ref, gain = ins
    x_ref, a_ref, u_ref = outs
    (acc,) = scr
    step = pl.program_id(0)
    grid_steps(jobs, FORWARD)

    @pl.when(step == 0)
    def _():
        acc[...] = xm_ref[...]

    up = up_ref[...]
    dn = dn_ref[...]
    cut = m_ref.shape[0] // SPLIT
    us = [mm(m_ref[i * cut : (i + 1) * cut], up) for i in range(SPLIT)]
    for i, u in enumerate(us):
        rows = slice(i * cut, (i + 1) * cut)
        u_ref[rows] = u.astype(BF)
        acc[rows] += mm(gelu(u).astype(BF), dn, NT)

    @pl.when(step == pl.num_programs(0) - 1)
    def _():
        x = acc[...]
        x_ref[...] = x
        xh, _ = norm_stats(x)
        a_ref[...] = (xh * gain[row : row + 1]).astype(BF)
        finish(jobs, FORWARD)


def mlp(xm, m, w, gain, row, jobs, cid):
    n, d = xm.shape
    ff = w.shape[1] // 2
    steps = MLP_STEPS if jobs else MLP_STEPS // 2
    fc = ff // steps
    full = pl.BlockSpec((n, d), lambda i: (0, 0))
    return run(
        functools.partial(mlp_body, row), "mlp",
        [xm, m, w, w, gain],
        [
            full,
            full,
            pl.BlockSpec((d, fc), lambda i: (0, i)),
            pl.BlockSpec((d, fc), lambda i: (0, i + steps)),
            pl.BlockSpec(gain.shape, lambda i: (0, 0)),
        ],
        [
            jax.ShapeDtypeStruct((n, d), F32),
            jax.ShapeDtypeStruct((n, d), BF),
            jax.ShapeDtypeStruct((n, ff), BF),
        ],
        [full, full, pl.BlockSpec((n, fc), lambda i: (0, i))],
        [pltpu.VMEM((n, d), F32)],
        jobs, cid,
        4 * n * d * ff, 4 * d * ff + 2 * n * ff + 10 * n * d, grid=(steps,),
    )


def mlp_back_body(at, ins, outs, scr, jobs):
    g_ref, xm_ref, m_ref, u_ref, up_ref, dn_ref, gain = ins[:7]
    gm_ref, go_ref, dup_ref, ddn_ref, dgain_ref = outs
    gy, gyt, mt, dm = scr[:4]
    step = pl.program_id(0)
    grid_steps(jobs, BACKWARD)
    if len(ins) > 7:
        counted, info = ins[7:]
        cot_ref, g_ref = g_ref, scr[4]

        @pl.when(step == 0)
        def _():
            n = cot_ref.shape[0]
            t = lax.axis_index("tensor")
            base = t % 2 * n
            masked = counted[:, pl.ds(aligned(base, 128), n)]
            pos = base + lax.broadcasted_iota(jnp.int32, (1, n), 1)
            live = (pos < info[0]) & ((t >= 2) | (masked == 1))
            col = jnp.broadcast_to(jnp.where(live, 1.0, 0.0), (8, n)).T[:, 0:1]
            g_ref[...] = cot_ref[...].astype(F32) * col

    @pl.when(step == 0)
    def _():
        gb = g_ref[...].astype(BF)
        gy[...] = gb
        gyt[...] = gb.T
        mt[...] = m_ref[...].T
        dm[...] = jnp.zeros_like(dm)

    cut = u_ref.shape[1] // SPLITB
    gyv, gytv, mtv = gy[...], gyt[...], mt[...]
    parts = [slice(i * cut, (i + 1) * cut) for i in range(SPLITB)]
    dhs = [mm(gyv, dn_ref[:, c]) for c in parts]
    add = None
    for c, dh in zip(parts, dhs):
        u = u_ref[:, c].astype(F32)
        u2 = u * u
        th = jnp.tanh(u * (GC + (GC * GA) * u2))
        half = 0.5 * th + 0.5
        h = (u * half).astype(BF)
        slope = half + (u * (1.0 - th * th)) * ((0.5 * GC) + (1.5 * GC * GA) * u2)
        du = (dh * slope).astype(BF)
        more = mm(du, up_ref[:, c], NT)
        add = more if add is None else add + more
        dup_ref[:, c] = mm(mtv, du).astype(BF)
        ddn_ref[:, c] = mm(gytv, h).astype(BF)
    dm[...] += add

    @pl.when(step == MLP_STEPS - 1)
    def _():
        dz, dgain = norm_back(xm_ref[...], gain[at : at + 1], dm[...])
        gm = g_ref[...] + dz
        gm_ref[...] = gm
        go_ref[...] = gm.astype(BF)
        dgain_ref[...] = dgain
        finish(jobs, BACKWARD)


def mlp_back(g, xm, m, u, w, gain, at, top, jobs, cid):
    n, d = xm.shape
    ff = w.shape[1] // 2
    steps = MLP_STEPS
    fc = ff // steps
    full = pl.BlockSpec((n, d), lambda i: (0, 0))
    row = pl.BlockSpec((1, d), lambda i: (0, 0))
    wide = pl.BlockSpec((d, fc), lambda i: (0, i))
    return run(
        functools.partial(mlp_back_body, at), "mlp_back",
        [g, xm, m, u, w, w, gain] + top,
        [
            full, full, full,
            pl.BlockSpec((n, fc), lambda i: (0, i)),
            wide,
            pl.BlockSpec((d, fc), lambda i: (0, i + steps)),
            pl.BlockSpec(gain.shape, lambda i: (0, 0)),
        ]
        + ([pl.BlockSpec(top[0].shape, lambda i: (0, 0)), smem()] if top else []),
        [
            jax.ShapeDtypeStruct((n, d), F32),
            jax.ShapeDtypeStruct((n, d), BF),
            jax.ShapeDtypeStruct((d, ff), BF),
            jax.ShapeDtypeStruct((d, ff), BF),
            jax.ShapeDtypeStruct((1, d), F32),
        ],
        [full, full, wide, wide, row],
        [
            pltpu.VMEM((n, d), BF),
            pltpu.VMEM((d, n), BF),
            pltpu.VMEM((d, n), BF),
            pltpu.VMEM((n, d), F32),
        ]
        + ([pltpu.VMEM((n, d), F32)] if top else []),
        jobs, cid,
        8 * n * d * ff, 8 * d * ff + 2 * n * ff + 16 * n * d, grid=(steps,),
    )


def back_pair(g, segs, q_ref, do_ref, o_ref, lse_ref, hot, dqt, dka, dva):
    n = q_ref.shape[0]
    sl = pl.ds(aligned(g * 128, 128), 128)
    q2 = q_ref[:, sl]
    do2 = do_ref[:, sl]
    qt = q2.T
    dot = do2.T
    prod = dot.astype(F32) * o_ref[:, sl].T.astype(F32)
    for h in range(2):
        hs = slice(h * HD, h * HD + HD)
        low = half_of(h, qt.shape, 0)
        side = half_of(h, q2.shape, 1)
        none = jnp.zeros_like(q2)
        qth = jnp.where(low, qt, jnp.zeros_like(qt) if hot is None else hot[...])
        doth = jnp.where(low, dot, jnp.zeros_like(dot))
        qh = jnp.where(side, q2, none)
        doh = jnp.where(side, do2, none)
        dsum = jnp.sum(prod[hs], axis=0, keepdims=True)
        ls = lse_ref[g, h : h + 1, :]
        for at, (kr, vr, mask, bias, whole, base) in enumerate(segs):
            k2 = kr[:, sl]
            v2 = vr[:, sl]
            kt = k2.T
            kh = jnp.where(side, k2, none if mask is None else mask[...])
            for b in range(n // QB):
                cs = slice(b * QB, b * QB + QB)
                width = n if whole else (b + 1) * QB
                s = mm(kh[0:width], qth[:, cs])
                if bias is not None:
                    s = s + bias[0:width, cs]
                p = jnp.exp(s - ls[:, cs])
                dp = mm(v2[0:width], doth[:, cs])
                ds = (p * (dp - dsum[:, cs])).astype(BF)
                dv = mm(p.astype(BF), doh[cs])
                dk = mm(ds, qh[cs])
                dq = mm(kt[hs, 0:width], ds)
                if h == 0 and b == 0:
                    dva[base : base + width, :] = dv
                    dka[base : base + width, :] = dk
                elif h == 0 and not whole:
                    dva[base : base + width - QB, :] += dv[: width - QB]
                    dka[base : base + width - QB, :] += dk[: width - QB]
                    dva[base + width - QB : base + width, :] = dv[width - QB :]
                    dka[base + width - QB : base + width, :] = dk[width - QB :]
                else:
                    dva[base : base + width, :] += dv
                    dka[base : base + width, :] += dk
                if at == 0:
                    dqt[hs, cs] = dq
                else:
                    dqt[hs, cs] += dq
    return sl


def back_far_body(ins, outs, scr, jobs):
    (
        info, go_in, w_in, q_in, o_in, lse_in, ks_in, vs_in, cos_in, sin_in, kf_in, vf_in, cosf_in, sinf_in,
    ) = ins
    do_ref, dqp_ref, dkf_ref, dvf_ref, dks_ref, dvs_ref, daf_ref = [x.ref for x in outs]
    mask1, mask2, hot, dqt, dka, dva, das = scr
    early = jobs[0]
    rest = jobs[1:]
    n, d = go_in.ref.shape
    pairs = d // 128
    for j in rest:
        j.advance()
    far_masks(info, mask1, mask2, hot)
    go_ref = go_in()
    w_ref = w_in()
    do_ref[...] = mm(go_ref[...], w_ref[:, 3 * d : 4 * d]).astype(BF)
    outs[0].flush()
    for j in rest:
        j.advance()
    wk = w_ref[:, d : 2 * d]
    wv = w_ref[:, 2 * d : 3 * d]

    def part(k_in, v_in, mask, whole, c_in, s_in, dk_ref, dv_ref, begin):
        q_ref, o_ref, lse_ref = q_in(), o_in(), lse_in()
        k_ref, v_ref = k_in(), v_in()
        cos, sin = c_in(), s_in()

        def pair(g, carry):
            segs = ((k_ref, v_ref, mask, None, whole, 0),)
            sl = back_pair(g, segs, q_ref, do_ref, o_ref, lse_ref, hot, dqt, dka, dva)
            if begin:
                dqp_ref[sl, :] = dqt[...]
            else:
                dqp_ref[sl, :] += dqt[...]
            dk_ref[:, sl] = turn(dka[...], cos[...], -sin[...]).astype(BF)
            dv_ref[:, sl] = dva[...].astype(BF)
            return carry

        return pair

    pair = part(ks_in, vs_in, mask2, False, cos_in, sin_in, dks_ref, dvs_ref, True)
    lax.fori_loop(0, pairs, pair, 0)
    das[...] = (mm(dks_ref[...], wk, NT) + mm(dvs_ref[...], wv, NT)).astype(BF)
    early.go(das)
    outs[4].flush()
    outs[5].flush()
    pair = part(kf_in, vf_in, mask1, True, cosf_in, sinf_in, dkf_ref, dvf_ref, False)
    lax.fori_loop(0, pairs // 3, pair, 0)
    for j in rest:
        j.advance()
    lax.fori_loop(pairs // 3, pairs, pair, 0)
    outs[1].flush()
    outs[2].flush()
    outs[3].flush()
    daf_ref[...] = (mm(dkf_ref[...], wk, NT) + mm(dvf_ref[...], wv, NT)).astype(BF)
    outs[6].flush()
    early.end(das)
    for j in rest:
        j.complete()


def back_far(info, go, o, lse, q, kf, vf, ks, vs, w, cosf, sinf, cos, sin, jobs, cid):
    n, d = go.shape
    sd = jax.ShapeDtypeStruct((n, d), BF)
    return run(
        back_far_body, "back_far",
        [info, go, w, q, o, lse, ks, vs, cos, sin, kf, vf, cosf, sinf], [smem()] + vmem(13),
        [sd, jax.ShapeDtypeStruct((d, n), F32)] + [sd] * 5, vmem(7),
        [
            pltpu.VMEM((n, 128), BF),
            pltpu.VMEM((n, 128), BF),
            pltpu.VMEM((128, n), BF),
            pltpu.VMEM((128, n), F32),
            pltpu.VMEM((n, 128), F32),
            pltpu.VMEM((n, 128), F32),
            pltpu.VMEM((n, d), BF),
        ],
        [Early((n, d))] + jobs, cid,
        10 * n * d * d + 70 * QB * QB * d * 4, 2 * (4 * d * d + 18 * n * d),
    )


def back_near_body(row, ins, outs, scr, jobs):
    (
        info, q_in, do_in, o_in, lse_in, ko_in, vo_in, dqp_in, cos_in, sin_in, go_in, af_in, dkf_in, dvf_in,
        as_in, dks_in, dvs_in, ao_in, w_in, x_in, gm_in, gain_in,
    ) = ins
    da_ref, db_ref, g_ref, dgain_ref = [x.ref for x in outs]
    bias, dqt, dka, dva, dq_s, dko_s, dvo_s, dao = scr
    back = jobs[0]
    rest = jobs[1:]
    n, d = do_in.ref.shape
    pairs = d // 128
    back.begin()
    for j in rest:
        j.advance()
    near_bias(info, bias)
    q_ref, do_ref, o_ref, lse_ref = q_in(), do_in(), o_in(), lse_in()
    ko_ref, vo_ref, dqp_ref, cos, sin = ko_in(), vo_in(), dqp_in(), cos_in(), sin_in()

    def pair(g, carry):
        segs = ((ko_ref, vo_ref, None, bias, False, 0),)
        sl = back_pair(g, segs, q_ref, do_ref, o_ref, lse_ref, None, dqt, dka, dva)
        dq = (dqt[...] + dqp_ref[sl, :]).T
        dq_s[:, sl] = turn(dq * SCALE, cos[...], -sin[...]).astype(BF)
        dko_s[:, sl] = turn(dka[...], cos[...], -sin[...]).astype(BF)
        dvo_s[:, sl] = dva[...].astype(BF)
        return carry

    lax.fori_loop(0, pairs // 2, pair, 0)
    for j in rest:
        j.advance()
    lax.fori_loop(pairs // 2, pairs, pair, 0)
    db_ref[:, d : 2 * d] = mm(go_in()[...].T, o_ref[...]).astype(BF)
    aot = ao_in()[...].T
    aft = af_in()[...].T
    ast = as_in()[...].T
    db_ref[:, 0:d] = (
        mm(aot, dvo_s[...]) + mm(aft, dvf_in()[...]) + mm(ast, dvs_in()[...])
    ).astype(BF)
    outs[1].flush()
    da_ref[:, 0:d] = mm(aot, dq_s[...]).astype(BF)
    da_ref[:, d : 2 * d] = (
        mm(aot, dko_s[...]) + mm(aft, dkf_in()[...]) + mm(ast, dks_in()[...])
    ).astype(BF)
    outs[0].flush()
    for j in rest:
        j.advance()
    w_ref = w_in()
    dao[...] = (
        mm(dko_s[...], w_ref[:, d : 2 * d], NT)
        + mm(dvo_s[...], w_ref[:, 2 * d : 3 * d], NT)
        + mm(dq_s[...], w_ref[:, 0:d], NT)
    )
    back.end(dao)
    dz, dgain = norm_back(x_in()[...].astype(F32), gain_in()[row : row + 1], dao[...])
    g_ref[...] = gm_in()[...] + dz
    dgain_ref[...] = dgain
    for j in rest:
        j.complete()


def back_near(row, ins, daf, got, jobs, cid):
    n, d = ins[1].shape
    wide = jax.ShapeDtypeStruct((d, 2 * d), BF)
    return run(
        functools.partial(back_near_body, row), "back_near",
        ins, [smem()] + vmem(len(ins) - 1),
        [wide, wide, jax.ShapeDtypeStruct((n, d), F32), jax.ShapeDtypeStruct((1, d), F32)], vmem(4),
        [
            pltpu.VMEM((n, n), F32),
            pltpu.VMEM((128, n), F32),
            pltpu.VMEM((n, 128), F32),
            pltpu.VMEM((n, 128), F32),
            pltpu.VMEM((n, d), BF),
            pltpu.VMEM((n, d), BF),
            pltpu.VMEM((n, d), BF),
            pltpu.VMEM((n, d), F32),
        ],
        [Return(daf, got)] + jobs, cid,
        22 * n * d * d + 30 * QB * QB * d * 4, 2 * (8 * d * d + 24 * n * d),
    )


def first_body(ins, outs, scr, jobs):
    x_in, gain_in = ins[0:2]
    narrow, (up, down) = ins[2:6], ins[6:8]
    layers, d = up.shape[0:2]
    pa0, ob, db, ot, dt, sem = scr
    rows = pa0.shape[1]
    pas = [pa0] + [x.ref for x in outs[1:layers]]
    pms = [x.ref for x in outs[layers:]]
    dp = lax.axis_index("dp")
    at_a = pl.ds(aligned(slot_of(dp, ORDERS[0]) * rows), rows)
    at_b = pl.ds(aligned(slot_of(dp, ORDERS[1]) * rows), rows)
    copies = []
    for l in range(layers):
        for i, (src, dst) in enumerate(
            [(x.at[l], ob.at[l, p]) for p, x in enumerate(narrow)]
            + [(down.at[l], db.at[l]), (up.at[l, at_a, :], pms[l].at[0])]
        ):
            copies.append(pltpu.make_async_copy(src, dst, sem.at[l * 6 + i]))
            copies[-1].start()

    def narrow_parts(l):
        for p in range(4):
            ot[p] = ob[l, p].T
            pas[l][p] = ot[p, at_a if p < 2 else at_b, :]

    for c in copies[0:4]:
        c.wait()
    narrow_parts(0)
    line = jobs[0]
    line.src = pa0
    line.advance()
    xh, _ = norm_stats(x_in()[...].astype(F32))
    outs[0].ref[...] = (xh * gain_in()[0:1]).astype(BF)
    outs[0].flush()
    line.advance()
    for c in copies[4:]:
        c.wait()
    for l in range(layers):
        dt[...] = db[l].T
        pms[l][1] = dt[at_b, :]
    line.advance()
    for l in range(1, layers):
        narrow_parts(l)
    line.complete()


def first(x, gain, weights, cid):
    n, d = x.shape
    q, up = weights[0], weights[4]
    layers, rows = q.shape[0], d >> BITS
    w, f = q.shape[1], up.shape[2]
    pa = jax.ShapeDtypeStruct((4, rows, w), BF)
    pm = jax.ShapeDtypeStruct((2, rows, d), BF)
    assert f == d
    return run(
        first_body, "first", [x, gain] + list(weights), vmem(2) + any_spec(6),
        [jax.ShapeDtypeStruct((n, d), BF)] + [pa] * (layers - 1) + [pm] * layers, vmem(2 * layers),
        [
            pltpu.VMEM((4, rows, w), BF),
            pltpu.VMEM((layers, 4, w, d), BF),
            pltpu.VMEM((layers, f, d), BF),
            pltpu.VMEM((4, d, w), BF),
            pltpu.VMEM((d, f), BF),
            dma(6 * layers),
        ],
        [Line(None, False, (4, rows, w))], cid, 10 * n * d, 4 * n * d,
    )


def layout_body(ins, outs, scr, jobs):
    count = len(ins) // 2
    for k in reversed(range(count)):
        ref = ins[count + k]()
        f = ref.shape[1] // 2
        outs[4].ref[k] = ref[:, 0:f].astype(F32)
        outs[5].ref[k] = ref[:, f : 2 * f].astype(F32).T
    outs[4].flush()
    outs[5].flush()
    for k in reversed(range(count)):
        v = ins[k]()[...].astype(F32)
        w = v.shape[1] // 4
        vt = v.T
        for i in range(4):
            outs[i].ref[k] = vt[i * w : i * w + w]
    for i in range(4):
        outs[i].flush()


def layout(att, mlps):
    layers = len(att)
    d = att[0].shape[0]
    w = att[0].shape[1] // 4
    f = mlps[0].shape[1] // 2
    shapes = [(layers, w, d)] * 4 + [(layers, d, f), (layers, f, d)]
    return run(
        layout_body, "layout", att + mlps, vmem(2 * layers),
        [jax.ShapeDtypeStruct(x, F32) for x in shapes], vmem(6), [], [], None, 1, 6 * layers * d * (4 * w + 2 * f),
    )[0]


def wide_of(every):
    return jnp.concatenate(
        [every[z, p] for p in range(every.shape[1]) for z in range(NZ)], axis=1
    )


def turning(n):
    position = np.arange(LMAX, dtype=np.float32)
    frequency = np.exp(
        (-math.log(10000.0) * np.arange(HD // 2, dtype=np.float32) / (HD // 2)).astype(np.float32)
    )
    angles = (position[:, None] * frequency[None, :]).astype(np.float32).astype(np.float64)
    cos = np.concatenate([np.cos(angles)] * 4, axis=1)
    sin = np.concatenate([-np.sin(angles), np.sin(angles)] * 2, axis=1)
    return [jnp.asarray(x.astype(np.float32).reshape(LMAX // n, n, 128)) for x in (cos, sin)]


def over_rest(arrays):
    n = lax.axis_size("dp")
    for b in range(BITS, n.bit_length() - 1):
        arrays = [x + lax.ppermute(x, "dp", [(i, i ^ (1 << b)) for i in range(n)]) for x in arrays]
    return arrays


def tail_body(ins, outs, scr, jobs):
    red, gains, wide, gain_line, att_line, wide_gather, att_gather = jobs
    every, part, total = scr
    for j in (red, gains, wide):
        j.advance()
    red.advance()
    gains.advance()
    red.advance()
    gains.advance()
    wide.complete()
    wide_gather.src = wide.o[0]
    gains.complete()
    gain_line.src, gain_line.dst = gains.o[0], total
    gain_line.advance()
    red.complete()
    a = red.o[0][...].astype(F32)
    b = red.o[1][...].astype(F32)
    w = a.shape[1] // 2
    c = w // NZ
    for z in range(NZ):
        cols = [x[:, k * w + z * c : k * w + z * c + c] for x in (a, b) for k in (0, 1)]
        every[z] = jnp.concatenate(cols, axis=1).astype(BF)
    att_line.src, att_line.dst = every, part
    att_line.advance()
    wide_gather.advance()
    wide_gather.advance()
    att_line.complete()
    att_gather.src = part
    att_gather.advance()
    wide_gather.advance()
    att_gather.advance()
    wide_gather.complete()
    att_gather.advance()
    gain_line.complete()
    outs[0].ref[...] = total[...]
    att_gather.complete()


def tail(att_grads, gain_rows, mlp_arrays, cid):
    rows = att_grads[0].shape[0] >> BITS
    w = att_grads[0].shape[1] // 2
    wide = LineSumWide(mlp_arrays)
    jobs = [
        Reduce(*att_grads), PlaneSum(gain_rows), wide,
        LineSum(None, gain_rows.shape, F32, True), LineSum(None, (rows, w)),
        Gather(None, wide.outs[0].shape), Gather(None, (rows, w)),
    ]
    res, extra = run(
        tail_body, "tail", [gain_rows], vmem(1), [jax.ShapeDtypeStruct(gain_rows.shape, F32)], vmem(1),
        [pltpu.VMEM((NZ, rows, w), BF), pltpu.VMEM((rows, w), BF), pltpu.VMEM(gain_rows.shape, F32)],
        jobs, cid, 1, 1 << 24,
    )
    return res[0], extra[5][0], extra[6][0]


def by_line(halves, counts):
    n = lax.axis_size("dp")
    cols = []
    for x, c in zip(halves, counts):
        for b in range(BITS, n.bit_length() - 1):
            x = x + lax.ppermute(x, "dp", [(i, i ^ (1 << b)) for i in range(n)])
        w = x.shape[1] // c
        for j in range(c):
            cols.append(x[:, j * w : (j + 1) * w].reshape(x.shape[0], NZ, w // NZ))
    return jnp.concatenate(cols, axis=2).transpose(1, 0, 2)


def on_device(
    tokens, lengths, noise_mask, cotangent, attn_gain, query_weight, key_weight, value_weight,
    out_weight, mlp_gain, up_weight, down_weight,
):
    n, d = tokens.shape
    info = lengths
    cos_t, sin_t = turning(n)
    cosf, sinf, cos, sin = (cos_t, 0), (sin_t, 0), (cos_t, 1), (sin_t, 1)

    res, ((every,),) = first(
        tokens, attn_gain,
        [x.transpose(0, 2, 1) for x in (query_weight, key_weight, value_weight)]
        + [out_weight, up_weight, down_weight],
        0,
    )
    a = res[0]
    pa = [None] + list(res[1:LAYERS])
    pm = res[LAYERS:]
    (wa,), (wide,) = transfer("gather_first", [Gather(wide_of(every)), Line(pm[0], True)], 1)
    was, wms, saved = [], [], []
    x = tokens
    for l in range(LAYERS):
        more = l + 1 < LAYERS
        jobs = [Gather(wide, None, True)] + ([Line(pa[l + 1], False)] if more else [])
        res, extra = attend(
            info, x, a, wa, cosf, sinf, cos, sin, mlp_gain, l, jobs, 10 + l
        )
        q, ko, vo, kf, vf, ks, vs, o, lse, xm, m = res
        af, as_ = extra[0]
        wm = extra[1][0]
        was.append(wa)
        wms.append(wm)
        jobs = []
        if more:
            piece = wide_of(extra[2][0])
            jobs = [Line(pm[l + 1], True), Gather(piece)]
        nxt = min(l + 1, LAYERS - 1)
        (x_next, a_next, u), extra = mlp(xm, m, wm, attn_gain, nxt, jobs, 20 + l)
        if more:
            wide, wa = extra[0][0], extra[1][0]
        saved.append((x, a, af, as_, q, kf, vf, ks, vs, ko, vo, o, lse, xm, m, u))
        x, a = x_next, a_next
    block_out = x

    g = cotangent
    top = [noise_mask, info]
    gains = [None] * (2 * LAYERS)
    att = [None] * LAYERS
    mlps = [None] * LAYERS
    att_grads = mlp_parts = mlp_arrays = None

    for l in reversed(range(LAYERS)):
        x, a, af, as_, q, kf, vf, ks, vs, ko, vo, o, lse, xm, m, u = saved[l]
        above = l + 1 < LAYERS
        jobs = []
        if above:
            jobs = [Reduce(*att_grads), LineSumWide(mlp_arrays)]
        res, extra = mlp_back(g, xm, m, u, wms[l], mlp_gain, l, top, jobs, 30 + l)
        top = []
        gm, go, dup, ddn, gains[LAYERS + l] = res
        jobs = [Reduce(dup, ddn, 0, 2)]
        if above:
            jobs += [LineSum(by_line(extra[0], (2, 2))), Gather(extra[1][0])]
        res, extra = back_far(
            info, go, o, lse, q, kf, vf, ks, vs, was[l], cosf, sinf, cos, sin, jobs, 40 + l
        )
        do, dqp, dkf, dvf, dks, dvs, daf = res
        got = extra[0][0]
        mlp_parts = [extra[1]]
        jobs = [Reduce(dup, ddn, 1, 2)]
        if above:
            mlps[l + 1] = extra[3][0]
            jobs.append(Gather(extra[2][0]))
        res, extra = back_near(
            l,
            [
                info, q, do, o, lse, ko, vo, dqp, cos, sin, go, af, dkf, dvf, as_, dks, dvs, a, was[l],
                x, gm, attn_gain,
            ],
            daf, got, jobs, 50 + l,
        )
        mlp_parts.append(extra[1])
        mlp_arrays = over_rest([p[i] for i in (0, 1) for p in mlp_parts])
        if above:
            att[l + 1] = extra[2][0]
        att_grads = res[0:2]
        g, gains[l] = res[2:4]

    gain_rows = jnp.concatenate(gains, axis=0)
    if lax.axis_size("dp") == 1 << BITS:
        gain_sums, mlps[0], att[0] = tail(att_grads, gain_rows, mlp_arrays, 2)
    else:
        (sums, (gain_rows,), (mlp_sum,)) = transfer(
            "reduce_last",
            [Reduce(*att_grads), PlaneSum(gain_rows), LineSumWide(mlp_arrays)],
            2,
        )
        for b in range(BITS, lax.axis_size("dp").bit_length() - 1):
            size = lax.axis_size("dp")
            gain_rows = gain_rows + lax.ppermute(
                gain_rows, "dp", [(i, i ^ (1 << b)) for i in range(size)]
            )
        (part,), (gain_sums,), (mlps[0],) = transfer(
            "line_last",
            [
                LineSum(by_line(sums, (2, 2))),
                LineSum(jnp.broadcast_to(gain_rows, (NZ,) + gain_rows.shape)),
                Gather(mlp_sum),
            ],
            3,
        )
        ((att[0],),) = transfer("gather_last", [Gather(part)], 4)
    grads = layout(att, mlps)
    return (
        block_out, g, gain_sums[:LAYERS], *[x.transpose(0, 2, 1) for x in grads[:3]], grads[3],
        gain_sums[LAYERS:], grads[4], grads[5],
    )


def solution(mesh):
    rows = P(("dp", "tensor"), None)
    cols = P(None, None, "tensor")
    mids = P(None, "tensor", None)
    return jax.shard_map(
        on_device,
        mesh=mesh,
        in_specs=(
            rows, P("dp"), P("dp", None), rows, P(), cols, cols, cols, mids, P(), cols, mids,
        ),
        out_specs=(rows, rows, P(), cols, cols, cols, mids, P(), cols, mids),
        check_vma=False,
    )
```
